32 devices in a mesh: dp: 4 (over x, core), seq: 2 (over y), fsdp: 4 (over z).
Axes of the slice: x: 2, y: 2, z: 4, core: 2. Of those that a mesh axis runs over, the one named last changes fastest.
Arguments:
- tokens: bfloat16 [16, 1536, 768], P(('dp', 'fsdp'), 'seq'), may hold values from -6 to 6
- attn_in: bfloat16 [768, 2304], P('fsdp'), may hold values from -0.21875 to 0.21875
- attn_out: bfloat16 [768, 768], P('fsdp'), may hold values from -1.75 to 1.75
- router: bfloat16 [768, 4], P('fsdp'), may hold values from -0.15625 to 0.15625
- gains: bfloat16 [768, 2], P('fsdp'), may hold values from 0.5 to 1.5
- expert_w: bfloat16 [3072, 4, 1536], P('fsdp'), may hold values from -0.21875 to 0.21875
- expert_ids: int32 [16, 1536, 2], P(('dp', 'fsdp'), 'seq'), may hold values from 0 to 3, all different within a row
- segments: int32 [16, 512], P(('dp', 'fsdp')), may hold values from 0 to 1, as said below
- cotangent: bfloat16 [16, 1536, 768], P(('dp', 'fsdp'), 'seq'), may hold values from -6 to 6
Outputs:
- block_out: bfloat16 [16, 1536, 768], P(('dp', 'fsdp'), 'seq')
- d_tokens: bfloat16 [16, 1536, 768], P(('dp', 'fsdp'), 'seq')
- d_attn_in: float32 [768, 2304], P('fsdp')
- d_attn_out: float32 [768, 768], P('fsdp')
- d_router: float32 [768, 4], P('fsdp')
- d_gains: float32 [768, 2], P('fsdp')
- d_expert: float32 [3072, 4, 1536], P('fsdp')
The draws below stay inside these ranges and needn't reach their ends.
Inputs may be any that keep to these rules, and one draw needn't show every extreme that they name: `expert_ids`: the two experts of a token differ. `segments`: never falls along a group; every continuation has 64 to 384 tokens, and in every group one has exactly 384.
All inputs are finite; a program needn't handle non-finite values.
Results may differ from the reference program's by a relative error of at most 0.018.
Values may be sent and summed in bfloat16 or wider, within the bound.
A program may use at most 384 MiB of HBM per device.

```python
import jax
import jax.numpy as jnp
from jax import lax

D = 768
HEADS = 12
HEAD_DIM = 64
FF = 3072
EXPERTS = 4
TOP_K = 2
PROMPT = 1024
CONT = 256
CONT_COUNT = 2
GROUP = 1536
TOK_DEV = 768
CAP = 384
GROUPS = 16
N_SEQ = 2


def one_group(key):
    longest = CONT + CONT // 2
    others = CONT_COUNT - 1
    rest = CONT_COUNT * CONT - longest
    key_place, key_shift = jax.random.split(key)
    where_long = jax.random.randint(key_place, (), 0, CONT_COUNT, dtype=jnp.int32)
    index = jnp.arange(others, dtype=jnp.int32)
    even_share = rest // others + (index < rest % others).astype(jnp.int32)
    shifts = jax.random.randint(key_shift, (max(CONT_COUNT // 2, 1),), -(CONT // 4), CONT // 4 + 1, dtype=jnp.int32)
    pair_index = index // 2
    sign_of = 1 - 2 * (index % 2)
    paired = pair_index * 2 + 1 < others
    lengths_other = even_share + jnp.where(paired, sign_of * shifts[pair_index], 0)
    slot_index = jnp.arange(CONT_COUNT, dtype=jnp.int32)
    other_slot = jnp.clip(slot_index - (slot_index > where_long).astype(jnp.int32), 0, others - 1)
    lengths = jnp.where(slot_index == where_long, longest, lengths_other[other_slot]).astype(jnp.int32)
    ends = jnp.cumsum(lengths)
    places = jnp.arange(CONT_COUNT * CONT, dtype=jnp.int32)
    return jnp.sum((places[:, None] >= ends[None, :]).astype(jnp.int32), axis=1).astype(jnp.int32)


def draw_segments(key, part):
    keys = jax.random.split(jax.random.fold_in(key, 7), GROUPS)
    return jax.vmap(one_group)(keys).astype(jnp.int32)


def block_levels(rng, shape, cuts, low, top_value):
    level = 1.0
    for dim, parts in cuts:
        draws = jax.random.uniform(jax.random.fold_in(jax.random.fold_in(rng, 6), dim), (parts,), jnp.float32, low / len(cuts), top_value / len(cuts))
        level = level * jnp.repeat(jnp.exp(draws), shape[dim] // parts).reshape((-1,) + (1,) * (len(shape) - 1 - dim))
    return level


def choose_distinct(key, rows, number_of, top, lift):
    order = jax.random.permutation(jax.random.fold_in(key, 1), number_of)
    favour = order
    for power in range(3):
        favour = favour * favour // number_of
    favour = favour * lift // number_of
    chance = jax.random.randint(jax.random.fold_in(key, 2), (rows, number_of), 0, 4096) + favour
    holders = jax.random.permutation(jax.random.fold_in(key, 3), rows)[jnp.arange(number_of) % rows]
    chance = jnp.where(jnp.arange(rows)[:, None] == holders[None, :], 1 << 14, chance)
    score = chance * number_of + jnp.arange(number_of)
    return lax.top_k(score.astype(jnp.int32), top)[1].astype(jnp.int32)


def gaussian(key, dims, scale, reach, cuts=(), kind=jnp.bfloat16):
    entries = jax.random.normal(key, dims, jnp.float32) * scale
    if len(cuts) > 0:
        entries = block_levels(key, dims, cuts, -0.22, 0.18) * entries
    return jnp.clip(entries, min=-reach, max=reach).astype(kind)


def setup_inputs(seed: int = 0) -> dict:
    key_of = jax.random.split(jax.random.key(seed), 10)
    return {
        "tokens": gaussian(key_of[0], (GROUPS, GROUP, D), 1.0, 6.0, ((0, 16), (1, 2))),
        "attn_in": gaussian(key_of[1], (D, 3 * D), D ** -0.5, 0.21875, ((0, 4),)),
        "attn_out": gaussian(key_of[2], (D, D), (D // 64) ** -0.5, 1.75, ((0, 4),)),
        "router": gaussian(key_of[3], (D, EXPERTS), (2 * D) ** -0.5, 0.15625, ((0, 4),)),
        "gains": jnp.clip(1.0 + 0.1 * jax.random.normal(key_of[4], (D, 2), jnp.float32), 0.5, 1.5).astype(jnp.bfloat16),
        "expert_w": gaussian(key_of[5], (FF, EXPERTS, 2 * D), D ** -0.5, 0.21875, ((0, 4),)),
        "expert_ids": choose_distinct(key_of[6], GROUPS * GROUP, EXPERTS, TOP_K, 4096).reshape((GROUPS, GROUP, TOP_K)),
        "segments": draw_segments(jax.random.fold_in(key_of[9], 71), 0),
        "cotangent": gaussian(key_of[8], (GROUPS, GROUP, D), 1.0, 6.0, ((0, 16), (1, 2))),
    }


EPSILON = 1e-06
NEGATIVE = -1e+30
HIGH = lax.Precision.HIGHEST

@jax.custom_vjp
def low(v):
    return lax.optimization_barrier(v.astype(jnp.bfloat16)).astype(jnp.float32)

@jax.custom_vjp
def low_back(v):
    return v

def low_keep(v):
    return (low(v), None)

def low_pass(kept, grad):
    return (grad,)

def back_keep(v):
    return (v, None)

def back_low(kept, grad):
    return (low(grad),)
low.defvjp(low_keep, low_pass)
low_back.defvjp(back_keep, back_low)

def route(choose, capacity, experts_count):
    pair_expert = choose.reshape(-1).astype(jnp.int32)
    one_hot = (pair_expert[:, None] == jnp.arange(experts_count, dtype=jnp.int32)[None, :]).astype(jnp.int32)
    before = jnp.cumsum(one_hot, axis=0) - one_hot
    place = lax.optimization_barrier(jnp.sum(before * one_hot, axis=1))
    kept = place < capacity
    slots = jnp.where(kept, pair_expert * capacity + place, experts_count * capacity).astype(jnp.int32)
    pair_count = pair_expert.shape[0]
    pair_of = jnp.zeros((experts_count * capacity + 1,), jnp.int32).at[slots].set(jnp.arange(pair_count, dtype=jnp.int32))
    filled = jnp.zeros((experts_count * capacity + 1,), jnp.int32).at[slots].set(jnp.ones((pair_count,), jnp.int32))
    return (slots, kept, pair_of[:-1], filled[:-1] > 0)

def attend(queries, keys, values, seg_full):
    block = min(512, GROUP)
    key_place = jnp.arange(GROUP, dtype=jnp.int32)

    def one_block(begin):
        query_block = lax.dynamic_slice_in_dim(queries, begin, block, 0)
        query_place = begin + jnp.arange(block, dtype=jnp.int32)
        query_seg = lax.dynamic_slice_in_dim(seg_full, begin, block, 0)
        raw = jnp.einsum('qhd,khd->hqk', query_block, keys, precision=HIGH) * HEAD_DIM ** (-0.5)
        raw = low_back(raw)
        allowed = (key_place[None, :] <= query_place[:, None]) & ((seg_full[None, :] < 0) | (seg_full[None, :] == query_seg[:, None]))
        masked = jnp.where(allowed[None], raw, NEGATIVE)
        probs = jax.nn.softmax(masked, axis=-1)
        return jnp.einsum('hqk,khd->qhd', low(probs), values, precision=HIGH)
    begins = jnp.arange(GROUP // block, dtype=jnp.int32) * block
    return lax.map(jax.checkpoint(one_block), begins).reshape(GROUP, HEADS, HEAD_DIM)

def forward(x_rows, w_qkv, w_proj, w_route, gain_pair, w_expert, seg_full, slots, kept, pair_of, filled, choose_map):
    r_one = lax.rsqrt(lax.optimization_barrier(jnp.mean(x_rows * x_rows, axis=-1, keepdims=True)) + EPSILON)
    normed = low(x_rows * r_one * gain_pair[:, 0])
    proj = low(low_back(jnp.dot(normed, w_qkv, precision=HIGH)))
    queries = proj[:, :D].reshape(GROUP, HEADS, HEAD_DIM)
    keys = proj[:, D:2 * D].reshape(GROUP, HEADS, HEAD_DIM)
    values = proj[:, 2 * D:].reshape(GROUP, HEADS, HEAD_DIM)
    attended = low(low_back(attend(queries, keys, values, seg_full).reshape(GROUP, D)))
    hidden = x_rows + low_back(jnp.dot(attended, w_proj, precision=HIGH))
    r_two = lax.rsqrt(lax.optimization_barrier(jnp.mean(hidden * hidden, axis=-1, keepdims=True)) + EPSILON)
    routed = low(hidden * r_two * gain_pair[:, 1])
    logits = jnp.dot(routed, w_route, precision=HIGH)
    probs_r = jax.nn.softmax(logits, axis=-1)
    gates = lax.optimization_barrier(jnp.sum(probs_r[:, None, :] * choose_map, axis=-1))
    shards = routed.reshape(N_SEQ, TOK_DEV, D)
    token_of = pair_of // 2
    taken = jax.vmap(lambda rows, index: rows[index])(shards, token_of)
    expert_in = jnp.where(filled[..., None], taken, 0.0).reshape(N_SEQ, EXPERTS, CAP, D)
    pre = low_back(jnp.einsum('secd,fed->secf', expert_in, w_expert[:, :, :D], precision=HIGH))
    act = low(jax.nn.gelu(pre))
    result = low_back(jnp.einsum('secf,fed->secd', act, w_expert[:, :, D:], precision=HIGH))
    padded = jnp.concatenate([result.reshape(N_SEQ, EXPERTS * CAP, D), jnp.zeros((N_SEQ, 1, D), result.dtype)], axis=1)
    picked = jax.vmap(lambda rows, index: rows[index])(padded, slots).reshape(GROUP, TOP_K, D)
    weight_pair = gates * kept.reshape(GROUP, TOP_K)
    return hidden + lax.optimization_barrier(jnp.sum(weight_pair[..., None] * picked, axis=1))

def reference(tokens, attn_in, attn_out, router, gains, expert_w, expert_ids, segments, cotangent):
    params = tuple((weight.astype(jnp.float32) for weight in (attn_in, attn_out, router, gains, expert_w)))

    def per_group(total, inputs):
        rows, choose, seg_ids, cot_rows = inputs
        seg_full = jnp.concatenate([jnp.full((PROMPT,), -1, jnp.int32), seg_ids.astype(jnp.int32)])
        slots, kept, pair_of, filled = jax.vmap(lambda index: route(index, CAP, EXPERTS))(choose.reshape(N_SEQ, TOK_DEV, TOP_K))
        choose_map = (choose[:, :, None] == jnp.arange(EXPERTS, dtype=jnp.int32)[None, None, :]).astype(jnp.float32)
        kept_f = kept.astype(jnp.float32)

        def run(x_rows, w_qkv, w_proj, w_route, gain_pair, w_expert):
            return forward(x_rows, w_qkv, w_proj, w_route, gain_pair, w_expert, seg_full, slots, kept_f, pair_of, filled, choose_map)
        out_rows, pull = jax.vjp(run, rows.astype(jnp.float32), *params)
        grads = pull(cot_rows.astype(jnp.float32))
        total = tuple((old + new for old, new in zip(total, grads[1:])))
        return (total, (out_rows.astype(jnp.bfloat16), grads[0].astype(jnp.bfloat16)))
    zeros = tuple((jnp.zeros_like(weight) for weight in params))
    total, (outs, grad_rows) = lax.scan(per_group, zeros, (tokens, expert_ids, segments, cotangent))
    return (outs, grad_rows, total[0], total[1], total[2], total[3], total[4])
```

```python
import functools

import jax
import jax.numpy as jnp
from jax import lax
from jax.experimental import pallas as pl
from jax.experimental.pallas import tpu as pltpu
from jax.sharding import PartitionSpec as P

HEADS = 12
HEAD_DIM = 64
EXPERTS = 4
EPSILON = 1e-06
NEGATIVE = -1e30
LOG2E = 1.4426950408889634
BF = jnp.bfloat16
F32 = jnp.float32
MESH = pl.DeviceIdType.MESH
VMEM_LIMIT = 60 << 20
QB = 256
ANY = pl.BlockSpec(memory_space=pl.ANY)
VM = pl.BlockSpec(memory_space=pltpu.VMEM)


def nn(a, b):
    return lax.dot_general(a, b, (((1,), (0,)), ((), ())), preferred_element_type=F32)


def nt(a, b):
    return lax.dot_general(a, b, (((1,), (1,)), ((), ())), preferred_element_type=F32)


def tn(a, b):
    return lax.dot_general(a, b, (((0,), (0,)), ((), ())), preferred_element_type=F32)


def iota(shape, dim):
    return lax.broadcasted_iota(jnp.int32, shape, dim)


def params(cid=None):
    if cid is None:
        return pltpu.CompilerParams(vmem_limit_bytes=VMEM_LIMIT)
    return pltpu.CompilerParams(
        vmem_limit_bytes=VMEM_LIMIT, collective_id=cid, has_side_effects=True
    )


def sds(shape, dtype):
    return jax.ShapeDtypeStruct(shape, dtype)


def place():
    dp, sq, z = lax.axis_index("dp"), lax.axis_index("seq"), lax.axis_index("fsdp")
    return dp, sq, z, dp // 2, lax.rem(dp, 2)


def greet(peers):
    barrier = pltpu.get_barrier_semaphore()
    for peer in peers:
        pl.semaphore_signal(barrier, inc=1, device_id=peer, device_id_type=MESH)
    pl.semaphore_wait(barrier, len(peers))


def remote(src, dst, send, recv, peer):
    return pltpu.make_async_remote_copy(
        src_ref=src, dst_ref=dst, send_sem=send, recv_sem=recv, device_id=peer, device_id_type=MESH
    )


def al(x):
    return pl.multiple_of(x, 128)


def heads_in_kernel(parts, src, dst, local, send, recv):
    dp, sq, z, _, _ = place()
    rows, half = src.shape[0], src.shape[1] // parts // 2
    peer = (dp, 1 - sq, z)
    greet([peer])
    mine = pl.ds(pl.multiple_of(sq * rows, rows), rows)
    copies = []
    for i in range(parts):
        out = dst.at[mine, pl.ds(i * half, half)]
        theirs = src.at[:, pl.ds(al((2 * i + 1 - sq) * half), half)]
        own = src.at[:, pl.ds(al((2 * i + sq) * half), half)]
        copies.append(remote(theirs, out, send.at[i], recv.at[i], peer))
        copies.append(pltpu.make_async_copy(own, out, local.at[i]))
    for c in copies:
        c.start()
    for c in copies:
        c.wait()


def heads_in(x, parts, cid):
    rows, cols = x.shape
    return pl.pallas_call(
        functools.partial(heads_in_kernel, parts),
        out_shape=sds((2 * rows, cols // 2), x.dtype),
        in_specs=[ANY],
        out_specs=ANY,
        scratch_shapes=[pltpu.SemaphoreType.DMA((parts,))] * 3,
        compiler_params=params(cid),
        name=f"heads_in_{parts}",
    )(x)


def heads_out_kernel(parts, *refs):
    srcs, dst, local, send, recv = refs[:parts], refs[parts], *refs[parts + 1 :]
    dp, sq, z, _, _ = place()
    rows, half = dst.shape[0], srcs[0].shape[1]
    peer = (dp, 1 - sq, z)
    greet([peer])
    copies = []
    for i in range(parts):
        out = dst.at[:, pl.ds(al((2 * i + sq) * half), half)]
        theirs = srcs[i].at[pl.ds(pl.multiple_of((1 - sq) * rows, rows), rows)]
        own = srcs[i].at[pl.ds(pl.multiple_of(sq * rows, rows), rows)]
        copies.append(remote(theirs, out, send.at[i], recv.at[i], peer))
        copies.append(pltpu.make_async_copy(own, out, local.at[i]))
    for c in copies:
        c.start()
    for c in copies:
        c.wait()


def heads_out(xs, cid):
    parts = len(xs)
    rows, half = xs[0].shape
    return pl.pallas_call(
        functools.partial(heads_out_kernel, parts),
        out_shape=sds((rows // 2, parts * 2 * half), xs[0].dtype),
        in_specs=[ANY] * parts,
        out_specs=ANY,
        scratch_shapes=[pltpu.SemaphoreType.DMA((parts,))] * 3,
        compiler_params=params(cid),
        name=f"heads_out_{parts}",
    )(*xs)


def chips_kernel(parts, *refs):
    srcs, dsts = refs[:parts], refs[parts : 2 * parts]
    local, send, recv = refs[2 * parts :]
    dp, sq, z, x, core = place()
    flips = [(1, 0), (0, 1), (1, 1)]

    def chip(fx, fy):
        px = x if fx == 0 else 1 - x
        py = sq if fy == 0 else 1 - sq
        return px * 2 + py, (px * 2 + core, py, z)

    me, _ = chip(0, 0)
    greet([chip(*f)[1] for f in flips])
    copies = []
    for i in range(parts):
        for j, f in enumerate(flips):
            there, peer = chip(*f)
            copies.append(
                remote(srcs[i].at[there], dsts[i].at[me], send.at[i, j], recv.at[i, j], peer)
            )
        copies.append(pltpu.make_async_copy(srcs[i].at[me], dsts[i].at[me], local.at[i]))
    for c in copies:
        c.start()
    for c in copies:
        c.wait()


def chips(xs, cid):
    parts = len(xs)
    return pl.pallas_call(
        functools.partial(chips_kernel, parts),
        out_shape=tuple(sds(x.shape, x.dtype) for x in xs),
        in_specs=[ANY] * parts,
        out_specs=tuple([ANY] * parts),
        scratch_shapes=[
            pltpu.SemaphoreType.DMA((parts,)),
            pltpu.SemaphoreType.DMA((parts, 3)),
            pltpu.SemaphoreType.DMA((parts, 3)),
        ],
        compiler_params=params(cid),
        name=f"chips_{parts}",
    )(*xs)


def cores_join_kernel(src, dst, local, send, recv):
    dp, sq, z, x, core = place()
    peer = (x * 2 + 1 - core, sq, z)
    greet([peer])
    copies = [
        remote(src, dst.at[:, core], send, recv, peer),
        pltpu.make_async_copy(src, dst.at[:, core], local),
    ]
    for c in copies:
        c.start()
    for c in copies:
        c.wait()


def cores_join(x, cid):
    n, r, k = x.shape
    return pl.pallas_call(
        cores_join_kernel,
        out_shape=sds((n, 2, r, k), x.dtype),
        in_specs=[ANY],
        out_specs=ANY,
        scratch_shapes=[pltpu.SemaphoreType.DMA(())] * 3,
        compiler_params=params(cid),
        name="cores_join",
    )(x)


def cores_sum_kernel(src, dst, got, own, sem, send, recv):
    dp, sq, z, x, core = place()
    peer = (x * 2 + 1 - core, sq, z)
    greet([peer])
    n = src.shape[0]
    there = [remote(src.at[i, 1 - core], got.at[i], send.at[i], recv.at[i], peer) for i in range(n)]
    here = pltpu.make_async_copy(src.at[:, core], own, sem)
    for c in there:
        c.start()
    here.start()
    here.wait()
    for i in range(n):
        there[i].wait()
        dst[i] = (own[i].astype(F32) + got[i].astype(F32)).astype(BF)


def cores_sum(x, cid):
    n, _, r, k = x.shape
    return pl.pallas_call(
        cores_sum_kernel,
        out_shape=sds((n, r, k), x.dtype),
        in_specs=[ANY],
        out_specs=VM,
        scratch_shapes=[
            pltpu.VMEM((n, r, k), x.dtype),
            pltpu.VMEM((n, r, k), x.dtype),
            pltpu.SemaphoreType.DMA(()),
            pltpu.SemaphoreType.DMA((n,)),
            pltpu.SemaphoreType.DMA((n,)),
        ],
        compiler_params=params(cid),
        name="cores_sum",
    )(x)


def front_kernel(x_ref, gain_ref, w_ref, proj_ref):
    x = x_ref[...].astype(F32)
    r_one = lax.rsqrt(jnp.mean(x * x, axis=1, keepdims=True) + EPSILON)
    normed = (x * r_one * gain_ref[...]).astype(BF)
    cols = 768
    for j in range(0, w_ref.shape[1], cols):
        proj_ref[:, j : j + cols] = nn(normed, w_ref[:, j : j + cols]).astype(BF)


def front(x, gain, w):
    return pl.pallas_call(
        front_kernel,
        out_shape=sds((x.shape[0], w.shape[1]), BF),
        in_specs=[VM] * 3,
        out_specs=VM,
        compiler_params=params(),
        name="front",
    )(x, gain, w)


def allowed_tile(j, i, prompt, seg_col, seg_row):
    mask = None
    if i == j:
        mask = iota((QB, QB), 0) <= iota((QB, QB), 1)
    if (j + 1) * QB > prompt:
        segs = seg_col[j * QB : (j + 1) * QB, :]
        same = segs == seg_row[:, i * QB : (i + 1) * QB]
        if j * QB < prompt:
            same = same | (segs < 0)
        mask = same if mask is None else mask & same
    return mask


def attend_kernel(prompt, seg_row, seg_col, q_ref, k_ref, v_ref, o_ref, lse_ref, vt):
    half = lax.rem(pl.program_id(0), 2)
    blocks = q_ref.shape[0] // QB
    width = q_ref.shape[1]
    lanes = iota((1, width), 1) // HEAD_DIM == half
    const = HEAD_DIM ** (-0.5) * LOG2E
    vt[0:width, :] = v_ref[...].T
    vt[width : width + 16, :] = jnp.ones((16, vt.shape[1]), BF)
    for i in range(blocks):
        rows = slice(i * QB, (i + 1) * QB)
        q = jnp.where(lanes, q_ref[rows, :], jnp.zeros((), BF))
        tiles = []
        for j in range(i + 1):
            s = nt(k_ref[j * QB : (j + 1) * QB, :], q)
            mask = allowed_tile(j, i, prompt, seg_col, seg_row)
            if mask is not None:
                s = jnp.where(mask, s, NEGATIVE)
            tiles.append(s)
        top = functools.reduce(jnp.maximum, [jnp.max(s, axis=0, keepdims=True) for s in tiles])
        top = top * const
        acc = None
        for j, s in enumerate(tiles):
            p = jnp.exp2(s * const - top).astype(BF)
            part = nn(vt[:, j * QB : (j + 1) * QB], p)
            acc = part if acc is None else acc + part
        total = acc[width : width + 1, :]
        lse_ref[0, 0:1, rows] = top + jnp.log2(total)
        out = (acc[0:width, :] * (1.0 / total)).T.astype(BF)
        o_ref[rows, :] = jnp.where(lanes, out, o_ref[rows, :])


def attend(qkv, seg_row, seg_col, prompt):
    group, cols = qkv.shape
    pairs = cols // 3 // 128
    return pl.pallas_call(
        functools.partial(attend_kernel, prompt),
        grid=(2 * pairs,),
        out_shape=(sds((group, cols // 3), BF), sds((2 * pairs, 8, group), F32)),
        in_specs=[
            pl.BlockSpec((1, group), lambda h: (0, 0)),
            pl.BlockSpec((group, 1), lambda h: (0, 0)),
            pl.BlockSpec((group, 128), lambda h: (0, h // 2)),
            pl.BlockSpec((group, 128), lambda h: (0, pairs + h // 2)),
            pl.BlockSpec((group, 128), lambda h: (0, 2 * pairs + h // 2)),
        ],
        out_specs=(
            pl.BlockSpec((group, 128), lambda h: (0, h // 2)),
            pl.BlockSpec((1, 8, group), lambda h: (h, 0, 0)),
        ),
        scratch_shapes=[pltpu.VMEM((128 + 16, group), BF)],
        compiler_params=params(),
        name="attend",
    )(seg_row, seg_col, qkv, qkv, qkv)


def attend_back_kernel(
    prompt, seg_row, seg_col, q_ref, k_ref, v_ref, o_ref, lse_ref, do_ref, dq_ref, dk_ref, dv_ref,
    qm, dom, kt, dqt,
):
    half = lax.rem(pl.program_id(0), 2)
    blocks = q_ref.shape[0] // QB
    width = q_ref.shape[1]
    lanes = iota((1, width), 1) // HEAD_DIM == half
    scale = HEAD_DIM ** (-0.5)
    zero = jnp.zeros((), BF)
    qm[...] = jnp.where(lanes, q_ref[...], zero) * jnp.asarray(scale, BF)
    dom[...] = jnp.where(lanes, do_ref[...], zero)
    kt[...] = k_ref[...].T
    prod = (dom[...].astype(F32) * o_ref[...].astype(F32)).T
    delta = jnp.sum(prod, axis=0, keepdims=True)
    lse = lse_ref[0, 0:1, :]
    for j in range(blocks):
        keys = slice(j * QB, (j + 1) * QB)
        k, v = k_ref[keys, :], v_ref[keys, :]
        dk = dv = None
        for i in range(j, blocks):
            rows = slice(i * QB, (i + 1) * QB)
            s = nt(k, qm[rows, :])
            dp = nt(v, dom[rows, :])
            p = jnp.exp2(s * LOG2E - lse[:, rows])
            mask = allowed_tile(j, i, prompt, seg_col, seg_row)
            if mask is not None:
                p = jnp.where(mask, p, 0.0)
            ds = (p * (dp - delta[:, rows])).astype(BF)
            a = nn(p.astype(BF), dom[rows, :])
            b = nn(ds, qm[rows, :])
            c = nn(kt[:, keys], ds)
            dv = a if dv is None else dv + a
            dk = b if dk is None else dk + b
            dqt[:, rows] = c if j == 0 else dqt[:, rows] + c
        dk_ref[keys, :] = jnp.where(lanes, dk.astype(BF), dk_ref[keys, :])
        dv_ref[keys, :] = jnp.where(lanes, dv.astype(BF), dv_ref[keys, :])
    dq = (dqt[...] * scale).T.astype(BF)
    dq_ref[...] = jnp.where(lanes, dq, dq_ref[...])


def attend_back(qkv, seg_row, seg_col, out, lse, grad, prompt):
    group, cols = qkv.shape
    pairs = cols // 3 // 128
    pair = pl.BlockSpec((group, 128), lambda h: (0, h // 2))
    return pl.pallas_call(
        functools.partial(attend_back_kernel, prompt),
        grid=(2 * pairs,),
        out_shape=tuple([sds((group, cols // 3), BF)] * 3),
        in_specs=[
            pl.BlockSpec((1, group), lambda h: (0, 0)),
            pl.BlockSpec((group, 1), lambda h: (0, 0)),
            pair,
            pl.BlockSpec((group, 128), lambda h: (0, pairs + h // 2)),
            pl.BlockSpec((group, 128), lambda h: (0, 2 * pairs + h // 2)),
            pair,
            pl.BlockSpec((1, 8, group), lambda h: (h, 0, 0)),
            pair,
        ],
        out_specs=(pair, pair, pair),
        scratch_shapes=[
            pltpu.VMEM((group, 128), BF),
            pltpu.VMEM((group, 128), BF),
            pltpu.VMEM((128, group), BF),
            pltpu.VMEM((128, group), F32),
        ],
        compiler_params=params(),
        name="attend_back",
    )(seg_row, seg_col, qkv, qkv, qkv, out, lse, grad)


def slot_rows(places_row, e, capacity):
    rows = places_row[e : e + 1, :]
    return (rows == iota((capacity, 1), 0).astype(F32)).astype(F32).astype(BF)


def slot_cols(places_col, e, capacity):
    cols = places_col[:, e : e + 1]
    return (cols == iota((1, capacity), 1).astype(F32)).astype(F32).astype(BF)


def take_kernel(capacity, places_row, rows_ref, out_ref):
    for e in range(EXPERTS):
        out_ref[e] = nn(slot_rows(places_row, e, capacity), rows_ref[...]).astype(BF)


def take(places_row, rows, capacity):
    return pl.pallas_call(
        functools.partial(take_kernel, capacity),
        out_shape=sds((EXPERTS, capacity, rows.shape[1]), BF),
        in_specs=[VM] * 2,
        out_specs=VM,
        compiler_params=params(),
        name="take",
    )(places_row, rows)


def softmax_lanes(logits):
    live = iota(logits.shape, 1) < EXPERTS
    logits = jnp.where(live, logits, NEGATIVE)
    expo = jnp.where(live, jnp.exp(logits - jnp.max(logits, axis=1, keepdims=True)), 0.0)
    return expo / jnp.sum(expo, axis=1, keepdims=True)


def middle_kernel(
    capacity, x_ref, att_ref, w_ref, gain_ref, router_ref, places_row, places_col,
    hidden_ref, probs_ref, in_ref, gate_ref,
):
    hidden = x_ref[...].astype(F32) + nn(att_ref[...], w_ref[...])
    hidden_ref[...] = hidden
    r_two = lax.rsqrt(jnp.mean(hidden * hidden, axis=1, keepdims=True) + EPSILON)
    routed = (hidden * r_two * gain_ref[...]).astype(BF)
    probs = softmax_lanes(nn(routed, router_ref[...]))
    probs_ref[...] = probs
    flat = probs.T[0:8, :]
    high = flat.astype(BF)
    rest = flat - high.astype(F32)
    mid = rest.astype(BF)
    low = (rest - mid.astype(F32)).astype(BF)
    split = jnp.concatenate([high.astype(F32), mid.astype(F32), low.astype(F32)], axis=0).astype(BF)
    for e in range(EXPERTS):
        in_ref[e] = nn(slot_rows(places_row, e, capacity), routed).astype(BF)
        three = nn(split, slot_cols(places_col, e, capacity))
        gate = three[0:8] + three[8:16] + three[16:24]
        gate_ref[e] = jnp.broadcast_to(gate[e : e + 1, :], gate.shape)


def middle(x, attended, w_proj, gain, router, places_row, places_col, capacity):
    rows, width = x.shape
    return pl.pallas_call(
        functools.partial(middle_kernel, capacity),
        out_shape=(
            sds((rows, width), F32),
            sds((rows, 128), F32),
            sds((EXPERTS, capacity, width), BF),
            sds((EXPERTS, 8, capacity), F32),
        ),
        in_specs=[VM] * 7,
        out_specs=(VM,) * 4,
        compiler_params=params(),
        name="middle",
    )(x, attended, w_proj, gain, router, places_row, places_col)


def expert_kernel(
    in_ref, raw_ref, gate_ref, w_ref, res_ref, gin_ref, dot_ref, dw_ref, grad, res_acc, gin_acc
):
    step = pl.program_id(0)
    sources, slots, width = in_ref.shape
    flat = sources * slots

    @pl.when(step == 0)
    def _():
        for i in range(sources):
            gate = gate_ref[i].T[:, 0:1]
            grad[i * slots : (i + 1) * slots, :] = (raw_ref[i].astype(F32) * gate).astype(BF)

    first, second = w_ref[:, :width], w_ref[:, width:]
    x = in_ref[...].reshape(flat, width)
    g = grad[...]
    pre = nt(x, first)
    back = nt(g, second)
    a, b = 0.7978845608028654, 0.7978845608028654 * 0.044715
    square = pre * pre
    t = jnp.tanh(pre * (a + b * square))
    rise = 0.5 + 0.5 * t
    act = (pre * rise).astype(BF)
    slope = rise + (0.5 * pre) * (1.0 - t * t) * (a + (3.0 * b) * square)
    grad_pre = (back * slope).astype(BF)
    res = nn(act, second)
    gin = nn(grad_pre, first)

    @pl.when(step == 0)
    def _():
        res_acc[...] = res
        gin_acc[...] = gin

    @pl.when(step > 0)
    def _():
        res_acc[...] += res
        gin_acc[...] += gin

    dw_ref[:, :width] = tn(grad_pre, x).astype(BF)
    dw_ref[:, width:] = tn(act, g).astype(BF)

    @pl.when(step == pl.num_programs(0) - 1)
    def _():
        for i in range(sources):
            rows = slice(i * slots, (i + 1) * slots)
            res_ref[i] = res_acc[rows, :].astype(BF)
            gin_ref[i] = gin_acc[rows, :].astype(BF)
            prod = res_acc[rows, :] * raw_ref[i].astype(F32)
            narrow = functools.reduce(
                jnp.add, [prod[:, j : j + 128] for j in range(0, width, 128)]
            )
            inner = jnp.sum(narrow.T, axis=0, keepdims=True)
            dot_ref[i] = jnp.broadcast_to(inner, (8, slots))


def expert(expert_in, raw, gate, w, chunk):
    sources, slots, width = expert_in.shape
    hidden = w.shape[0]
    flat = sources * slots
    whole = lambda shape: pl.BlockSpec(shape, lambda s: (0,) * len(shape))
    rows = whole((sources, slots, width))
    small = whole((sources, 8, slots))
    piece = pl.BlockSpec((chunk, 2 * width), lambda s: (s, 0))
    return pl.pallas_call(
        expert_kernel,
        grid=(hidden // chunk,),
        out_shape=(
            sds((sources, slots, width), BF),
            sds((sources, slots, width), BF),
            sds((sources, 8, slots), F32),
            sds((hidden, 2 * width), BF),
        ),
        in_specs=[rows, rows, small, piece],
        out_specs=(rows, rows, small, piece),
        scratch_shapes=[
            pltpu.VMEM((flat, width), BF),
            pltpu.VMEM((flat, width), F32),
            pltpu.VMEM((flat, width), F32),
        ],
        compiler_params=params(),
        name="expert",
    )(expert_in, raw, gate, w)


def after_kernel(
    capacity, res_ref, gin_ref, dot_ref, hidden_ref, probs_ref, places_col, cot_ref, gain_ref,
    router_ref, w_ref, att_ref, out_ref, gh_ref, gatt_ref, dw_ref, dr_ref, dg_ref,
):
    hidden = hidden_ref[...]
    probs = probs_ref[...]
    gain = gain_ref[...]
    lane = iota(probs.shape, 1)
    total = hidden
    back = None
    grad_probs = jnp.zeros_like(probs)
    for e in range(EXPERTS):
        pick = slot_cols(places_col, e, capacity)
        total = total + probs[:, e : e + 1] * nn(pick, res_ref[e])
        part = nn(pick, gin_ref[e])
        back = part if back is None else back + part
        inner = jnp.sum(pick.astype(F32) * dot_ref[e][0:1, :], axis=1, keepdims=True)
        grad_probs = jnp.where(lane == e, inner, grad_probs)
    out_ref[...] = total.astype(BF)
    mixed = jnp.sum(probs * grad_probs, axis=1, keepdims=True)
    grad_logits = probs * (grad_probs - mixed)
    low = grad_logits.astype(BF)
    r_two = lax.rsqrt(jnp.mean(hidden * hidden, axis=1, keepdims=True) + EPSILON)
    h_norm = hidden * r_two
    routed = (h_norm * gain).astype(BF)
    dr_ref[...] = tn(routed, low)
    grad_routed = back + nt(low, router_ref[...])
    dg_ref[...] = jnp.sum(grad_routed * h_norm, axis=0, keepdims=True)
    u = grad_routed * gain
    grad_hidden = cot_ref[...].astype(F32) + r_two * (
        u - h_norm * jnp.mean(u * h_norm, axis=1, keepdims=True)
    )
    gh_ref[...] = grad_hidden
    hid_low = grad_hidden.astype(BF)
    gatt_ref[...] = nt(hid_low, w_ref[...]).astype(BF)
    dw_ref[...] = tn(att_ref[...], hid_low).astype(BF)


def after(res, gin, inner, hidden, probs, places_col, cot, gain, router, w_proj, attended, capacity):
    rows, width = hidden.shape
    return pl.pallas_call(
        functools.partial(after_kernel, capacity),
        out_shape=(
            sds((rows, width), BF),
            sds((rows, width), F32),
            sds((rows, width), BF),
            sds((width, width), BF),
            sds((width, 128), F32),
            sds((1, width), F32),
        ),
        in_specs=[VM] * 11,
        out_specs=(VM,) * 6,
        compiler_params=params(),
        name="after",
    )(res, gin, inner, hidden, probs, places_col, cot, gain, router, w_proj, attended)


def tail_kernel(x_ref, gain_ref, gp_ref, w_ref, gh_ref, dx_ref, dw_ref, dg_ref):
    x = x_ref[...].astype(F32)
    gain = gain_ref[...]
    r_one = lax.rsqrt(jnp.mean(x * x, axis=1, keepdims=True) + EPSILON)
    x_norm = x * r_one
    normed = (x_norm * gain).astype(BF)
    cols = 768
    for j in range(0, gp_ref.shape[1], cols):
        dw_ref[:, j : j + cols] = tn(normed, gp_ref[:, j : j + cols]).astype(BF)
    grad = nt(gp_ref[...], w_ref[...])
    dg_ref[...] = jnp.sum(grad * x_norm, axis=0, keepdims=True)
    u = grad * gain
    dx = gh_ref[...] + r_one * (u - x_norm * jnp.mean(u * x_norm, axis=1, keepdims=True))
    dx_ref[...] = dx.astype(BF)


def tail(x, gain, grad_proj, w_qkv, grad_hidden):
    rows, width = x.shape
    return pl.pallas_call(
        tail_kernel,
        out_shape=(sds((rows, width), BF), sds(w_qkv.shape, BF), sds((1, width), F32)),
        in_specs=[VM] * 5,
        out_specs=(VM,) * 3,
        compiler_params=params(),
        name="tail",
    )(x, gain, grad_proj, w_qkv, grad_hidden)


def shards(tokens, attn_in, attn_out, router, gains, expert_w, expert_ids, segments, cotangent):
    x = tokens[0]
    cot = cotangent[0]
    rows, width = x.shape
    nz = lax.axis_size("fsdp")
    group = 2 * rows
    prompt = group - segments.shape[1]
    capacity = 2 * rows // EXPERTS
    dp, sq = lax.axis_index("dp"), lax.axis_index("seq")
    core = lax.rem(dp, 2)
    mine = (dp // 2) * 2 + sq

    chosen = jnp.sum(
        (expert_ids[0][:, :, None] == jnp.arange(EXPERTS, dtype=jnp.int32)).astype(F32), axis=1
    )
    earlier = (iota((rows, rows), 1) < iota((rows, rows), 0)).astype(BF)
    before = nn(earlier, chosen.astype(BF))
    places = jnp.where(chosen > 0, before, -1.0)
    places_col = jnp.pad(places, ((0, 0), (0, 128 - EXPERTS)), constant_values=-1.0)
    places_row = jnp.pad(places.T, ((0, 8 - EXPERTS), (0, 0)), constant_values=-1.0)
    seg_full = jnp.concatenate([jnp.full((prompt,), -1, jnp.int32), segments[0]])
    seg_row, seg_col = seg_full[None, :], seg_full[:, None]

    packed = jnp.concatenate(
        [attn_in, attn_out, jnp.pad(jnp.concatenate([router, gains], axis=1), ((0, 0), (0, 122)))],
        axis=1,
    )
    whole = lax.all_gather(packed, "fsdp", axis=0, tiled=True)
    w_qkv, w_proj, small = whole[:, : 3 * width], whole[:, 3 * width : 4 * width], whole[:, 4 * width :]
    w_route = jnp.where(jnp.arange(128) < EXPERTS, small, jnp.zeros((), BF))
    gain_rows = small[:, EXPERTS : EXPERTS + 2].astype(F32).T
    gain_one, gain_two = gain_rows[0:1], gain_rows[1:2]
    shard = expert_w.shape[0]
    part = shard // 2
    piece = lax.dynamic_slice(expert_w, (core * part, mine, 0), (part, 1, 2 * width))[:, 0]
    pieces = lax.all_gather(piece, "fsdp", axis=0, tiled=False)

    proj = front(x, gain_one, w_qkv)
    raw = take(places_row, cot, capacity)
    qkv = heads_in(proj, 3, 0)
    mixed, lse = attend(qkv, seg_row, seg_col, prompt)
    attended = heads_out([mixed], 1)
    hidden, probs, expert_in, gate = middle(
        x, attended, w_proj, gain_two, w_route, places_row, places_col, capacity
    )
    there_in, there_raw, there_gate = chips([expert_in, raw, gate], 2)
    w_mine = cores_join(pieces, 3).reshape(nz * shard, 2 * width)
    res, gin, inner, dw = expert(there_in, there_raw, there_gate, w_mine, 512)
    back_res, back_gin, back_inner = chips([res, gin, inner], 4)
    block_out, grad_hidden, grad_att, d_out, d_route, d_gain_two = after(
        back_res, back_gin, back_inner, hidden, probs, places_col, cot, gain_two, w_route, w_proj,
        attended, capacity,
    )
    dw_half = cores_sum(dw.reshape(nz, 2, part, 2 * width), 5)
    dw_own = lax.psum_scatter(
        dw_half.reshape(nz * part, 2 * width), "fsdp", scatter_dimension=0, tiled=True
    )

    grad_mixed = heads_in(grad_att, 1, 6)
    dq, dk, dv = attend_back(qkv, seg_row, seg_col, mixed, lse, grad_mixed, prompt)
    grad_proj = heads_out([dq, dk, dv], 7)
    d_tokens, d_in, d_gain_one = tail(x, gain_one, grad_proj, w_qkv, grad_hidden)

    dw_all = lax.all_gather(dw_own, ("dp", "seq"), axis=0, tiled=False)
    dw_all = dw_all.reshape(2, 2, 2, part, 2 * width).transpose(1, 3, 0, 2, 4)
    d_expert = dw_all.reshape(shard, EXPERTS, 2 * width).astype(F32)

    d_gains = jnp.concatenate([d_gain_one, d_gain_two], axis=0).T
    d_small = jnp.pad(jnp.concatenate([d_route[:, :EXPERTS], d_gains], axis=1), ((0, 0), (0, 122)))
    grads = jnp.concatenate([d_in, d_out, d_small.astype(BF)], axis=1)
    own = lax.psum_scatter(grads, "fsdp", scatter_dimension=0, tiled=True)
    total = lax.psum(own, ("dp", "seq")).astype(F32)
    return (
        block_out[None],
        d_tokens[None],
        total[:, : 3 * width],
        total[:, 3 * width : 4 * width],
        total[:, 4 * width : 4 * width + EXPERTS],
        total[:, 4 * width + EXPERTS : 4 * width + EXPERTS + 2],
        d_expert,
    )


def solution(mesh):
    in_specs = (
        P(("dp", "fsdp"), "seq", None),
        P("fsdp", None),
        P("fsdp", None),
        P("fsdp", None),
        P("fsdp", None),
        P("fsdp", None, None),
        P(("dp", "fsdp"), "seq", None),
        P(("dp", "fsdp"), None),
        P(("dp", "fsdp"), "seq", None),
    )
    out_specs = (
        P(("dp", "fsdp"), "seq", None),
        P(("dp", "fsdp"), "seq", None),
        P("fsdp", None),
        P("fsdp", None),
        P("fsdp", None),
        P("fsdp", None),
        P("fsdp", None, None),
    )
    return jax.shard_map(shards, mesh=mesh, in_specs=in_specs, out_specs=out_specs, check_vma=False)
```

```python
import functools

import jax
import jax.numpy as jnp
from jax import lax
from jax.experimental import pallas as pl
from jax.experimental.pallas import tpu as pltpu
from jax.sharding import PartitionSpec as P

HEADS = 12
HEAD_DIM = 64
EXPERTS = 4
PROMPT = 1024
EPSILON = 1e-06
NEGATIVE = -1e30
HIGH = lax.Precision.HIGHEST
LOG2E = 1.4426950408889634
BF = jnp.bfloat16
F32 = jnp.float32
MESH = pl.DeviceIdType.MESH
VMEM_LIMIT = 60 << 20
QB = 256
ANY = pl.BlockSpec(memory_space=pl.ANY)
VM = pl.BlockSpec(memory_space=pltpu.VMEM)


def nn(a, b):
    return lax.dot_general(a, b, (((1,), (0,)), ((), ())), preferred_element_type=F32)


def nt(a, b):
    return lax.dot_general(a, b, (((1,), (1,)), ((), ())), preferred_element_type=F32)


def tn(a, b):
    return lax.dot_general(a, b, (((0,), (0,)), ((), ())), preferred_element_type=F32)


def iota(shape, dim):
    return lax.broadcasted_iota(jnp.int32, shape, dim)


def params(cid=None):
    if cid is None:
        return pltpu.CompilerParams(vmem_limit_bytes=VMEM_LIMIT)
    return pltpu.CompilerParams(
        vmem_limit_bytes=VMEM_LIMIT, collective_id=cid, has_side_effects=True
    )


def sds(shape, dtype):
    return jax.ShapeDtypeStruct(shape, dtype)


def place():
    dp, sq, z = lax.axis_index("dp"), lax.axis_index("seq"), lax.axis_index("fsdp")
    return dp, sq, z, dp // 2, lax.rem(dp, 2)


def greet(peers):
    barrier = pltpu.get_barrier_semaphore()
    for peer in peers:
        pl.semaphore_signal(barrier, inc=1, device_id=peer, device_id_type=MESH)
    pl.semaphore_wait(barrier, len(peers))


def remote(src, dst, send, recv, peer):
    return pltpu.make_async_remote_copy(
        src_ref=src, dst_ref=dst, send_sem=send, recv_sem=recv, device_id=peer, device_id_type=MESH
    )


def al(x):
    return pl.multiple_of(x, 128)


def allowed_tile(j, i, prompt, seg_col, seg_row):
    mask = None
    if i == j:
        mask = iota((QB, QB), 0) <= iota((QB, QB), 1)
    if j * QB >= prompt:
        keys, queries = j * QB - prompt, i * QB - prompt
        same = seg_col[keys : keys + QB, :] == seg_row[:, queries : queries + QB]
        mask = same if mask is None else mask & same
    return mask


def flip_chip(x, sq, fx, fy):
    px = 1 - x if fx else x
    py = 1 - sq if fy else sq
    return px, py


SOURCES = ((1, 0), (0, 1), (0, 0), (1, 1))
OWN = 2
AWAY = (0, 1, 3)


class Line:
    def __init__(self, nz, dp, sq, z, sources, target, sems):
        self.nz, self.dp, self.sq, self.z = nz, dp, sq, z
        self.sources, self.target, self.sems = sources, target, sems

    def copy(self, stage, up):
        nz, z = self.nz, self.z
        zone = z - (stage - 1) if up else z + (stage - 1)
        zone = lax.rem(zone + nz, nz)
        to = lax.rem(z + 1, nz) if up else lax.rem(z + nz - 1, nz)
        i = stage - 1
        send, recv = (self.sems[0], self.sems[1]) if up else (self.sems[2], self.sems[3])
        return remote(
            self.sources(stage, zone), self.target.at[zone], send.at[i], recv.at[i], (self.dp, self.sq, to)
        )

    def arrival(self, stage, up):
        nz, z = self.nz, self.z
        zone = lax.rem((z - stage if up else z + stage) + nz, nz)
        to = lax.rem(z + 1, nz) if up else lax.rem(z + nz - 1, nz)
        i = stage - 1
        send, recv = (self.sems[0], self.sems[1]) if up else (self.sems[2], self.sems[3])
        return remote(
            self.sources(stage, zone), self.target.at[zone], send.at[i], recv.at[i], (self.dp, self.sq, to)
        )

    def sends(self, stage, up):
        z, nz = self.z, self.nz
        return (z < nz - 1) & (z >= stage - 1) if up else (z > 0) & (z <= nz - stage)

    def gets(self, stage, up):
        return self.z >= stage if up else self.z <= self.nz - 1 - stage

    def start(self, stage):
        for up in (True, False):

            @pl.when(self.sends(stage, up))
            def _(up=up):
                self.copy(stage, up).start()

    def wait_recv(self, stage):
        for up in (True, False):

            @pl.when(self.gets(stage, up))
            def _(up=up):
                self.arrival(stage, up).wait_recv()

    def wait_send(self, stage):
        for up in (True, False):

            @pl.when(self.sends(stage, up))
            def _(up=up):
                self.copy(stage, up).wait_send()


def eighth(x, prompt):
    row = x.astype(F32)
    col = jnp.broadcast_to(row, (128, row.shape[1])).T[:, 0:1]
    return row, col


def begin_kernel(
    prompt, nz, capacity, x_ref, in_ref, out_ref, router_ref, gains_ref, seg_ref, ids_ref, cot_ref, piece_ref,
    xs_ref, w_ref, qkv_ref, mixed_ref, lse_ref, att_ref, raw_ref, row_ref, col_ref, near_ref,
    pack, vt, local, send_t, recv_t, send_z, recv_z, send_p, recv_p, send_c, recv_c, send_o, recv_o, *line_sems,
):
    dp, sq, z, x, core = place()
    rows, width = x_ref.shape
    shard = in_ref.shape[0]
    part = shard // 4
    half = width // 2
    pairs = half // 128
    own_cols = 3 * half
    lead = own_cols + 128
    sibling = (x * 2 + 1 - core, sq, z)
    partner = (dp, 1 - sq, z)
    across = ((1 - x) * 2 + core, sq, z)
    others = [(dp, sq, lax.rem(z + d, nz)) for d in range(1, nz)]
    base = pl.multiple_of(sq * rows, rows)
    there = pl.multiple_of((1 - sq) * rows, rows)
    groups = (pl.ds(0, lead), pl.ds(lead, width))

    packs = [
        pltpu.make_async_copy(
            in_ref.at[:, pl.ds(al(i * width + sq * half), half)], pack.at[:, pl.ds(i * half, half)], local.at[i]
        )
        for i in range(3)
    ]
    packs.append(pltpu.make_async_copy(out_ref, pack.at[:, groups[1]], local.at[3]))
    for c in packs:
        c.start()
    lane = iota((1, 128), 1)
    small = jnp.zeros((shard, 128), F32)
    for e in range(EXPERTS):
        small = jnp.where(lane == e, router_ref[:, e : e + 1].astype(F32), small)
    for e in range(2):
        small = jnp.where(lane == EXPERTS + e, gains_ref[:, e : e + 1].astype(F32), small)
    pack[:, own_cols:lead] = small.astype(BF)
    greet([sibling, partner, across] + others)
    tokens = remote(x_ref, xs_ref.at[pl.ds(base, rows)], send_t, recv_t, partner)
    tokens.start()
    for c in packs:
        c.wait()

    def at(zs, px, co, g):
        return w_ref.at[pl.ds(pl.multiple_of(zs * shard + (px * 2 + co) * part, part), part), groups[g]]

    def along(d, g):
        src = pack.at[pl.ds(pl.multiple_of((x * 2 + core) * part, part), part), groups[g]]
        return remote(src, at(z, x, core, g), send_z.at[d - 1, g], recv_z.at[d - 1, g], others[d - 1])

    def source(d):
        return lax.rem(z + nz - d, nz)

    def over(d, g, px):
        ref = at(source(d), px, core, g)
        return remote(ref, ref, send_p.at[d - 1, g], recv_p.at[d - 1, g], across)

    def beside(d, g, i, co):
        ref = at(source(d), (x, 1 - x)[i], co, g)
        return remote(ref, ref, send_c.at[d - 1, g, i], recv_c.at[d - 1, g, i], sibling)

    for d in range(1, nz):
        along(d, 0).start()
    own = pltpu.make_async_copy(pack, w_ref.at[pl.ds(pl.multiple_of(z * shard, shard), shard)], local.at[4])
    own.start()
    xs_ref[pl.ds(base, rows), :] = x_ref[...]
    ids = ids_ref[...]
    chosen = jnp.where((ids[:, 0:1] == lane) | (ids[:, 1:2] == lane), 1.0, 0.0)
    earlier = (iota((rows, rows), 1) < iota((rows, rows), 0)).astype(F32).astype(BF)
    places = jnp.where(chosen > 0, nn(earlier, chosen.astype(BF)), -1.0)
    col_ref[...] = places
    places = places.T[0:8, :]
    row_ref[...] = places

    def gather(g):
        for d in range(1, nz):
            along(d, g).wait_recv()
            over(d, g, x).start()
            beside(d, g, 0, core).start()
        if g == 0:
            line.start(1)
            for d in range(1, nz):
                along(d, 1).start()
        for d in range(1, nz):
            over(d, g, 1 - x).wait_recv()
            beside(d, g, 1, core).start()

    def gathered(g):
        for d in range(1, nz):
            for i in range(2):
                beside(d, g, i, 1 - core).wait_recv()

    stay = pltpu.make_async_copy(piece_ref, near_ref.at[z], local.at[5])
    stay.start()
    line = Line(
        nz, dp, sq, z, lambda stage, zone: piece_ref if stage == 1 else near_ref.at[zone], near_ref, line_sems
    )
    gather(0)
    gathered(0)
    own.wait()
    tokens.wait_recv()

    gain = w_ref[:, own_cols:lead].astype(F32).T[EXPERTS : EXPERTS + 1, :]
    xf = xs_ref[...].astype(F32)
    normed = (xf * lax.rsqrt(jnp.mean(xf * xf, axis=1, keepdims=True) + EPSILON) * gain).astype(BF)
    for i in range(3):
        got = nn(normed, w_ref[:, i * half : (i + 1) * half]).astype(BF)
        for p in range(pairs):
            qkv_ref[p, i] = got[:, p * 128 : (p + 1) * 128]

    blocks = 2 * rows // QB
    const = HEAD_DIM ** (-0.5) * LOG2E
    seg_row, seg_col = eighth(seg_ref[...], prompt)

    def back(p, own_side):
        src = mixed_ref.at[p, pl.ds(there, rows)]
        side = sq if own_side else 1 - sq
        return remote(
            src, att_ref.at[:, pl.ds(al(side * half + p * 128), 128)], send_o.at[p], recv_o.at[p], partner
        )

    @pl.loop(0, pairs)
    def _(p):
        vt[0:128, :] = qkv_ref[p, 2].T
        vt[128:144, :] = jnp.ones((16, vt.shape[1]), BF)
        for i in range(blocks):
            here = slice(i * QB, (i + 1) * QB)
            both = []
            for h in range(2):
                lanes = iota((1, 128), 1) // HEAD_DIM == h
                q = jnp.where(lanes, qkv_ref[p, 0, here, :], jnp.zeros((), BF))
                tiles = []
                for j in range(i + 1):
                    s = nt(qkv_ref[p, 1, j * QB : (j + 1) * QB, :], q)
                    mask = allowed_tile(j, i, prompt, seg_col, seg_row)
                    if mask is not None:
                        s = jnp.where(mask, s, NEGATIVE)
                    tiles.append(s)
                top = functools.reduce(
                    jnp.maximum, [jnp.max(s, axis=0, keepdims=True) for s in tiles]
                )
                top = top * const
                acc = None
                for j, s in enumerate(tiles):
                    pr = jnp.exp2(s * const - top).astype(BF)
                    add = nn(vt[:, j * QB : (j + 1) * QB], pr)
                    acc = add if acc is None else acc + add
                total = acc[128:129, :]
                lse_ref[p, h : h + 1, here] = top + jnp.log2(total)
                low = h * HEAD_DIM
                both.append(acc[low : low + HEAD_DIM, :] * (1.0 / total))
            mixed_ref[p, here, :] = jnp.concatenate(both, axis=0).T.astype(BF)
        back(p, True).start()
        att_ref[:, pl.ds(al(sq * half + p * 128), 128)] = mixed_ref[p, pl.ds(base, rows), :]

        @pl.when(p == 0)
        def _():
            line.wait_recv(1)
            line.start(2)
            gather(1)

    for j, (px, py) in enumerate([flip_chip(x, sq, *f) for f in SOURCES]):
        hot = hot_rows(pick_row(row_ref[...], px * 2 + py), capacity)
        raw_ref[j] = nn(hot, cot_ref[...]).astype(BF)
    for p in range(pairs):
        back(p, False).wait_recv()
        back(p, True).wait_send()
    gathered(1)
    tokens.wait_send()
    for g in range(2):
        for d in range(1, nz):
            along(d, g).wait_send()
            over(d, g, x).wait_send()
            for i in range(2):
                beside(d, g, i, core).wait_send()
    line.wait_recv(2)
    line.wait_send(1)
    line.wait_send(2)
    stay.wait()


def begin(x, attn_in, attn_out, router, gains, segments, ids, cot, piece, prompt, nz, capacity, cid):
    rows, width = x.shape
    shard = attn_in.shape[0]
    pairs = width // 256
    cols = 3 * width // 2 + 128 + width
    dma = pltpu.SemaphoreType.DMA
    two = lambda *shape: [dma(shape), dma(shape)]
    return pl.pallas_call(
        functools.partial(begin_kernel, prompt, nz, capacity),
        out_shape=(
            sds((2 * rows, width), BF),
            sds((shard * nz, cols), BF),
            sds((pairs, 3, 2 * rows, 128), BF),
            sds((pairs, 2 * rows, 128), BF),
            sds((pairs, 8, 2 * rows), F32),
            sds((rows, width), BF),
            sds((4, capacity, width), BF),
            sds((8, rows), F32),
            sds((rows, 128), F32),
            sds((nz,) + piece.shape, BF),
        ),
        in_specs=[VM, ANY, ANY, VM, VM, VM, VM, VM, ANY],
        out_specs=(VM,) * 9 + (ANY,),
        scratch_shapes=[
            pltpu.VMEM((shard, cols), BF),
            pltpu.VMEM((144, 2 * rows), BF),
            dma((6,)),
        ]
        + two() + two(nz - 1, 2) + two(nz - 1, 2) + two(nz - 1, 2, 2) + two(pairs) + two(2) + two(2),
        compiler_params=params(cid),
        name="begin",
    )(x, attn_in, attn_out, router, gains, segments, ids, cot, piece)


def softmax_lanes(logits):
    live = iota(logits.shape, 1) < EXPERTS
    logits = jnp.where(live, logits, NEGATIVE)
    expo = jnp.where(live, jnp.exp(logits - jnp.max(logits, axis=1, keepdims=True)), 0.0)
    return expo / jnp.sum(expo, axis=1, keepdims=True)


def pick_row(table, e):
    return jnp.sum(jnp.where(iota((8, 1), 0) == e, table, 0.0), axis=0, keepdims=True)


def pick_col(table, e):
    return jnp.sum(jnp.where(iota((1, 128), 1) == e, table, 0.0), axis=1, keepdims=True)


def hot_rows(row, capacity):
    return (row == iota((capacity, 1), 0).astype(F32)).astype(F32).astype(BF)


def hot_cols(col, capacity):
    return (col == iota((1, capacity), 1).astype(F32)).astype(F32).astype(BF)


GELU_A = 0.7978845608028654
GELU_B = GELU_A * 0.044715


def expert_step(x, g, w):
    width = x.shape[1]
    first, second = w[:, :width], w[:, width:]
    pre = nt(x, first)
    back = nt(g, second)
    square = pre * pre
    t = jnp.tanh(pre * (GELU_A + GELU_B * square))
    rise = 0.5 + 0.5 * t
    act = (pre * rise).astype(BF)
    slope = rise + (0.5 * pre) * (1.0 - t * t) * (GELU_A + (3.0 * GELU_B) * square)
    grad_pre = (back * slope).astype(BF)
    return nn(act, second), nn(grad_pre, first), tn(grad_pre, x), tn(act, g)


def experts_kernel(
    capacity, nz, x_ref, att_ref, w_hbm, places_row, places_col, raw_send, near_ref,
    hidden_ref, probs_ref, back_gin, out_res, back_dot, dw_ref,
    wp, send_in, got_in, send_gate, got_gate, own_w, theirs, grad, res_acc, gin_acc, out_gin, out_dot, dw_away, dw_got,
    raw_ref, local, send_x, recv_x, send_w, recv_w, send_i, recv_i, send_t, recv_t, send_r, recv_r, send_d, recv_d, send_v, recv_v, *line_sems,
):
    dp, sq, z, x, core = place()
    rows, width = x_ref.shape
    sibling = (x * 2 + 1 - core, sq, z)
    corner = [flip_chip(x, sq, *f) for f in SOURCES]
    plane = [(px * 2 + core, py, z) for px, py in corner]
    experts_of = [px * 2 + py for px, py in corner]
    below, above = (dp, sq, lax.rem(z + nz - 1, nz)), (dp, sq, lax.rem(z + 1, nz))
    shift = jnp.where(z >= nz // 2, 1, 0)
    far_zone = jnp.where(z >= nz // 2, 0, nz - 1)
    greet([sibling, below, above] + [plane[j] for j in AWAY])
    line = Line(nz, dp, sq, z, lambda stage, zone: near_ref.at[zone], own_w, line_sems)
    line.start(nz - 1)
    at_end = (z == 0) | (z == nz - 1)

    def go_raw(j):
        return remote(raw_send.at[j], raw_ref.at[j], send_x.at[j], recv_x.at[j], plane[j])

    go_raw(0).start()
    go_raw(1).start()

    def weights(slot):
        if slot == nz - 1:
            return remote(own_w.at[far_zone], theirs.at[far_zone], send_w.at[slot], recv_w.at[slot], sibling)
        zone = slot + shift
        return remote(near_ref.at[zone], theirs.at[zone], send_w.at[slot], recv_w.at[slot], sibling)

    lifts = []
    for i in range(nz - 1):
        weights(i).start()
        lifts.append(pltpu.make_async_copy(near_ref.at[i + shift], own_w.at[i + shift], local.at[2 + i]))
    for c in lifts:
        c.start()
    far_lift = pltpu.make_async_copy(near_ref.at[far_zone], own_w.at[far_zone], local.at[1 + nz])

    @pl.when(jnp.logical_not(at_end))
    def _():
        far_lift.start()

    own_raw = pltpu.make_async_copy(raw_send.at[OWN], raw_ref.at[OWN], local.at[1])
    own_raw.start()
    load = pltpu.make_async_copy(w_hbm.at[:, 3 * width // 2 :], wp, local.at[0])
    load.start()
    load.wait()

    hidden = x_ref[...].astype(F32) + nn(att_ref[...], wp[:, 128:])
    hidden_ref[...] = hidden
    r_two = lax.rsqrt(jnp.mean(hidden * hidden, axis=1, keepdims=True) + EPSILON)
    small = wp[:, :128]
    gain = small.astype(F32).T[EXPERTS + 1 : EXPERTS + 2, :]
    routed = (hidden * r_two * gain).astype(BF)
    probs = softmax_lanes(nn(routed, small))
    probs_ref[...] = probs
    flat = probs.T[0:8, :]
    high = flat.astype(BF)
    rest = flat - high.astype(F32)
    mid = rest.astype(BF)
    low = (rest - mid.astype(F32)).astype(BF)
    split = jnp.concatenate([high.astype(F32), mid.astype(F32), low.astype(F32)], axis=0).astype(BF)

    def go_in(j):
        return remote(send_in.at[j], got_in.at[j], send_i.at[j], recv_i.at[j], plane[j])

    def go_gate(j):
        return remote(send_gate.at[j], got_gate.at[j], send_t.at[j], recv_t.at[j], plane[j])

    for j in range(4):
        e = experts_of[j]
        taken = nn(hot_rows(pick_row(places_row[...], e), capacity), routed).astype(BF)
        three = nn(split, hot_cols(pick_col(places_col[...], e), capacity))
        gate = three[0:8] + three[8:16] + three[16:24]
        gate = jnp.broadcast_to(pick_row(gate, e), gate.shape)
        if j != OWN:
            send_in[j] = taken
            send_gate[j] = gate
            go_gate(j).start()
        if j < OWN:
            go_in(j).start()
        if j == OWN:
            got_in[j] = taken
            got_gate[j] = gate
    own_raw.wait()
    for c in lifts:
        c.wait()
    for i in range(nz - 1):
        weights(i).wait_recv()

    def go_gin(j):
        return remote(out_gin.at[j], back_gin.at[j], send_r.at[j], recv_r.at[j], plane[j])

    def go_dot(j):
        return remote(out_dot.at[j], back_dot.at[j], send_d.at[j], recv_d.at[j], plane[j])

    def go_dw(n):
        return remote(dw_away.at[n], dw_got.at[n], send_v.at[n], recv_v.at[n], sibling)

    def arrive(lo, hi):
        for j in range(lo, hi):
            if j != OWN:
                go_raw(j).wait_recv()
                go_in(j).wait_recv()
                go_gate(j).wait_recv()
            gate = got_gate[j].T[:, 0:1]
            grad[j] = (raw_ref[j].astype(F32) * gate).astype(BF)

    def chunk(lo, hi, w_ref, dw, d, first, at):
        count = (hi - lo) * capacity
        xs = got_in[lo:hi].reshape(count, width)
        gs = grad[lo:hi].reshape(count, width)
        res, gin, d_first, d_second = expert_step(xs, gs, w_ref[d])
        here = slice(at * capacity, at * capacity + count)
        res_acc[here, :] += res
        gin_acc[here, :] += gin
        if first:
            dw[d, :, :width] = d_first.astype(BF)
            dw[d, :, width:] = d_second.astype(BF)
        else:
            dw[d, :, :width] = (dw[d, :, :width].astype(F32) + d_first).astype(BF)
            dw[d, :, width:] = (dw[d, :, width:].astype(F32) + d_second).astype(BF)

    def send_back(lo, hi, at):
        for j in range(lo, hi):
            here = slice((at + j - lo) * capacity, (at + j - lo + 1) * capacity)
            prod = res_acc[here, :] * raw_ref[j].astype(F32)
            narrow = functools.reduce(jnp.add, [prod[:, i : i + 128] for i in range(0, width, 128)])
            inner = jnp.broadcast_to(jnp.sum(narrow.T, axis=0, keepdims=True), (8, capacity))
            if j != OWN:
                out_gin[j] = gin_acc[here, :].astype(BF)
                out_dot[j] = inner
                go_gin(j).start()
                go_dot(j).start()
            else:
                back_gin[j] = gin_acc[here, :].astype(BF)
                back_dot[j] = inner
        for j in range(lo, hi):
            here = slice((at + j - lo) * capacity, (at + j - lo + 1) * capacity)
            out_res[j] = res_acc[here, :].astype(BF)

    both = ((theirs, dw_away), (own_w, dw_ref))
    res_acc[...] = jnp.zeros(res_acc.shape, F32)
    gin_acc[...] = jnp.zeros(gin_acc.shape, F32)
    arrive(OWN, OWN + 1)
    for w_ref, dw in both:

        @pl.loop(0, nz - 1)
        def _(i):
            chunk(OWN, OWN + 1, w_ref, dw, i + shift, True, OWN)

    arrive(0, OWN)
    go_raw(3).start()
    go_in(3).start()
    for w_ref, dw in both:

        @pl.loop(0, nz - 1)
        def _(i):
            chunk(0, OWN, w_ref, dw, i + shift, False, 0)

    @pl.when(jnp.logical_not(at_end))
    def _():
        far_lift.wait()

    line.wait_recv(nz - 1)
    weights(nz - 1).start()
    chunk(0, OWN + 1, own_w, dw_ref, far_zone, True, 0)
    weights(nz - 1).wait_recv()
    chunk(0, OWN + 1, theirs, dw_away, far_zone, True, 0)
    send_back(0, OWN + 1, 0)
    arrive(3, 4)
    res_acc[0:capacity, :] = jnp.zeros((capacity, width), F32)
    gin_acc[0:capacity, :] = jnp.zeros((capacity, width), F32)

    @pl.loop(0, nz)
    def _(d):
        chunk(3, 4, theirs, dw_away, d, False, 0)
        go_dw(d).start()

    @pl.loop(0, nz)
    def _(d):
        chunk(3, 4, own_w, dw_ref, d, False, 0)

    send_back(3, 4, 0)
    for n in range(nz):
        go_dw(n).wait_recv()
        dw_ref[n] = (dw_ref[n].astype(F32) + dw_got[n].astype(F32)).astype(BF)
    for j in AWAY:
        go_gin(j).wait_recv()
        go_dot(j).wait_recv()
    line.wait_send(nz - 1)
    for n in range(nz):
        weights(n).wait_send()
        go_dw(n).wait_send()
    for j in AWAY:
        for c in (go_raw(j), go_in(j), go_gate(j), go_gin(j), go_dot(j)):
            c.wait_send()


def experts(x, attended, whole, places_row, places_col, raw, near, capacity, nz, cid):
    rows, width = x.shape
    part = near.shape[1]
    slots = sds((4, capacity, width), BF)
    small = sds((4, 8, capacity), F32)
    dma = pltpu.SemaphoreType.DMA
    two = lambda *shape: [dma(shape), dma(shape)]
    vm = pltpu.VMEM
    return pl.pallas_call(
        functools.partial(experts_kernel, capacity, nz),
        out_shape=(
            sds((rows, width), F32),
            sds((rows, 128), F32),
            slots,
            slots,
            small,
            sds((nz, part, 2 * width), BF),
        ),
        in_specs=[VM, VM, ANY, VM, VM, ANY, ANY],
        out_specs=(VM,) * 6,
        scratch_shapes=[
            vm((rows, width + 128), BF),
            vm((4, capacity, width), BF),
            vm((4, capacity, width), BF),
            vm((4, 8, capacity), F32),
            vm((4, 8, capacity), F32),
            vm((nz, part, 2 * width), BF),
            vm((nz, part, 2 * width), BF),
            vm((4, capacity, width), BF),
            vm((3 * capacity, width), F32),
            vm((3 * capacity, width), F32),
            vm((4, capacity, width), BF),
            vm((4, 8, capacity), F32),
            vm((nz, part, 2 * width), BF),
            vm((nz, part, 2 * width), BF),
            vm((4, capacity, width), BF),
            dma((2 + nz,)),
        ]
        + two(4) + two(nz) + two(4) + two(4) + two(4) + two(4) + two(nz) + two(nz - 1) + two(nz - 1),
        compiler_params=params(cid),
        name="experts",
    )(x, attended, whole, places_row, places_col, raw, near)


def after_kernel(
    capacity, nz, gin_ref, res_ref, dot_ref, hidden_ref, probs_ref, places_col, cot_ref, w_hbm, att_ref, part_ref,
    out_ref, gh_ref, gatt_ref, dw_ref, dr_ref, dg_ref, got_ref,
    wp, got_res, local, send, recv, send_z, recv_z,
):
    dp, sq, z, x, core = place()
    rows, width = hidden_ref.shape
    corner = [flip_chip(x, sq, *f) for f in SOURCES]
    plane = [(px * 2 + core, py, z) for px, py in corner]
    experts_of = [px * 2 + py for px, py in corner]
    others = [(dp, sq, lax.rem(z + d, nz)) for d in range(1, nz)]
    greet([plane[j] for j in AWAY] + others)
    first = pl.ds(0, got_ref.shape[1])
    zones = [
        remote(part_ref.at[lax.rem(z + d, nz), first], got_ref.at[d - 1], send_z.at[d - 1], recv_z.at[d - 1], others[d - 1])
        for d in range(1, nz)
    ]
    for c in zones:
        c.start()
    copies = {j: remote(res_ref.at[j], got_res.at[j], send.at[j], recv.at[j], plane[j]) for j in AWAY}
    for c in copies.values():
        c.start()
    load = pltpu.make_async_copy(w_hbm.at[:, 3 * width // 2 :], wp, local)
    load.start()
    load.wait()
    hidden = hidden_ref[...]
    probs = probs_ref[...]
    small = wp[:, :128]
    gain = small.astype(F32).T[EXPERTS + 1 : EXPERTS + 2, :]
    lane = iota(probs.shape, 1)
    back = None
    grad_probs = jnp.zeros_like(probs)
    for j in range(4):
        pick = hot_cols(pick_col(places_col[...], experts_of[j]), capacity)
        part = nn(pick, gin_ref[j])
        back = part if back is None else back + part
        inner = jnp.sum(pick.astype(F32) * dot_ref[j][0:1, :], axis=1, keepdims=True)
        grad_probs = jnp.where(lane == experts_of[j], inner, grad_probs)
    mixed = jnp.sum(probs * grad_probs, axis=1, keepdims=True)
    low = (probs * (grad_probs - mixed)).astype(BF)
    r_two = lax.rsqrt(jnp.mean(hidden * hidden, axis=1, keepdims=True) + EPSILON)
    h_norm = hidden * r_two
    routed = (h_norm * gain).astype(BF)
    grad_routed = back + nt(low, small)
    dg_ref[...] = jnp.sum(grad_routed * h_norm, axis=0, keepdims=True)
    u = grad_routed * gain
    grad_hidden = cot_ref[...].astype(F32) + r_two * (
        u - h_norm * jnp.mean(u * h_norm, axis=1, keepdims=True)
    )
    gh_ref[...] = grad_hidden
    hid_low = grad_hidden.astype(BF)
    gatt_ref[...] = nt(hid_low, wp[:, 128:]).astype(BF)
    dr_ref[...] = tn(routed, low)
    dw_ref[...] = tn(att_ref[...], hid_low).astype(BF)
    total = hidden
    for j in (OWN,) + AWAY:
        if j != OWN:
            copies[j].wait_recv()
        value = res_ref[j] if j == OWN else got_res[j]
        pick = hot_cols(pick_col(places_col[...], experts_of[j]), capacity)
        total = total + pick_col(probs, experts_of[j]) * nn(pick, value)
    out_ref[...] = total.astype(BF)
    for c in copies.values():
        c.wait_send()
    for c in zones:
        c.wait()


def after(gin, res, inner, hidden, probs, places_col, cot, whole, attended, dw_half, capacity, cid):
    nz, part, deep = dw_half.shape
    rows, width = hidden.shape
    dma = pltpu.SemaphoreType.DMA
    return pl.pallas_call(
        functools.partial(after_kernel, capacity, nz),
        out_shape=(
            sds((rows, width), BF),
            sds((rows, width), F32),
            sds((rows, width), BF),
            sds((width, width), BF),
            sds((width, 128), F32),
            sds((1, width), F32),
            sds((nz - 1, part // PARTS, deep), BF),
        ),
        in_specs=[VM] * 7 + [ANY, VM, ANY],
        out_specs=(VM,) * 6 + (ANY,),
        scratch_shapes=[
            pltpu.VMEM((rows, width + 128), BF),
            pltpu.VMEM((4, capacity, width), BF),
            dma(()),
            dma((4,)),
            dma((4,)),
            dma((nz - 1,)),
            dma((nz - 1,)),
        ],
        compiler_params=params(cid),
        name="after",
    )(gin, res, inner, hidden, probs, places_col, cot, whole, attended, dw_half)


PARTS = 4


def finish_kernel(
    prompt, nz, xs_ref, gatt_ref, qkv_ref, mixed_ref, lse_ref, w_ref, gh_ref, dout_ref, droute_ref, dgain_ref,
    seg_ref, part_ref, got_first,
    dx_ref, din_out, dout_out, droute_out, dgains_out, got_rest, dw_all,
    grad, qm, dom, kt, dqt, dcat, norm_t, sums, got_c, got_x, got_z, mine, fin, got_f, total, send_dx, got_dx, own_gn,
    stage, dw_sum,
    local, send_g, recv_g, send_c, recv_c, send_x, recv_x, send_z, recv_z, send_d, recv_d, send_f, recv_f,
    send_a, recv_a, send_b, recv_b, send_s, recv_s, send_v, recv_v, send_h, recv_h, send_k, recv_k,
):
    dp, sq, z, x, core = place()
    rows, width = gatt_ref.shape
    half = width // 2
    pairs = half // 128
    shard = width // nz
    part = shard // 4
    own_cols = 3 * half
    lead = own_cols + 128
    chip = x * 2 + sq
    chip_x, chip_y, chip_d = (1 - x) * 2 + sq, x * 2 + 1 - sq, (1 - x) * 2 + 1 - sq
    sibling = (x * 2 + 1 - core, sq, z)
    partner = (dp, 1 - sq, z)
    across = ((1 - x) * 2 + core, sq, z)
    others = [(dp, sq, lax.rem(z + d, nz)) for d in range(1, nz)]
    base = pl.multiple_of(sq * rows, rows)
    there = pl.multiple_of((1 - sq) * rows, rows)
    greet([sibling, partner, across] + others)

    quarter = got_first.shape[1]

    def zone_part(k, d):
        return remote(
            part_ref.at[lax.rem(z + d, nz), pl.ds(k * quarter, quarter)],
            got_rest.at[k - 1, d - 1],
            send_s.at[k - 1, d - 1],
            recv_s.at[k - 1, d - 1],
            others[d - 1],
        )

    def share(k, ch, send, recv, peer, own=False):
        at = dw_all.at[core, ch, pl.ds(k * quarter, quarter)]
        return remote(dw_sum.at[k] if own else at, at, send, recv, peer)

    def keep(k):
        return pltpu.make_async_copy(
            dw_sum.at[k], dw_all.at[core, chip, pl.ds(k * quarter, quarter)], local.at[nz + k]
        )

    def start_part(k):
        for d in range(1, nz):
            zone_part(k, d).start()

    def sum_part(k):
        loads = []
        for d in range(nz - 1):
            if k > 0:
                zone_part(k, d + 1).wait_recv()
            src = got_first.at[d] if k == 0 else got_rest.at[k - 1, d]
            loads.append(pltpu.make_async_copy(src, stage.at[d], local.at[d]))
        loads.append(
            pltpu.make_async_copy(part_ref.at[z, pl.ds(k * quarter, quarter)], stage.at[nz - 1], local.at[nz - 1])
        )
        for c in loads:
            c.start()
        for c in loads:
            c.wait()
        acc = stage[0].astype(F32)
        for d in range(1, nz):
            acc = acc + stage[d].astype(F32)
        dw_sum[k] = acc.astype(BF)
        share(k, chip, send_v.at[k], recv_v.at[k], partner, True).start()
        share(k, chip, send_h.at[k, 0], recv_h.at[k, 0], across, True).start()
        share(k, chip, send_k.at[k, 0], recv_k.at[k, 0], sibling, True).start()
        keep(k).start()

    def pass_part(k):
        share(k, chip_y, send_v.at[k], recv_v.at[k], partner).wait_recv()
        share(k, chip_y, send_h.at[k, 1], recv_h.at[k, 1], across).start()
        share(k, chip_y, send_k.at[k, 1], recv_k.at[k, 1], sibling).start()

    def last_part(k):
        share(k, chip_x, send_h.at[k, 0], recv_h.at[k, 0], across).wait_recv()
        share(k, chip_x, send_k.at[k, 2], recv_k.at[k, 2], sibling).start()
        share(k, chip_d, send_h.at[k, 1], recv_h.at[k, 1], across).wait_recv()
        share(k, chip_d, send_k.at[k, 3], recv_k.at[k, 3], sibling).start()

    def end_part(k):
        other = [chip, chip_y, chip_x, chip_d]
        for i in range(4):
            at = dw_all.at[1 - core, other[i], pl.ds(k * quarter, quarter)]
            remote(at, at, send_k.at[k, i], recv_k.at[k, i], sibling).wait_recv()
            share(k, other[i], send_k.at[k, i], recv_k.at[k, i], sibling, i == 0).wait_send()
        share(k, chip, send_v.at[k], recv_v.at[k], partner, True).wait_send()
        share(k, chip, send_h.at[k, 0], recv_h.at[k, 0], across, True).wait_send()
        share(k, chip_y, send_h.at[k, 1], recv_h.at[k, 1], across).wait_send()
        keep(k).wait()
        if k > 0:
            for d in range(1, nz):
                zone_part(k, d).wait_send()

    groups = (pl.ds(0, lead), pl.ds(lead, width))
    order = [lax.rem(z + d, nz) for d in range(1, nz + 1)]

    def piece(zz, px, co):
        return pl.ds(pl.multiple_of(zz * shard + (px * 2 + co) * part, part), part)

    def to_core(g, n, i):
        src = sums.at[piece(order[n], (1 - x, x)[i], 1 - core), groups[g]]
        return remote(src, got_c.at[n, i, :, groups[g]], send_c.at[g, n, i], recv_c.at[g, n, i], sibling)

    def to_x(g, n):
        src = sums.at[piece(order[n], 1 - x, core), groups[g]]
        return remote(src, got_x.at[n, :, groups[g]], send_x.at[g, n], recv_x.at[g, n], across)

    def to_z(g, n):
        return remote(
            mine.at[n, :, groups[g]], got_z.at[n, :, groups[g]], send_z.at[g, n], recv_z.at[g, n], others[n]
        )

    def cols_of(g):
        return slice(0, lead) if g == 0 else slice(lead, lead + width)

    def reduce_core(g, n):
        cols = cols_of(g)
        for i in range(2):
            to_core(g, n, i).wait_recv()
            at = piece(order[n], (1 - x, x)[i], core)
            sums[at, cols] = (sums[at, cols].astype(F32) + got_c[n, i, :, cols].astype(F32)).astype(BF)
            if i == 0:
                to_x(g, n).start()

    def reduce_x(g, n):
        cols = cols_of(g)
        to_x(g, n).wait_recv()
        acc = sums[piece(order[n], x, core), cols].astype(F32) + got_x[n, :, cols].astype(F32)
        if n < nz - 1:
            mine[n, :, cols] = acc.astype(BF)
            to_z(g, n).start()
        return acc

    def reduce_z(g, acc):
        cols = cols_of(g)
        for n in range(nz - 1):
            to_z(g, n).wait_recv()
            acc = acc + got_z[n, :, cols].astype(F32)
        fin[:, cols] = acc.astype(BF)

    def give(p, to):
        return remote(
            gatt_ref.at[:, pl.ds(al((1 - sq) * half + p * 128), 128)],
            grad.at[p, pl.ds(to, rows)],
            send_g.at[p],
            recv_g.at[p],
            partner,
        )

    for p in range(pairs):
        give(p, base).start()
    start_part(1)
    for p in range(pairs):
        grad[p, pl.ds(base, rows), :] = gatt_ref[:, pl.ds(al(sq * half + p * 128), 128)]
    sums[:, cols_of(1)] = dout_ref[...]
    for n in range(nz):
        for i in range(2):
            to_core(1, n, i).start()
    seg_row, seg_col = eighth(seg_ref[...], prompt)
    gain = w_ref[:, own_cols:lead].astype(F32).T[EXPERTS : EXPERTS + 1, :]

    def norm_of(at):
        xf = xs_ref[at, :].astype(F32)
        r_one = lax.rsqrt(jnp.mean(xf * xf, axis=1, keepdims=True) + EPSILON)
        return xf * r_one, r_one

    for i in range(2):
        at = slice(i * rows, (i + 1) * rows)
        norm_t[:, at] = (norm_of(at)[0] * gain).astype(BF).T

    blocks = 2 * rows // QB
    scale = HEAD_DIM ** (-0.5)
    zero = jnp.zeros((), BF)

    @pl.loop(0, pairs)
    def _(p):
        give(p, there).wait_recv()
        kt[...] = qkv_ref[p, 1].T
        prod = (grad[p].astype(F32) * mixed_ref[p].astype(F32)).T
        delta = []
        for h in range(2):
            lanes = iota((1, 128), 1) // HEAD_DIM == h
            qm[h] = jnp.where(lanes, qkv_ref[p, 0], zero) * jnp.asarray(scale, BF)
            dom[h] = jnp.where(lanes, grad[p], zero)
            low = h * HEAD_DIM
            delta.append(jnp.sum(prod[low : low + HEAD_DIM, :], axis=0, keepdims=True))
        for j in range(blocks):
            keys = slice(j * QB, (j + 1) * QB)
            k, v = qkv_ref[p, 1, keys, :], qkv_ref[p, 2, keys, :]
            dk = dv = None
            for i in range(j, blocks):
                at = slice(i * QB, (i + 1) * QB)
                mask = allowed_tile(j, i, prompt, seg_col, seg_row)
                for h in range(2):
                    s = nt(k, qm[h, at, :])
                    dpr = nt(v, dom[h, at, :])
                    pr = jnp.exp2(s * LOG2E - lse_ref[p, h : h + 1, at])
                    if mask is not None:
                        pr = jnp.where(mask, pr, 0.0)
                    ds = (pr * (dpr - delta[h][:, at])).astype(BF)
                    a = nn(pr.astype(BF), dom[h, at, :])
                    b = nn(ds, qm[h, at, :])
                    c = nn(kt[h * HEAD_DIM : (h + 1) * HEAD_DIM, keys], ds)
                    dv = a if dv is None else dv + a
                    dk = b if dk is None else dk + b
                    to = slice(h * HEAD_DIM, (h + 1) * HEAD_DIM)
                    dqt[to, at] = c if j == 0 else dqt[to, at] + c
            dcat[keys, pl.ds(al(half + p * 128), 128)] = dk.astype(BF)
            dcat[keys, pl.ds(al(2 * half + p * 128), 128)] = dv.astype(BF)
        dcat[:, pl.ds(al(p * 128), 128)] = (dqt[...] * scale).T.astype(BF)

        @pl.when(p == 0)
        def _():
            sum_part(0)
            start_part(2)
            for n in range(nz):
                reduce_core(1, n)

        @pl.when(p == 1)
        def _():
            pass_part(0)
            sum_part(1)
            start_part(3)
            for n in range(nz - 1):
                reduce_x(1, n)

    partial = nt(dcat[pl.ds(there, rows), :], w_ref[:, 0:own_cols])
    send_dx[...] = partial.astype(BF)
    to_dx = remote(send_dx, got_dx, send_d, recv_d, partner)
    to_dx.start()
    dg_one = jnp.sum(partial * norm_of(pl.ds(there, rows))[0], axis=0, keepdims=True)
    partial = nt(dcat[pl.ds(base, rows), :], w_ref[:, 0:own_cols])
    own_gn[...] = partial
    dg_one = dg_one + jnp.sum(partial * norm_of(pl.ds(base, rows))[0], axis=0, keepdims=True)
    stacked = jnp.concatenate([dg_one, dgain_ref[...], jnp.zeros((126, width), F32)], axis=0).T
    lane = iota((1, 128), 1)
    small = jnp.where(lane < EXPERTS, droute_ref[...], 0.0)
    for i in range(2):
        small = jnp.where(lane == EXPERTS + i, stacked[:, i : i + 1], small)
    sums[:, own_cols:lead] = small.astype(BF)
    for n in range(nz):
        zone = pl.ds(pl.multiple_of(order[n] * shard, shard), shard)
        sums[zone, 0:own_cols] = nn(norm_t[zone, :], dcat[...]).astype(BF)
        for i in range(2):
            to_core(0, n, i).start()
    pass_part(1)
    sum_part(2)
    last_part(0)
    reduce_core(0, 0)
    for n in range(1, nz):
        reduce_core(0, n)
        reduce_x(0, n - 1)
    reduce_z(1, reduce_x(1, nz - 1))
    last_part(1)
    pass_part(2)
    sum_part(3)
    reduce_z(0, reduce_x(0, nz - 1))
    to_f = remote(fin, got_f, send_f, recv_f, partner)
    to_f.start()
    to_dx.wait_recv()
    grad_n = own_gn[...] + got_dx[...].astype(F32)
    x_norm, r_one = norm_of(pl.ds(base, rows))
    u = grad_n * gain
    dx = gh_ref[...] + r_one * (u - x_norm * jnp.mean(u * x_norm, axis=1, keepdims=True))
    dx_ref[...] = dx.astype(BF)
    pass_part(3)
    last_part(2)
    to_f.wait_recv()

    def spot(px, co):
        return pl.ds(pl.multiple_of((px * 2 + co) * part, part), part)

    here = spot(x, core)
    for i in range(3):
        cols = slice(i * half, (i + 1) * half)
        total[here, pl.ds(al(i * width + sq * half), half)] = fin[:, cols]
        total[here, pl.ds(al(i * width + (1 - sq) * half), half)] = got_f[:, cols]
    total[here, 3 * width :] = (fin[:, own_cols:].astype(F32) + got_f[:, own_cols:].astype(F32)).astype(BF)

    def pass_on(px, co, send, recv, peer):
        return remote(total.at[spot(px, co)], total.at[spot(px, co)], send, recv, peer)

    pass_on(x, core, send_a, recv_a, across).start()
    pass_on(x, core, send_b.at[0], recv_b.at[0], sibling).start()
    pass_on(1 - x, core, send_a, recv_a, across).wait_recv()
    pass_on(1 - x, core, send_b.at[1], recv_b.at[1], sibling).start()
    pass_on(x, 1 - core, send_b.at[0], recv_b.at[0], sibling).wait_recv()
    pass_on(1 - x, 1 - core, send_b.at[1], recv_b.at[1], sibling).wait_recv()
    din_out[...] = total[:, 0 : 3 * width].astype(F32)
    small = total[:, 3 * width : 3 * width + 128].astype(F32)
    droute_out[...] = small[:, 0:EXPERTS]
    dgains_out[...] = small[:, EXPERTS : EXPERTS + 2]
    dout_out[...] = total[:, 3 * width + 128 :].astype(F32)
    last_part(3)
    for k in range(PARTS):
        end_part(k)
    pass_on(x, core, send_a, recv_a, across).wait_send()
    pass_on(x, core, send_b.at[0], recv_b.at[0], sibling).wait_send()
    pass_on(1 - x, core, send_b.at[1], recv_b.at[1], sibling).wait_send()
    to_f.wait_send()
    to_dx.wait_send()
    for g in range(2):
        for n in range(nz):
            for i in range(2):
                to_core(g, n, i).wait_send()
            to_x(g, n).wait_send()
            if n < nz - 1:
                to_z(g, n).wait_send()
    for p in range(pairs):
        give(p, base).wait_send()


def finish(xs, grad_att, qkv, mixed, lse, whole, grad_hidden, d_out, d_route, d_gain, segments, dw_half, dw_first, prompt, nz, cid):
    rows, width = grad_att.shape
    pairs = width // 256
    cols = whole.shape[1]
    shard = width // nz
    part = shard // 4
    group = 2 * rows
    dma = pltpu.SemaphoreType.DMA
    two = lambda *shape: [dma(shape), dma(shape)]
    vm = pltpu.VMEM
    return pl.pallas_call(
        functools.partial(finish_kernel, prompt, nz),
        out_shape=(
            sds((rows, width), BF),
            sds((shard, 3 * width), F32),
            sds((shard, width), F32),
            sds((shard, EXPERTS), F32),
            sds((shard, 2), F32),
            sds((PARTS - 1,) + dw_first.shape, BF),
            sds((2, 4) + dw_half.shape[1:], BF),
        ),
        in_specs=[VM] * 11 + [ANY, ANY],
        out_specs=(VM,) * 5 + (ANY, ANY),
        scratch_shapes=[
            vm((pairs, group, 128), BF),
            vm((2, group, 128), BF),
            vm((2, group, 128), BF),
            vm((128, group), BF),
            vm((128, group), F32),
            vm((group, 3 * width // 2), BF),
            vm((width, group), BF),
            vm((width, cols), BF),
            vm((nz, 2, part, cols), BF),
            vm((nz, part, cols), BF),
            vm((nz - 1, part, cols), BF),
            vm((nz - 1, part, cols), BF),
            vm((part, cols), BF),
            vm((part, cols), BF),
            vm((shard, 4 * width + 128), BF),
            vm((rows, width), BF),
            vm((rows, width), BF),
            vm((rows, width), F32),
            vm((nz,) + dw_first.shape[1:], BF),
            vm((PARTS,) + dw_first.shape[1:], BF),
            dma((nz + PARTS,)),
        ]
        + two(pairs) + two(2, nz, 2) + two(2, nz) + two(2, nz - 1) + two() + two() + two() + two(2)
        + two(PARTS - 1, nz - 1) + two(PARTS) + two(PARTS, 2) + two(PARTS, 4),
        compiler_params=params(cid),
        name="finish",
    )(xs, grad_att, qkv, mixed, lse, whole, grad_hidden, d_out, d_route, d_gain, segments, dw_half, dw_first)


def spread_kernel(in_ref, out_ref):
    for e in range(EXPERTS):
        out_ref[:, e, :] = in_ref[e].astype(F32)


def spread_experts(parts):
    cores, experts_, r, k = parts.shape
    block = r // 8
    return pl.pallas_call(
        spread_kernel,
        grid=(cores, 8),
        out_shape=sds((cores * r, experts_, k), F32),
        in_specs=[pl.BlockSpec((None, experts_, block, k), lambda c, i: (c, 0, i, 0))],
        out_specs=pl.BlockSpec((block, experts_, k), lambda c, i: (c * 8 + i, 0, 0)),
        compiler_params=params(),
        name="spread",
    )(parts)


def shards(tokens, attn_in, attn_out, router, gains, expert_w, expert_ids, segments, cotangent):
    x = tokens[0]
    cot = cotangent[0]
    rows, width = x.shape
    nz = lax.axis_size("fsdp")
    group = 2 * rows
    prompt = group - segments.shape[1]
    capacity = 2 * rows // EXPERTS
    dp, sq = lax.axis_index("dp"), lax.axis_index("seq")
    core = lax.rem(dp, 2)
    mine = (dp // 2) * 2 + sq

    part = expert_w.shape[0] // 2
    piece = lax.dynamic_slice(expert_w, (core * part, mine, 0), (part, 1, 2 * width))[:, 0]
    xs, whole, qkv, mixed, lse, attended, raw, places_row, places_col, near = begin(
        x, attn_in, attn_out, router, gains, segments, expert_ids[0], cot, piece, prompt, nz, capacity, 0
    )
    hidden, probs, gin, res, inner, dw_half = experts(
        x, attended, whole, places_row, places_col, raw, near, capacity, nz, 1
    )
    block_out, grad_hidden, grad_att, d_out, d_route, d_gain_two, dw_first = after(
        gin, res, inner, hidden, probs, places_col, cot, whole, attended, dw_half, capacity, 2
    )
    d_tokens, d_in, d_out, d_route, d_gains, _, dw_all = finish(
        xs, grad_att, qkv, mixed, lse, whole, grad_hidden, d_out, d_route, d_gain_two, segments, dw_half, dw_first,
        prompt, nz, 3,
    )
    d_expert = spread_experts(dw_all)
    return (
        block_out[None],
        d_tokens[None],
        d_in,
        d_out,
        d_route,
        d_gains,
        d_expert,
    )


def route(choose, capacity, experts_count):
    pair_expert = choose.reshape(-1)
    one_hot = (pair_expert[:, None] == jnp.arange(experts_count, dtype=jnp.int32)[None, :]).astype(
        jnp.int32
    )
    before = jnp.cumsum(one_hot, axis=0) - one_hot
    place = jnp.sum(before * one_hot, axis=1)
    kept = place < capacity
    slots = jnp.where(kept, pair_expert * capacity + place, experts_count * capacity)
    pair_count = pair_expert.shape[0]
    pair_of = (
        jnp.zeros((experts_count * capacity + 1,), jnp.int32)
        .at[slots]
        .set(jnp.arange(pair_count, dtype=jnp.int32))
    )
    filled = (
        jnp.zeros((experts_count * capacity + 1,), jnp.int32)
        .at[slots]
        .set(jnp.ones((pair_count,), jnp.int32))
    )
    return (slots, kept, pair_of[:-1], filled[:-1] > 0)


def expert_pre(expert_in, piece):
    width = piece.shape[2] // 2
    return jnp.einsum(
        "ecd,fed->ecf", expert_in, piece[:, :, :width], preferred_element_type=jnp.float32
    )


def expert_out(activity, piece):
    width = piece.shape[2] // 2
    return jnp.einsum(
        "ecf,fed->ecd", activity, piece[:, :, width:], preferred_element_type=jnp.float32
    )


def expert_back(grad_result, pre_rows, piece):
    width = piece.shape[2] // 2
    grad_act = jnp.einsum(
        "ecd,fed->ecf", grad_result, piece[:, :, width:], preferred_element_type=jnp.float32
    )
    grad_pre = jax.vjp(jax.nn.gelu, pre_rows)[1](grad_act)[0].astype(jnp.bfloat16)
    grad_in = jnp.einsum(
        "ecf,fed->ecd", grad_pre, piece[:, :, :width], preferred_element_type=jnp.float32
    )
    return (grad_pre, grad_in)


def general_shards(tokens, attn_in, attn_out, router, gains, expert_w, expert_ids, segments, cotangent):
    x_rows = tokens[0].astype(jnp.float32)
    tok_rows = x_rows.shape[0]
    width = x_rows.shape[1]
    seq_count = lax.axis_size("seq")
    scale = HEAD_DIM ** (-0.5)
    w_qkv, w_proj, w_route, gain_pair = (
        lax.all_gather(attn_in, "fsdp", axis=0, tiled=True),
        lax.all_gather(attn_out, "fsdp", axis=0, tiled=True),
        lax.all_gather(router, "fsdp", axis=0, tiled=True),
        lax.all_gather(gains, "fsdp", axis=0, tiled=True),
    )
    gain_f = gain_pair.astype(jnp.float32)
    r_one = lax.rsqrt(jnp.mean(x_rows * x_rows, axis=-1, keepdims=True) + EPSILON)
    normed_one = x_rows * r_one
    normed_low = (normed_one * gain_f[:, 0]).astype(jnp.bfloat16)
    projected = jnp.dot(normed_low, w_qkv, preferred_element_type=jnp.float32).astype(jnp.bfloat16)
    local_heads = HEADS // seq_count
    head_cols = local_heads * HEAD_DIM
    arrived = lax.all_to_all(
        projected.reshape(tok_rows, 3, seq_count, head_cols),
        "seq",
        split_axis=2,
        concat_axis=0,
        tiled=True,
    )
    group_len = arrived.shape[0]
    queries = arrived[:, 0, 0].reshape(group_len, local_heads, HEAD_DIM)
    keys = arrived[:, 1, 0].reshape(group_len, local_heads, HEAD_DIM)
    values = arrived[:, 2, 0].reshape(group_len, local_heads, HEAD_DIM)
    seg_full = jnp.concatenate([jnp.full((PROMPT,), -1, jnp.int32), segments[0]])
    block = min(512, group_len)
    key_place = jnp.arange(group_len, dtype=jnp.int32)
    begins = jnp.arange(group_len // block, dtype=jnp.int32) * block

    def block_scores(begin):
        query_block = lax.dynamic_slice_in_dim(queries, begin, block, 0)
        query_place = begin + jnp.arange(block, dtype=jnp.int32)
        query_seg = lax.dynamic_slice_in_dim(seg_full, begin, block, 0)
        raw = (
            jnp.einsum("qhd,khd->hqk", query_block, keys, preferred_element_type=jnp.float32)
            * scale
        )
        allowed = (key_place[None, :] <= query_place[:, None]) & (
            (seg_full[None, :] < 0) | (seg_full[None, :] == query_seg[:, None])
        )
        return (jnp.where(allowed[None], raw, NEGATIVE), query_block)

    def forward_block(begin):
        masked, query_block = block_scores(begin)
        row_max = jnp.max(masked, axis=-1, keepdims=True)
        expo = jnp.exp(masked - row_max)
        row_total = jnp.sum(expo, axis=-1, keepdims=True)
        probs = expo / row_total
        mixed_block = jnp.einsum(
            "hqk,khd->qhd", probs.astype(jnp.bfloat16), values, preferred_element_type=jnp.float32
        )
        return (mixed_block.astype(jnp.bfloat16), (row_max + jnp.log(row_total))[:, :, 0])

    mixed_blocks, log_totals = lax.map(forward_block, begins)
    mixed_heads = mixed_blocks.reshape(group_len, 1, head_cols)
    returned = lax.all_to_all(mixed_heads, "seq", split_axis=0, concat_axis=1, tiled=True)
    attended = returned.reshape(tok_rows, width)
    hidden = x_rows + jnp.dot(attended, w_proj, preferred_element_type=jnp.float32)
    r_two = lax.rsqrt(jnp.mean(hidden * hidden, axis=-1, keepdims=True) + EPSILON)
    normed_two = hidden * r_two
    routed_low = (normed_two * gain_f[:, 1]).astype(jnp.bfloat16)
    logits = jnp.dot(routed_low, w_route, preferred_element_type=jnp.float32)
    probs_r = jax.nn.softmax(logits, axis=-1)
    choose = expert_ids[0]
    choose_map = (choose[:, :, None] == jnp.arange(EXPERTS, dtype=jnp.int32)[None, None, :]).astype(
        jnp.float32
    )
    gates = jnp.sum(probs_r[:, None, :] * choose_map, axis=-1)
    capacity = 2 * tok_rows // EXPERTS
    slots, kept, pair_of, filled = route(choose, capacity, EXPERTS)
    token_of = pair_of // 2
    expert_in = jnp.where(
        filled[:, None], routed_low[token_of], jnp.zeros((), jnp.bfloat16)
    ).reshape(EXPERTS, capacity, width)
    piece = lax.all_gather(expert_w, "fsdp", axis=0, tiled=True)
    pre_rows = expert_pre(expert_in, piece)
    result = expert_out(jax.nn.gelu(pre_rows).astype(jnp.bfloat16), piece)
    padded = jnp.concatenate(
        [result.reshape(EXPERTS * capacity, width), jnp.zeros((1, width), jnp.float32)], axis=0
    )
    picked = padded[slots].reshape(tok_rows, 2, width)
    kept_f = kept.astype(jnp.float32).reshape(tok_rows, 2)
    weight_pair = gates * kept_f
    block_out = hidden + jnp.sum(weight_pair[..., None] * picked, axis=1)
    grad_out_rows = cotangent[0].astype(jnp.float32)
    grad_gates = kept_f * jnp.sum(grad_out_rows[:, None, :] * picked, axis=-1)
    grad_probs = jnp.sum(grad_gates[:, :, None] * choose_map, axis=1)
    grad_logits = probs_r * (grad_probs - jnp.sum(probs_r * grad_probs, axis=-1, keepdims=True))
    grad_route_w = jnp.dot(routed_low.astype(jnp.float32).T, grad_logits, precision=HIGH)
    grad_routed = jnp.dot(grad_logits, w_route.astype(jnp.float32).T, precision=HIGH)
    scaled = (weight_pair[:, :, None] * grad_out_rows[:, None, :]).reshape(2 * tok_rows, width)
    grad_result = (
        jnp.where(filled[:, None], scaled[pair_of], 0.0)
        .astype(jnp.bfloat16)
        .reshape(EXPERTS, capacity, width)
    )
    piece = lax.all_gather(expert_w, "fsdp", axis=0, tiled=True)
    pre_rows = expert_pre(expert_in, piece)
    act_rows = jax.nn.gelu(pre_rows).astype(jnp.bfloat16)
    grad_pre_rows, grad_in_rows = expert_back(grad_result, pre_rows, piece)
    act_store = act_rows
    pre_rows = grad_pre_rows
    act_rows = act_store
    grad_first = jnp.einsum("ecd,ecf->fed", expert_in, pre_rows, preferred_element_type=jnp.float32)
    grad_second = jnp.einsum(
        "ecf,ecd->fed", act_rows, grad_result, preferred_element_type=jnp.float32
    )
    expert_shard = lax.psum_scatter(
        jnp.concatenate([grad_first, grad_second], axis=2).astype(jnp.bfloat16),
        "fsdp",
        scatter_dimension=0,
        tiled=True,
    )
    padded_in = jnp.concatenate(
        [grad_in_rows.reshape(EXPERTS * capacity, width), jnp.zeros((1, width), jnp.float32)],
        axis=0,
    )
    grad_routed = grad_routed + jnp.sum(padded_in[slots].reshape(tok_rows, 2, width), axis=1)
    grad_gain_two = jnp.sum(grad_routed * normed_two, axis=0)
    scaled_two = grad_routed * gain_f[:, 1]
    grad_hidden = grad_out_rows + r_two * (
        scaled_two - normed_two * jnp.mean(scaled_two * normed_two, axis=-1, keepdims=True)
    )
    hid_low = grad_hidden.astype(jnp.bfloat16)
    grad_proj_w = jnp.dot(attended.T, hid_low, preferred_element_type=jnp.float32)
    grad_attended = jnp.dot(hid_low, w_proj.T, preferred_element_type=jnp.float32).astype(
        jnp.bfloat16
    )
    grad_heads = lax.all_to_all(
        grad_attended.reshape(tok_rows, seq_count, head_cols),
        "seq",
        split_axis=1,
        concat_axis=0,
        tiled=True,
    )
    grad_mixed = grad_heads.reshape(group_len, local_heads, HEAD_DIM)

    def back_block(carry, inputs):
        begin, log_rows = inputs
        masked, query_block = block_scores(begin)
        probs = jnp.exp(masked - log_rows[:, :, None])
        grad_block = lax.dynamic_slice_in_dim(grad_mixed, begin, block, 0)
        grad_p = jnp.einsum("qhd,khd->hqk", grad_block, values, preferred_element_type=jnp.float32)
        inner = jnp.sum(probs * grad_p, axis=-1, keepdims=True)
        grad_scores = (probs * (grad_p - inner)).astype(jnp.bfloat16)
        grad_query = (
            jnp.einsum("hqk,khd->qhd", grad_scores, keys, preferred_element_type=jnp.float32)
            * scale
        )
        grad_key = (
            carry[0]
            + jnp.einsum(
                "hqk,qhd->khd", grad_scores, query_block, preferred_element_type=jnp.float32
            )
            * scale
        )
        grad_value = carry[1] + jnp.einsum(
            "hqk,qhd->khd",
            probs.astype(jnp.bfloat16),
            grad_block,
            preferred_element_type=jnp.float32,
        )
        return ((grad_key, grad_value), grad_query)

    zero_heads = jnp.zeros((group_len, local_heads, HEAD_DIM), jnp.float32)
    (grad_keys, grad_values), grad_queries = lax.scan(
        back_block, (zero_heads, zero_heads), (begins, log_totals)
    )
    stacked = jnp.stack(
        [
            grad_queries.reshape(group_len, head_cols),
            grad_keys.reshape(group_len, head_cols),
            grad_values.reshape(group_len, head_cols),
        ],
        axis=1,
    )
    stacked = stacked.astype(jnp.bfloat16).reshape(group_len, 3, 1, head_cols)
    grad_back = lax.all_to_all(stacked, "seq", split_axis=0, concat_axis=2, tiled=True)
    grad_proj_rows = grad_back.reshape(tok_rows, 3 * width)
    grad_qkv_w = jnp.dot(normed_low.T, grad_proj_rows, preferred_element_type=jnp.float32)
    grad_normed = jnp.dot(grad_proj_rows, w_qkv.T, preferred_element_type=jnp.float32)
    grad_gain_one = jnp.sum(grad_normed * normed_one, axis=0)
    scaled_one = grad_normed * gain_f[:, 0]
    grad_x = grad_hidden + r_one * (
        scaled_one - normed_one * jnp.mean(scaled_one * normed_one, axis=-1, keepdims=True)
    )
    grad_gains = jnp.stack([grad_gain_one, grad_gain_two], axis=1)
    shard_qkv, shard_proj, shard_route, shard_gains = (
        lax.psum_scatter(
            grad_qkv_w.astype(jnp.bfloat16), "fsdp", scatter_dimension=0, tiled=True
        ).astype(jnp.float32),
        lax.psum_scatter(
            grad_proj_w.astype(jnp.bfloat16), "fsdp", scatter_dimension=0, tiled=True
        ).astype(jnp.float32),
        lax.psum_scatter(
            grad_route_w.astype(jnp.bfloat16), "fsdp", scatter_dimension=0, tiled=True
        ).astype(jnp.float32),
        lax.psum_scatter(
            grad_gains.astype(jnp.bfloat16), "fsdp", scatter_dimension=0, tiled=True
        ).astype(jnp.float32),
    )
    part_qkv, part_proj, part_expert = (
        lax.psum_scatter(
            shard_qkv.astype(jnp.bfloat16), ("dp", "seq"), scatter_dimension=1, tiled=True
        ).astype(jnp.float32),
        lax.psum_scatter(
            shard_proj.astype(jnp.bfloat16), ("dp", "seq"), scatter_dimension=1, tiled=True
        ).astype(jnp.float32),
        lax.psum_scatter(expert_shard, ("dp", "seq"), scatter_dimension=2, tiled=True).astype(
            jnp.float32
        ),
    )
    summed_qkv, summed_proj, summed_expert = (
        lax.all_gather(part_qkv.astype(jnp.bfloat16), ("dp", "seq"), axis=1, tiled=True).astype(
            part_qkv.dtype
        ),
        lax.all_gather(part_proj.astype(jnp.bfloat16), ("dp", "seq"), axis=1, tiled=True).astype(
            part_proj.dtype
        ),
        lax.all_gather(part_expert.astype(jnp.bfloat16), ("dp", "seq"), axis=2, tiled=True).astype(
            part_expert.dtype
        ),
    )
    summed_route, summed_gains = lax.psum((shard_route, shard_gains), ("dp", "seq"))
    return (
        block_out.astype(jnp.bfloat16)[None],
        grad_x.astype(jnp.bfloat16)[None],
        summed_qkv,
        summed_proj,
        summed_route,
        summed_gains,
        summed_expert,
    )


def fits(mesh):
    return mesh.shape["fsdp"] == 4 and mesh.shape["dp"] == 4 and mesh.shape["seq"] == 2


def solution(mesh):
    body = shards if fits(mesh) else general_shards
    in_specs = (
        P(("dp", "fsdp"), "seq", None),
        P("fsdp", None),
        P("fsdp", None),
        P("fsdp", None),
        P("fsdp", None),
        P("fsdp", None, None),
        P(("dp", "fsdp"), "seq", None),
        P(("dp", "fsdp"), None),
        P(("dp", "fsdp"), "seq", None),
    )
    out_specs = (
        P(("dp", "fsdp"), "seq", None),
        P(("dp", "fsdp"), "seq", None),
        P("fsdp", None),
        P("fsdp", None),
        P("fsdp", None),
        P("fsdp", None),
        P("fsdp", None, None),
    )
    return jax.shard_map(body, mesh=mesh, in_specs=in_specs, out_specs=out_specs, check_vma=False)
```

```python
import functools

import jax
import jax.numpy as jnp
from jax import lax
from jax.experimental import pallas as pl
from jax.experimental.pallas import tpu as pltpu
from jax.sharding import PartitionSpec as P

HEADS = 12
HEAD_DIM = 64
EXPERTS = 4
PROMPT = 1024
EPSILON = 1e-06
NEGATIVE = -1e30
HIGH = lax.Precision.HIGHEST
LOG2E = 1.4426950408889634
BF = jnp.bfloat16
F32 = jnp.float32
MESH = pl.DeviceIdType.MESH
VMEM_LIMIT = 60 << 20
QB = 256
ANY = pl.BlockSpec(memory_space=pl.ANY)
VM = pl.BlockSpec(memory_space=pltpu.VMEM)


def nn(a, b):
    return lax.dot_general(a, b, (((1,), (0,)), ((), ())), preferred_element_type=F32)


def nt(a, b):
    return lax.dot_general(a, b, (((1,), (1,)), ((), ())), preferred_element_type=F32)


def tn(a, b):
    return lax.dot_general(a, b, (((0,), (0,)), ((), ())), preferred_element_type=F32)


def iota(shape, dim):
    return lax.broadcasted_iota(jnp.int32, shape, dim)


def params(cid=None):
    if cid is None:
        return pltpu.CompilerParams(vmem_limit_bytes=VMEM_LIMIT)
    return pltpu.CompilerParams(
        vmem_limit_bytes=VMEM_LIMIT, collective_id=cid, has_side_effects=True
    )


def sds(shape, dtype):
    return jax.ShapeDtypeStruct(shape, dtype)


def place():
    dp, sq, z = lax.axis_index("dp"), lax.axis_index("seq"), lax.axis_index("fsdp")
    return dp, sq, z, dp // 2, lax.rem(dp, 2)


def greet(peers):
    barrier = pltpu.get_barrier_semaphore()
    for peer in peers:
        pl.semaphore_signal(barrier, inc=1, device_id=peer, device_id_type=MESH)
    pl.semaphore_wait(barrier, len(peers))


def remote(src, dst, send, recv, peer):
    return pltpu.make_async_remote_copy(
        src_ref=src, dst_ref=dst, send_sem=send, recv_sem=recv, device_id=peer, device_id_type=MESH
    )


def al(x):
    return pl.multiple_of(x, 128)


def allowed_tile(j, i, prompt, seg_col, seg_row):
    mask = None
    if i == j:
        mask = iota((QB, QB), 0) <= iota((QB, QB), 1)
    if j * QB >= prompt:
        keys, queries = j * QB - prompt, i * QB - prompt
        same = seg_col[keys : keys + QB, :] == seg_row[:, queries : queries + QB]
        mask = same if mask is None else mask & same
    return mask


def flip_chip(x, sq, fx, fy):
    px = 1 - x if fx else x
    py = 1 - sq if fy else sq
    return px, py


SOURCES = ((1, 0), (0, 1), (0, 0), (1, 1))
OWN = 2
AWAY = (0, 1, 3)


class Line:
    def __init__(self, nz, dp, sq, z, sources, target, sems):
        self.nz, self.dp, self.sq, self.z = nz, dp, sq, z
        self.sources, self.target, self.sems = sources, target, sems

    def copy(self, stage, up):
        nz, z = self.nz, self.z
        zone = z - (stage - 1) if up else z + (stage - 1)
        zone = lax.rem(zone + nz, nz)
        to = lax.rem(z + 1, nz) if up else lax.rem(z + nz - 1, nz)
        i = stage - 1
        send, recv = (self.sems[0], self.sems[1]) if up else (self.sems[2], self.sems[3])
        return remote(
            self.sources(stage, zone), self.target.at[zone], send.at[i], recv.at[i], (self.dp, self.sq, to)
        )

    def arrival(self, stage, up):
        nz, z = self.nz, self.z
        zone = lax.rem((z - stage if up else z + stage) + nz, nz)
        to = lax.rem(z + 1, nz) if up else lax.rem(z + nz - 1, nz)
        i = stage - 1
        send, recv = (self.sems[0], self.sems[1]) if up else (self.sems[2], self.sems[3])
        return remote(
            self.sources(stage, zone), self.target.at[zone], send.at[i], recv.at[i], (self.dp, self.sq, to)
        )

    def sends(self, stage, up):
        z, nz = self.z, self.nz
        return (z < nz - 1) & (z >= stage - 1) if up else (z > 0) & (z <= nz - stage)

    def gets(self, stage, up):
        return self.z >= stage if up else self.z <= self.nz - 1 - stage

    def start(self, stage):
        for up in (True, False):

            @pl.when(self.sends(stage, up))
            def _(up=up):
                self.copy(stage, up).start()

    def wait_recv(self, stage):
        for up in (True, False):

            @pl.when(self.gets(stage, up))
            def _(up=up):
                self.arrival(stage, up).wait_recv()

    def wait_send(self, stage):
        for up in (True, False):

            @pl.when(self.sends(stage, up))
            def _(up=up):
                self.copy(stage, up).wait_send()


def eighth(x, prompt):
    row = x.astype(F32)
    col = jnp.broadcast_to(row, (128, row.shape[1])).T[:, 0:1]
    return row, col


def begin_kernel(
    prompt, nz, capacity, x_ref, in_ref, out_ref, router_ref, gains_ref, seg_ref, ids_ref, cot_ref, piece_ref,
    xs_ref, w_ref, qkv_ref, mixed_ref, lse_ref, att_ref, raw_ref, row_ref, col_ref, near_ref,
    pack, vt, local, send_t, recv_t, send_z, recv_z, send_p, recv_p, send_c, recv_c, send_o, recv_o, *line_sems,
):
    dp, sq, z, x, core = place()
    rows, width = x_ref.shape
    shard = in_ref.shape[0]
    part = shard // 4
    half = width // 2
    pairs = half // 128
    own_cols = 3 * half
    lead = own_cols + 128
    sibling = (x * 2 + 1 - core, sq, z)
    partner = (dp, 1 - sq, z)
    across = ((1 - x) * 2 + core, sq, z)
    others = [(dp, sq, lax.rem(z + d, nz)) for d in range(1, nz)]
    base = pl.multiple_of(sq * rows, rows)
    there = pl.multiple_of((1 - sq) * rows, rows)
    groups = (pl.ds(0, lead), pl.ds(lead, width))

    packs = [
        pltpu.make_async_copy(
            in_ref.at[:, pl.ds(al(i * width + sq * half), half)], pack.at[:, pl.ds(i * half, half)], local.at[i]
        )
        for i in range(3)
    ]
    packs.append(pltpu.make_async_copy(out_ref, pack.at[:, groups[1]], local.at[3]))
    for c in packs:
        c.start()
    lane = iota((1, 128), 1)
    small = jnp.zeros((shard, 128), F32)
    for e in range(EXPERTS):
        small = jnp.where(lane == e, router_ref[:, e : e + 1].astype(F32), small)
    for e in range(2):
        small = jnp.where(lane == EXPERTS + e, gains_ref[:, e : e + 1].astype(F32), small)
    pack[:, own_cols:lead] = small.astype(BF)
    greet([sibling, partner, across] + others)
    tokens = remote(x_ref, xs_ref.at[pl.ds(base, rows)], send_t, recv_t, partner)
    tokens.start()
    for c in packs:
        c.wait()

    def at(zs, px, co, g):
        return w_ref.at[pl.ds(pl.multiple_of(zs * shard + (px * 2 + co) * part, part), part), groups[g]]

    def along(d, g):
        src = pack.at[pl.ds(pl.multiple_of((x * 2 + core) * part, part), part), groups[g]]
        return remote(src, at(z, x, core, g), send_z.at[d - 1, g], recv_z.at[d - 1, g], others[d - 1])

    def source(d):
        return lax.rem(z + nz - d, nz)

    def over(d, g, px):
        ref = at(source(d), px, core, g)
        return remote(ref, ref, send_p.at[d - 1, g], recv_p.at[d - 1, g], across)

    def beside(d, g, i, co):
        ref = at(source(d), (x, 1 - x)[i], co, g)
        return remote(ref, ref, send_c.at[d - 1, g, i], recv_c.at[d - 1, g, i], sibling)

    for d in range(1, nz):
        along(d, 0).start()
    own = pltpu.make_async_copy(pack, w_ref.at[pl.ds(pl.multiple_of(z * shard, shard), shard)], local.at[4])
    own.start()
    xs_ref[pl.ds(base, rows), :] = x_ref[...]
    ids = ids_ref[...]
    chosen = jnp.where((ids[:, 0:1] == lane) | (ids[:, 1:2] == lane), 1.0, 0.0)
    earlier = (iota((rows, rows), 1) < iota((rows, rows), 0)).astype(F32).astype(BF)
    places = jnp.where(chosen > 0, nn(earlier, chosen.astype(BF)), -1.0)
    col_ref[...] = places
    places = places.T[0:8, :]
    row_ref[...] = places

    def gather(g):
        for d in range(1, nz):
            along(d, g).wait_recv()
            over(d, g, x).start()
            beside(d, g, 0, core).start()
        if g == 0:
            line.start(1)
            for d in range(1, nz):
                along(d, 1).start()
        for d in range(1, nz):
            over(d, g, 1 - x).wait_recv()
            beside(d, g, 1, core).start()

    def gathered(g):
        for d in range(1, nz):
            for i in range(2):
                beside(d, g, i, 1 - core).wait_recv()

    stay = pltpu.make_async_copy(piece_ref, near_ref.at[z], local.at[5])
    stay.start()
    line = Line(
        nz, dp, sq, z, lambda stage, zone: piece_ref if stage == 1 else near_ref.at[zone], near_ref, line_sems
    )
    gather(0)
    gathered(0)
    own.wait()
    tokens.wait_recv()

    gain = w_ref[:, own_cols:lead].astype(F32).T[EXPERTS : EXPERTS + 1, :]
    xf = xs_ref[...].astype(F32)
    normed = (xf * lax.rsqrt(jnp.mean(xf * xf, axis=1, keepdims=True) + EPSILON) * gain).astype(BF)
    for i in range(3):
        got = nn(normed, w_ref[:, i * half : (i + 1) * half]).astype(BF)
        for p in range(pairs):
            qkv_ref[p, i] = got[:, p * 128 : (p + 1) * 128]

    blocks = 2 * rows // QB
    const = HEAD_DIM ** (-0.5) * LOG2E
    seg_row, seg_col = eighth(seg_ref[...], prompt)

    def back(p, own_side):
        src = mixed_ref.at[p, pl.ds(there, rows)]
        side = sq if own_side else 1 - sq
        return remote(
            src, att_ref.at[:, pl.ds(al(side * half + p * 128), 128)], send_o.at[p], recv_o.at[p], partner
        )

    @pl.loop(0, pairs)
    def _(p):
        vt[0:128, :] = qkv_ref[p, 2].T
        vt[128:144, :] = jnp.ones((16, vt.shape[1]), BF)
        for i in range(blocks):
            here = slice(i * QB, (i + 1) * QB)
            both = []
            for h in range(2):
                lanes = iota((1, 128), 1) // HEAD_DIM == h
                q = jnp.where(lanes, qkv_ref[p, 0, here, :], jnp.zeros((), BF))
                tiles = []
                for j in range(i + 1):
                    s = nt(qkv_ref[p, 1, j * QB : (j + 1) * QB, :], q)
                    mask = allowed_tile(j, i, prompt, seg_col, seg_row)
                    if mask is not None:
                        s = jnp.where(mask, s, NEGATIVE)
                    tiles.append(s)
                top = functools.reduce(
                    jnp.maximum, [jnp.max(s, axis=0, keepdims=True) for s in tiles]
                )
                top = top * const
                acc = None
                for j, s in enumerate(tiles):
                    pr = jnp.exp2(s * const - top).astype(BF)
                    add = nn(vt[:, j * QB : (j + 1) * QB], pr)
                    acc = add if acc is None else acc + add
                total = acc[128:129, :]
                lse_ref[p, h : h + 1, here] = top + jnp.log2(total)
                low = h * HEAD_DIM
                both.append(acc[low : low + HEAD_DIM, :] * (1.0 / total))
            mixed_ref[p, here, :] = jnp.concatenate(both, axis=0).T.astype(BF)
        back(p, True).start()
        att_ref[:, pl.ds(al(sq * half + p * 128), 128)] = mixed_ref[p, pl.ds(base, rows), :]

        @pl.when(p == 0)
        def _():
            line.wait_recv(1)
            line.start(2)
            gather(1)

    for j, (px, py) in enumerate([flip_chip(x, sq, *f) for f in SOURCES]):
        hot = hot_rows(pick_row(row_ref[...], px * 2 + py), capacity)
        raw_ref[j] = nn(hot, cot_ref[...]).astype(BF)
    for p in range(pairs):
        back(p, False).wait_recv()
        back(p, True).wait_send()
    gathered(1)
    tokens.wait_send()
    for g in range(2):
        for d in range(1, nz):
            along(d, g).wait_send()
            over(d, g, x).wait_send()
            for i in range(2):
                beside(d, g, i, core).wait_send()
    line.wait_recv(2)
    line.wait_send(1)
    line.wait_send(2)
    stay.wait()


def begin(x, attn_in, attn_out, router, gains, segments, ids, cot, piece, prompt, nz, capacity, cid):
    rows, width = x.shape
    shard = attn_in.shape[0]
    pairs = width // 256
    cols = 3 * width // 2 + 128 + width
    dma = pltpu.SemaphoreType.DMA
    two = lambda *shape: [dma(shape), dma(shape)]
    return pl.pallas_call(
        functools.partial(begin_kernel, prompt, nz, capacity),
        out_shape=(
            sds((2 * rows, width), BF),
            sds((shard * nz, cols), BF),
            sds((pairs, 3, 2 * rows, 128), BF),
            sds((pairs, 2 * rows, 128), BF),
            sds((pairs, 8, 2 * rows), F32),
            sds((rows, width), BF),
            sds((4, capacity, width), BF),
            sds((8, rows), F32),
            sds((rows, 128), F32),
            sds((nz,) + piece.shape, BF),
        ),
        in_specs=[VM, ANY, ANY, VM, VM, VM, VM, VM, ANY],
        out_specs=(VM,) * 9 + (ANY,),
        scratch_shapes=[
            pltpu.VMEM((shard, cols), BF),
            pltpu.VMEM((144, 2 * rows), BF),
            dma((6,)),
        ]
        + two() + two(nz - 1, 2) + two(nz - 1, 2) + two(nz - 1, 2, 2) + two(pairs) + two(2) + two(2),
        compiler_params=params(cid),
        name="begin",
    )(x, attn_in, attn_out, router, gains, segments, ids, cot, piece)


def softmax_lanes(logits):
    live = iota(logits.shape, 1) < EXPERTS
    logits = jnp.where(live, logits, NEGATIVE)
    expo = jnp.where(live, jnp.exp(logits - jnp.max(logits, axis=1, keepdims=True)), 0.0)
    return expo / jnp.sum(expo, axis=1, keepdims=True)


def pick_row(table, e):
    return jnp.sum(jnp.where(iota((8, 1), 0) == e, table, 0.0), axis=0, keepdims=True)


def pick_col(table, e):
    return jnp.sum(jnp.where(iota((1, 128), 1) == e, table, 0.0), axis=1, keepdims=True)


def hot_rows(row, capacity):
    return (row == iota((capacity, 1), 0).astype(F32)).astype(F32).astype(BF)


def hot_cols(col, capacity):
    return (col == iota((1, capacity), 1).astype(F32)).astype(F32).astype(BF)


GELU_A = 0.7978845608028654
GELU_B = GELU_A * 0.044715


def expert_step(x, g, w):
    width = x.shape[1]
    first, second = w[:, :width], w[:, width:]
    pre = nt(x, first)
    back = nt(g, second)
    square = pre * pre
    t = jnp.tanh(pre * (GELU_A + GELU_B * square))
    rise = 0.5 + 0.5 * t
    act = (pre * rise).astype(BF)
    slope = rise + (0.5 * pre) * (1.0 - t * t) * (GELU_A + (3.0 * GELU_B) * square)
    grad_pre = (back * slope).astype(BF)
    return nn(act, second), nn(grad_pre, first), tn(grad_pre, x), tn(act, g)


def experts_kernel(
    capacity, nz, x_ref, att_ref, w_hbm, places_row, places_col, raw_send, near_ref,
    hidden_ref, probs_ref, back_gin, out_res, back_dot, dw_ref,
    wp, send_in, got_in, send_gate, got_gate, own_w, theirs, grad, res_acc, gin_acc, out_gin, out_dot, dw_away, dw_got,
    raw_ref, local, send_x, recv_x, send_w, recv_w, send_i, recv_i, send_t, recv_t, send_r, recv_r, send_d, recv_d, send_v, recv_v, *line_sems,
):
    dp, sq, z, x, core = place()
    rows, width = x_ref.shape
    sibling = (x * 2 + 1 - core, sq, z)
    corner = [flip_chip(x, sq, *f) for f in SOURCES]
    plane = [(px * 2 + core, py, z) for px, py in corner]
    experts_of = [px * 2 + py for px, py in corner]
    beside_z = (dp, sq, z + 1 - 2 * lax.rem(z, 2))
    shift = jnp.where(z >= nz // 2, 1, 0)
    far_zone = jnp.where(z >= nz // 2, 0, nz - 1)
    at_end = (z == 0) | (z == nz - 1)
    near_peers = [sibling] + [plane[j] for j in AWAY]
    barrier = pltpu.get_barrier_semaphore()
    for peer in near_peers:
        pl.semaphore_signal(barrier, inc=1, device_id=peer, device_id_type=MESH)

    @pl.when(at_end)
    def _():
        pl.semaphore_signal(barrier, inc=1, device_id=beside_z, device_id_type=MESH)

    pl.semaphore_wait(barrier, len(near_peers) + jnp.where(at_end, 0, 1))
    line = Line(nz, dp, sq, z, lambda stage, zone: near_ref.at[zone], own_w, line_sems)
    line.start(nz - 1)

    def go_raw(j):
        return remote(raw_send.at[j], raw_ref.at[j], send_x.at[j], recv_x.at[j], plane[j])

    go_raw(0).start()
    go_raw(1).start()

    def weights(slot):
        if slot == nz - 1:
            return remote(own_w.at[far_zone], theirs.at[far_zone], send_w.at[slot], recv_w.at[slot], sibling)
        zone = slot + shift
        return remote(near_ref.at[zone], theirs.at[zone], send_w.at[slot], recv_w.at[slot], sibling)

    lifts = []
    for i in range(nz - 1):
        weights(i).start()
        lifts.append(pltpu.make_async_copy(near_ref.at[i + shift], own_w.at[i + shift], local.at[2 + i]))
    for c in lifts:
        c.start()
    far_lift = pltpu.make_async_copy(near_ref.at[far_zone], own_w.at[far_zone], local.at[1 + nz])

    @pl.when(jnp.logical_not(at_end))
    def _():
        far_lift.start()

    own_raw = pltpu.make_async_copy(raw_send.at[OWN], raw_ref.at[OWN], local.at[1])
    own_raw.start()
    load = pltpu.make_async_copy(w_hbm.at[:, 3 * width // 2 :], wp, local.at[0])
    load.start()
    load.wait()

    hidden = x_ref[...].astype(F32) + nn(att_ref[...], wp[:, 128:])
    hidden_ref[...] = hidden
    r_two = lax.rsqrt(jnp.mean(hidden * hidden, axis=1, keepdims=True) + EPSILON)
    small = wp[:, :128]
    gain = small.astype(F32).T[EXPERTS + 1 : EXPERTS + 2, :]
    routed = (hidden * r_two * gain).astype(BF)
    probs = softmax_lanes(nn(routed, small))
    probs_ref[...] = probs
    flat = probs.T[0:8, :]
    high = flat.astype(BF)
    rest = flat - high.astype(F32)
    mid = rest.astype(BF)
    low = (rest - mid.astype(F32)).astype(BF)
    split = jnp.concatenate([high.astype(F32), mid.astype(F32), low.astype(F32)], axis=0).astype(BF)

    def go_in(j):
        return remote(send_in.at[j], got_in.at[j], send_i.at[j], recv_i.at[j], plane[j])

    def go_gate(j):
        return remote(send_gate.at[j], got_gate.at[j], send_t.at[j], recv_t.at[j], plane[j])

    for j in range(4):
        e = experts_of[j]
        taken = nn(hot_rows(pick_row(places_row[...], e), capacity), routed).astype(BF)
        three = nn(split, hot_cols(pick_col(places_col[...], e), capacity))
        gate = three[0:8] + three[8:16] + three[16:24]
        gate = jnp.broadcast_to(pick_row(gate, e), gate.shape)
        if j != OWN:
            send_in[j] = taken
            send_gate[j] = gate
            go_gate(j).start()
        if j < OWN:
            go_in(j).start()
        if j == OWN:
            got_in[j] = taken
            got_gate[j] = gate
    own_raw.wait()
    for c in lifts:
        c.wait()
    for i in range(nz - 1):
        weights(i).wait_recv()

    def go_gin(j):
        return remote(out_gin.at[j], back_gin.at[j], send_r.at[j], recv_r.at[j], plane[j])

    def go_dot(j):
        return remote(out_dot.at[j], back_dot.at[j], send_d.at[j], recv_d.at[j], plane[j])

    def go_dw(n):
        return remote(dw_away.at[n], dw_got.at[n], send_v.at[n], recv_v.at[n], sibling)

    def arrive(lo, hi):
        for j in range(lo, hi):
            if j != OWN:
                go_raw(j).wait_recv()
                go_in(j).wait_recv()
                go_gate(j).wait_recv()
            gate = got_gate[j].T[:, 0:1]
            grad[j] = (raw_ref[j].astype(F32) * gate).astype(BF)

    def chunk(lo, hi, w_ref, dw, d, first, at):
        count = (hi - lo) * capacity
        xs = got_in[lo:hi].reshape(count, width)
        gs = grad[lo:hi].reshape(count, width)
        res, gin, d_first, d_second = expert_step(xs, gs, w_ref[d])
        here = slice(at * capacity, at * capacity + count)
        res_acc[here, :] += res
        gin_acc[here, :] += gin
        if first:
            dw[d, :, :width] = d_first.astype(BF)
            dw[d, :, width:] = d_second.astype(BF)
        else:
            dw[d, :, :width] = (dw[d, :, :width].astype(F32) + d_first).astype(BF)
            dw[d, :, width:] = (dw[d, :, width:].astype(F32) + d_second).astype(BF)

    def send_back(lo, hi, at):
        for j in range(lo, hi):
            here = slice((at + j - lo) * capacity, (at + j - lo + 1) * capacity)
            prod = res_acc[here, :] * raw_ref[j].astype(F32)
            narrow = functools.reduce(jnp.add, [prod[:, i : i + 128] for i in range(0, width, 128)])
            inner = jnp.broadcast_to(jnp.sum(narrow.T, axis=0, keepdims=True), (8, capacity))
            if j != OWN:
                out_gin[j] = gin_acc[here, :].astype(BF)
                out_dot[j] = inner
                go_gin(j).start()
                go_dot(j).start()
            else:
                back_gin[j] = gin_acc[here, :].astype(BF)
                back_dot[j] = inner
        for j in range(lo, hi):
            here = slice((at + j - lo) * capacity, (at + j - lo + 1) * capacity)
            out_res[j] = res_acc[here, :].astype(BF)

    both = ((theirs, dw_away), (own_w, dw_ref))
    res_acc[...] = jnp.zeros(res_acc.shape, F32)
    gin_acc[...] = jnp.zeros(gin_acc.shape, F32)
    arrive(OWN, OWN + 1)
    for w_ref, dw in both:

        @pl.loop(0, nz - 1)
        def _(i):
            chunk(OWN, OWN + 1, w_ref, dw, i + shift, True, OWN)

    arrive(0, OWN)
    go_raw(3).start()
    go_in(3).start()
    for w_ref, dw in both:

        @pl.loop(0, nz - 1)
        def _(i):
            chunk(0, OWN, w_ref, dw, i + shift, False, 0)

    @pl.when(jnp.logical_not(at_end))
    def _():
        far_lift.wait()

    line.wait_recv(nz - 1)
    weights(nz - 1).start()
    chunk(0, OWN + 1, own_w, dw_ref, far_zone, True, 0)
    weights(nz - 1).wait_recv()
    chunk(0, OWN + 1, theirs, dw_away, far_zone, True, 0)
    send_back(0, OWN + 1, 0)
    arrive(3, 4)
    res_acc[0:capacity, :] = jnp.zeros((capacity, width), F32)
    gin_acc[0:capacity, :] = jnp.zeros((capacity, width), F32)

    @pl.loop(0, nz)
    def _(d):
        chunk(3, 4, theirs, dw_away, d, False, 0)
        go_dw(d).start()

    @pl.loop(0, nz)
    def _(d):
        chunk(3, 4, own_w, dw_ref, d, False, 0)

    send_back(3, 4, 0)
    for n in range(nz):
        go_dw(n).wait_recv()
        dw_ref[n] = (dw_ref[n].astype(F32) + dw_got[n].astype(F32)).astype(BF)
    for j in AWAY:
        go_gin(j).wait_recv()
        go_dot(j).wait_recv()
    line.wait_send(nz - 1)
    for n in range(nz):
        weights(n).wait_send()
        go_dw(n).wait_send()
    for j in AWAY:
        for c in (go_raw(j), go_in(j), go_gate(j), go_gin(j), go_dot(j)):
            c.wait_send()


def experts(x, attended, whole, places_row, places_col, raw, near, capacity, nz, cid):
    rows, width = x.shape
    part = near.shape[1]
    slots = sds((4, capacity, width), BF)
    small = sds((4, 8, capacity), F32)
    dma = pltpu.SemaphoreType.DMA
    two = lambda *shape: [dma(shape), dma(shape)]
    vm = pltpu.VMEM
    return pl.pallas_call(
        functools.partial(experts_kernel, capacity, nz),
        out_shape=(
            sds((rows, width), F32),
            sds((rows, 128), F32),
            slots,
            slots,
            small,
            sds((nz, part, 2 * width), BF),
        ),
        in_specs=[VM, VM, ANY, VM, VM, ANY, ANY],
        out_specs=(VM,) * 6,
        scratch_shapes=[
            vm((rows, width + 128), BF),
            vm((4, capacity, width), BF),
            vm((4, capacity, width), BF),
            vm((4, 8, capacity), F32),
            vm((4, 8, capacity), F32),
            vm((nz, part, 2 * width), BF),
            vm((nz, part, 2 * width), BF),
            vm((4, capacity, width), BF),
            vm((3 * capacity, width), F32),
            vm((3 * capacity, width), F32),
            vm((4, capacity, width), BF),
            vm((4, 8, capacity), F32),
            vm((nz, part, 2 * width), BF),
            vm((nz, part, 2 * width), BF),
            vm((4, capacity, width), BF),
            dma((2 + nz,)),
        ]
        + two(4) + two(nz) + two(4) + two(4) + two(4) + two(4) + two(nz) + two(nz - 1) + two(nz - 1),
        compiler_params=params(cid),
        name="experts",
    )(x, attended, whole, places_row, places_col, raw, near)


PARTS = 4


def finish_kernel(
    prompt, nz, capacity, xs_ref, qkv_ref, mixed_ref, lse_ref, w_ref, seg_ref, hidden_ref, probs_ref, places_ref,
    dot_ref, gin_ref, res_ref, cot_ref, att_ref, part_ref,
    out_ref, dx_ref, din_out, dout_out, droute_out, dgains_out, got_up, got_down, dw_all,
    gh, gatt, got_res, grad, qm, dom, kt, dqt, dcat, norm_t, sums, got_c, got_x, got_z, mine, fin, got_f, total,
    send_dx, got_dx, own_gn, stage, dw_sum, ahead,
    local, send_r, recv_r, send_g, recv_g, send_c, recv_c, send_x, recv_x, send_z, recv_z, send_d, recv_d, send_f, recv_f,
    send_a, recv_a, send_b, recv_b, send_u, recv_u, send_l, recv_l, send_v, recv_v, send_h, recv_h, send_k, recv_k,
):
    dp, sq, z, x, core = place()
    rows, width = gatt.shape
    half = width // 2
    pairs = half // 128
    shard = width // nz
    part = shard // 4
    own_cols = 3 * half
    lead = own_cols + 128
    chip = x * 2 + sq
    chip_x, chip_y, chip_d = (1 - x) * 2 + sq, x * 2 + 1 - sq, (1 - x) * 2 + 1 - sq
    sibling = (x * 2 + 1 - core, sq, z)
    partner = (dp, 1 - sq, z)
    across = ((1 - x) * 2 + core, sq, z)
    others = [(dp, sq, lax.rem(z + d, nz)) for d in range(1, nz)]
    base = pl.multiple_of(sq * rows, rows)
    there = pl.multiple_of((1 - sq) * rows, rows)
    corner = [flip_chip(x, sq, *f) for f in SOURCES]
    plane = [(px * 2 + core, py, z) for px, py in corner]
    experts_of = [px * 2 + py for px, py in corner]
    greet([sibling] + [plane[j] for j in AWAY] + others)

    quarter = stage.shape[1]

    def rows_of(k):
        return pl.ds(k * quarter, quarter)

    def hop(k, t, up, src):
        to = lax.rem(z + 1, nz) if up else lax.rem(z + nz - 1, nz)
        got, send, recv = (got_up, send_u, recv_u) if up else (got_down, send_l, recv_l)
        return remote(src, got.at[k, t], send.at[k, t], recv.at[k, t], (dp, sq, to))

    def legs(slot):
        ups = (True, slot, list(range(nz - 1, slot, -1)))
        downs = (False, nz - 1 - slot, list(range(0, nz - 1 - slot)))
        return ups, downs

    def line_slot(k, slot):
        for up, sender, zones in legs(slot):

            @pl.when(z == sender)
            def _(up=up, zones=zones):
                if slot == 0:
                    for t in zones:
                        hop(k, t, up, part_ref.at[t, rows_of(k)]).start()
                    return
                got = got_up if up else got_down
                loads = []
                for i, t in enumerate(zones):
                    hop(k, t, up, ahead.at[k % 2, 0]).wait_recv()
                    loads.append(pltpu.make_async_copy(got.at[k, t], stage.at[2 * i], local.at[2 * i]))
                    loads.append(pltpu.make_async_copy(part_ref.at[t, rows_of(k)], stage.at[2 * i + 1], local.at[2 * i + 1]))
                for c in loads:
                    c.start()
                for i, t in enumerate(zones):
                    to = ahead.at[k % 2, i if slot == 1 else 2]
                    if k > 1:
                        hop(k - 2, t, up, to).wait_send()
                    loads[2 * i].wait()
                    loads[2 * i + 1].wait()
                    to[...] = (stage[2 * i].astype(F32) + stage[2 * i + 1].astype(F32)).astype(BF)
                    hop(k, t, up, to).start()

    def line_end():
        for slot in range(nz - 1):
            for up, sender, zones in legs(slot):

                @pl.when(z == sender)
                def _(up=up, zones=zones, slot=slot):
                    for k in range(PARTS) if slot == 0 else range(PARTS - 2, PARTS):
                        for i, t in enumerate(zones):
                            src = part_ref.at[t, rows_of(k)] if slot == 0 else ahead.at[k % 2, i if slot == 1 else 2]
                            hop(k, t, up, src).wait_send()

    def share(k, ch, send, recv, peer, own=False):
        at = dw_all.at[core, ch, pl.ds(k * quarter, quarter)]
        return remote(dw_sum.at[k] if own else at, at, send, recv, peer)

    def keep(k):
        return pltpu.make_async_copy(
            dw_sum.at[k], dw_all.at[core, chip, pl.ds(k * quarter, quarter)], local.at[nz + k]
        )

    def sum_part(k):
        own = pltpu.make_async_copy(part_ref.at[z, rows_of(k)], stage.at[2], local.at[2])
        own.start()
        for i, up in enumerate((True, False)):
            got = got_up if up else got_down
            has = z > 0 if up else z < nz - 1

            @pl.when(has)
            def _(i=i, up=up, got=got):
                hop(k, z, up, ahead.at[0, 0]).wait_recv()
                c = pltpu.make_async_copy(got.at[k, z], stage.at[i], local.at[i])
                c.start()
                c.wait()

            @pl.when(jnp.logical_not(has))
            def _(i=i):
                stage[i] = jnp.zeros(stage.shape[1:], BF)

        own.wait()
        dw_sum[k] = (stage[0].astype(F32) + stage[1].astype(F32) + stage[2].astype(F32)).astype(BF)
        share(k, chip, send_v.at[k], recv_v.at[k], partner, True).start()
        share(k, chip, send_h.at[k, 0], recv_h.at[k, 0], across, True).start()
        share(k, chip, send_k.at[k, 0], recv_k.at[k, 0], sibling, True).start()
        keep(k).start()

    def pass_part(k):
        share(k, chip_y, send_v.at[k], recv_v.at[k], partner).wait_recv()
        share(k, chip_y, send_h.at[k, 1], recv_h.at[k, 1], across).start()
        share(k, chip_y, send_k.at[k, 1], recv_k.at[k, 1], sibling).start()

    def last_part(k):
        share(k, chip_x, send_h.at[k, 0], recv_h.at[k, 0], across).wait_recv()
        share(k, chip_x, send_k.at[k, 2], recv_k.at[k, 2], sibling).start()
        share(k, chip_d, send_h.at[k, 1], recv_h.at[k, 1], across).wait_recv()
        share(k, chip_d, send_k.at[k, 3], recv_k.at[k, 3], sibling).start()

    others_of = [chip, chip_y, chip_x, chip_d]

    def end_parts():
        for k in range(PARTS):
            for i in range(4):
                at = dw_all.at[1 - core, others_of[i], rows_of(k)]
                remote(at, at, send_k.at[k, i], recv_k.at[k, i], sibling).wait_recv()
                share(k, others_of[i], send_k.at[k, i], recv_k.at[k, i], sibling, i == 0).wait_send()
            share(k, chip, send_v.at[k], recv_v.at[k], partner, True).wait_send()
            share(k, chip, send_h.at[k, 0], recv_h.at[k, 0], across, True).wait_send()
            share(k, chip_y, send_h.at[k, 1], recv_h.at[k, 1], across).wait_send()
            keep(k).wait()
        line_end()

    groups = (pl.ds(0, lead), pl.ds(lead, width))
    order = [lax.rem(z + d, nz) for d in range(1, nz + 1)]

    def piece(zz, px, co):
        return pl.ds(pl.multiple_of(zz * shard + (px * 2 + co) * part, part), part)

    def to_core(g, n, i):
        src = sums.at[piece(order[n], (1 - x, x)[i], 1 - core), groups[g]]
        return remote(src, got_c.at[n, i, :, groups[g]], send_c.at[g, n, i], recv_c.at[g, n, i], sibling)

    def to_x(g, n):
        src = sums.at[piece(order[n], 1 - x, core), groups[g]]
        return remote(src, got_x.at[n, :, groups[g]], send_x.at[g, n], recv_x.at[g, n], across)

    def to_z(g, n):
        return remote(
            mine.at[n, :, groups[g]], got_z.at[n, :, groups[g]], send_z.at[g, n], recv_z.at[g, n], others[n]
        )

    def cols_of(g):
        return slice(0, lead) if g == 0 else slice(lead, lead + width)

    def reduce_core(g, n):
        cols = cols_of(g)
        for i in range(2):
            to_core(g, n, i).wait_recv()
            at = piece(order[n], (1 - x, x)[i], core)
            sums[at, cols] = (sums[at, cols].astype(F32) + got_c[n, i, :, cols].astype(F32)).astype(BF)
            if i == 0:
                to_x(g, n).start()

    def reduce_x(g, n):
        cols = cols_of(g)
        to_x(g, n).wait_recv()
        acc = sums[piece(order[n], x, core), cols].astype(F32) + got_x[n, :, cols].astype(F32)
        if n < nz - 1:
            mine[n, :, cols] = acc.astype(BF)
            to_z(g, n).start()
        return acc

    def reduce_z(g, acc):
        cols = cols_of(g)
        for n in range(nz - 1):
            to_z(g, n).wait_recv()
            acc = acc + got_z[n, :, cols].astype(F32)
        fin[:, cols] = acc.astype(BF)

    line_slot(0, 0)
    fetch = [pltpu.make_async_copy(gin_ref.at[j], dcat.at[pl.ds(j * capacity, capacity), 0:width], local.at[j]) for j in range(4)]
    fetch.append(pltpu.make_async_copy(cot_ref, send_dx, local.at[4]))
    fetch.append(pltpu.make_async_copy(att_ref, norm_t.at[:, 0:rows], local.at[5]))
    fetch.append(pltpu.make_async_copy(res_ref.at[OWN], got_res.at[OWN], local.at[6]))
    for c in fetch:
        c.start()
    results = {j: remote(res_ref.at[j], got_res.at[j], send_r.at[j], recv_r.at[j], plane[j]) for j in AWAY}
    for c in fetch:
        c.wait()
    hidden = hidden_ref[...]
    probs = probs_ref[...]
    small = w_ref[:, own_cols:lead]
    gain_two = small.astype(F32).T[EXPERTS + 1 : EXPERTS + 2, :]
    lane = iota(probs.shape, 1)
    back = None
    grad_probs = jnp.zeros_like(probs)
    for j in range(4):
        pick = hot_cols(pick_col(places_ref[...], experts_of[j]), capacity)
        add = nn(pick, dcat[j * capacity : (j + 1) * capacity, 0:width])
        back = add if back is None else back + add
        inner = jnp.sum(pick.astype(F32) * dot_ref[j][0:1, :], axis=1, keepdims=True)
        grad_probs = jnp.where(lane == experts_of[j], inner, grad_probs)
    mixed = jnp.sum(probs * grad_probs, axis=1, keepdims=True)
    low = (probs * (grad_probs - mixed)).astype(BF)
    r_two = lax.rsqrt(jnp.mean(hidden * hidden, axis=1, keepdims=True) + EPSILON)
    h_norm = hidden * r_two
    routed = (h_norm * gain_two).astype(BF)
    grad_routed = back + nt(low, small)
    dg_two = jnp.sum(grad_routed * h_norm, axis=0, keepdims=True)
    u = grad_routed * gain_two
    grad_hidden = send_dx[...].astype(F32) + r_two * (
        u - h_norm * jnp.mean(u * h_norm, axis=1, keepdims=True)
    )
    gh[...] = grad_hidden
    hid_low = grad_hidden.astype(BF)
    gatt[...] = nt(hid_low, w_ref[:, lead:]).astype(BF)

    def give(p, to):
        return remote(
            gatt.at[:, pl.ds(al((1 - sq) * half + p * 128), 128)],
            grad.at[p, pl.ds(to, rows)],
            send_g.at[p],
            recv_g.at[p],
            partner,
        )

    for p in range(pairs):
        give(p, base).start()
    line_slot(1, 0)
    for p in range(pairs):
        grad[p, pl.ds(base, rows), :] = gatt[:, pl.ds(al(sq * half + p * 128), 128)]
    d_route = tn(routed, low)
    sums[:, cols_of(1)] = tn(norm_t[:, 0:rows], hid_low).astype(BF)
    for n in range(nz):
        for i in range(2):
            to_core(1, n, i).start()
    seg_row, seg_col = eighth(seg_ref[...], prompt)
    gain = w_ref[:, own_cols:lead].astype(F32).T[EXPERTS : EXPERTS + 1, :]

    def norm_of(at):
        xf = xs_ref[at, :].astype(F32)
        r_one = lax.rsqrt(jnp.mean(xf * xf, axis=1, keepdims=True) + EPSILON)
        return xf * r_one, r_one

    for i in range(2):
        at = slice(i * rows, (i + 1) * rows)
        norm_t[:, at] = (norm_of(at)[0] * gain).astype(BF).T

    line_slot(0, 1)
    blocks = 2 * rows // QB
    scale = HEAD_DIM ** (-0.5)
    zero = jnp.zeros((), BF)

    @pl.loop(0, pairs)
    def _(p):
        give(p, there).wait_recv()
        kt[...] = qkv_ref[p, 1].T
        prod = (grad[p].astype(F32) * mixed_ref[p].astype(F32)).T
        delta = []
        for h in range(2):
            lanes = iota((1, 128), 1) // HEAD_DIM == h
            qm[h] = jnp.where(lanes, qkv_ref[p, 0], zero) * jnp.asarray(scale, BF)
            dom[h] = jnp.where(lanes, grad[p], zero)
            low = h * HEAD_DIM
            delta.append(jnp.sum(prod[low : low + HEAD_DIM, :], axis=0, keepdims=True))
        for j in range(blocks):
            keys = slice(j * QB, (j + 1) * QB)
            k, v = qkv_ref[p, 1, keys, :], qkv_ref[p, 2, keys, :]
            dk = dv = None
            for i in range(j, blocks):
                at = slice(i * QB, (i + 1) * QB)
                mask = allowed_tile(j, i, prompt, seg_col, seg_row)
                for h in range(2):
                    s = nt(k, qm[h, at, :])
                    dpr = nt(v, dom[h, at, :])
                    pr = jnp.exp2(s * LOG2E - lse_ref[p, h : h + 1, at])
                    if mask is not None:
                        pr = jnp.where(mask, pr, 0.0)
                    ds = (pr * (dpr - delta[h][:, at])).astype(BF)
                    a = nn(pr.astype(BF), dom[h, at, :])
                    b = nn(ds, qm[h, at, :])
                    c = nn(kt[h * HEAD_DIM : (h + 1) * HEAD_DIM, keys], ds)
                    dv = a if dv is None else dv + a
                    dk = b if dk is None else dk + b
                    to = slice(h * HEAD_DIM, (h + 1) * HEAD_DIM)
                    dqt[to, at] = c if j == 0 else dqt[to, at] + c
            dcat[keys, pl.ds(al(half + p * 128), 128)] = dk.astype(BF)
            dcat[keys, pl.ds(al(2 * half + p * 128), 128)] = dv.astype(BF)
        dcat[:, pl.ds(al(p * 128), 128)] = (dqt[...] * scale).T.astype(BF)

        @pl.when(p == 0)
        def _():
            line_slot(2, 0)
            for c in results.values():
                c.start()
            line_slot(0, 2)
            for n in range(nz):
                reduce_core(1, n)

        @pl.when(p == 1)
        def _():
            line_slot(3, 0)
            line_slot(1, 1)
            sum_part(0)
            for n in range(nz - 1):
                reduce_x(1, n)

        @pl.when(p == 2)
        def _():
            line_slot(1, 2)
            line_slot(2, 1)
            pass_part(0)

    partial = nt(dcat[pl.ds(there, rows), :], w_ref[:, 0:own_cols])
    send_dx[...] = partial.astype(BF)
    to_dx = remote(send_dx, got_dx, send_d, recv_d, partner)
    to_dx.start()
    dg_one = jnp.sum(partial * norm_of(pl.ds(there, rows))[0], axis=0, keepdims=True)
    partial = nt(dcat[pl.ds(base, rows), :], w_ref[:, 0:own_cols])
    own_gn[...] = partial
    dg_one = dg_one + jnp.sum(partial * norm_of(pl.ds(base, rows))[0], axis=0, keepdims=True)
    stacked = jnp.concatenate([dg_one, dg_two, jnp.zeros((126, width), F32)], axis=0).T
    lane = iota((1, 128), 1)
    small = jnp.where(lane < EXPERTS, d_route, 0.0)
    for i in range(2):
        small = jnp.where(lane == EXPERTS + i, stacked[:, i : i + 1], small)
    sums[:, own_cols:lead] = small.astype(BF)
    for n in range(nz):
        zone = pl.ds(pl.multiple_of(order[n] * shard, shard), shard)
        sums[zone, 0:own_cols] = nn(norm_t[zone, :], dcat[...]).astype(BF)
        for i in range(2):
            to_core(0, n, i).start()
    reduce_core(0, 0)
    for n in range(1, nz):
        reduce_core(0, n)
        if n == 1:
            line_slot(2, 2)
            sum_part(1)
        reduce_x(0, n - 1)
    line_slot(3, 1)
    last_part(0)
    pass_part(1)
    reduce_z(1, reduce_x(1, nz - 1))
    total_out = hidden_ref[...]
    for j in (OWN,) + AWAY:
        if j != OWN:
            results[j].wait_recv()
        pick = hot_cols(pick_col(places_ref[...], experts_of[j]), capacity)
        total_out = total_out + pick_col(probs_ref[...], experts_of[j]) * nn(pick, got_res[j])
    out_ref[...] = total_out.astype(BF)
    sum_part(2)
    line_slot(3, 2)
    reduce_z(0, reduce_x(0, nz - 1))
    to_f = remote(fin, got_f, send_f, recv_f, partner)
    to_f.start()
    to_dx.wait_recv()
    grad_n = own_gn[...] + got_dx[...].astype(F32)
    x_norm, r_one = norm_of(pl.ds(base, rows))
    u = grad_n * gain
    dx = gh[...] + r_one * (u - x_norm * jnp.mean(u * x_norm, axis=1, keepdims=True))
    dx_ref[...] = dx.astype(BF)
    last_part(1)
    pass_part(2)
    to_f.wait_recv()

    def spot(px, co):
        return pl.ds(pl.multiple_of((px * 2 + co) * part, part), part)

    here = spot(x, core)
    for i in range(3):
        cols = slice(i * half, (i + 1) * half)
        total[here, pl.ds(al(i * width + sq * half), half)] = fin[:, cols]
        total[here, pl.ds(al(i * width + (1 - sq) * half), half)] = got_f[:, cols]
    total[here, 3 * width :] = (fin[:, own_cols:].astype(F32) + got_f[:, own_cols:].astype(F32)).astype(BF)

    def pass_on(px, co, send, recv, peer):
        return remote(total.at[spot(px, co)], total.at[spot(px, co)], send, recv, peer)

    pass_on(x, core, send_a, recv_a, across).start()
    pass_on(x, core, send_b.at[0], recv_b.at[0], sibling).start()
    sum_part(3)
    last_part(2)
    pass_part(3)
    pass_on(1 - x, core, send_a, recv_a, across).wait_recv()
    pass_on(1 - x, core, send_b.at[1], recv_b.at[1], sibling).start()
    pass_on(x, 1 - core, send_b.at[0], recv_b.at[0], sibling).wait_recv()
    pass_on(1 - x, 1 - core, send_b.at[1], recv_b.at[1], sibling).wait_recv()
    din_out[...] = total[:, 0 : 3 * width].astype(F32)
    small = total[:, 3 * width : 3 * width + 128].astype(F32)
    droute_out[...] = small[:, 0:EXPERTS]
    dgains_out[...] = small[:, EXPERTS : EXPERTS + 2]
    dout_out[...] = total[:, 3 * width + 128 :].astype(F32)
    last_part(3)
    end_parts()
    for c in results.values():
        c.wait_send()
    pass_on(x, core, send_a, recv_a, across).wait_send()
    pass_on(x, core, send_b.at[0], recv_b.at[0], sibling).wait_send()
    pass_on(1 - x, core, send_b.at[1], recv_b.at[1], sibling).wait_send()
    to_f.wait_send()
    to_dx.wait_send()
    for g in range(2):
        for n in range(nz):
            for i in range(2):
                to_core(g, n, i).wait_send()
            to_x(g, n).wait_send()
            if n < nz - 1:
                to_z(g, n).wait_send()
    for p in range(pairs):
        give(p, base).wait_send()


def finish(
    xs, qkv, mixed, lse, whole, segments, hidden, probs, places, inner, gin, res, cot, attended, dw_half,
    prompt, nz, capacity, cid,
):
    rows, width = cot.shape
    pairs = width // 256
    cols = whole.shape[1]
    shard = width // nz
    part = shard // 4
    group = 2 * rows
    deep = dw_half.shape[1]
    quarter = (deep // PARTS, dw_half.shape[2])
    dma = pltpu.SemaphoreType.DMA
    two = lambda *shape: [dma(shape), dma(shape)]
    vm = pltpu.VMEM
    return pl.pallas_call(
        functools.partial(finish_kernel, prompt, nz, capacity),
        out_shape=(
            sds((rows, width), BF),
            sds((rows, width), BF),
            sds((shard, 3 * width), F32),
            sds((shard, width), F32),
            sds((shard, EXPERTS), F32),
            sds((shard, 2), F32),
            sds((PARTS, nz) + quarter, BF),
            sds((PARTS, nz) + quarter, BF),
            sds((2, 4) + dw_half.shape[1:], BF),
        ),
        in_specs=[VM] * 10 + [ANY] * 5,
        out_specs=(VM,) * 6 + (ANY,) * 3,
        scratch_shapes=[
            vm((rows, width), F32),
            vm((rows, width), BF),
            vm((4, capacity, width), BF),
            vm((pairs, group, 128), BF),
            vm((2, group, 128), BF),
            vm((2, group, 128), BF),
            vm((128, group), BF),
            vm((128, group), F32),
            vm((group, 3 * width // 2), BF),
            vm((width, group), BF),
            vm((width, cols), BF),
            vm((nz, 2, part, cols), BF),
            vm((nz, part, cols), BF),
            vm((nz - 1, part, cols), BF),
            vm((nz - 1, part, cols), BF),
            vm((part, cols), BF),
            vm((part, cols), BF),
            vm((shard, 4 * width + 128), BF),
            vm((rows, width), BF),
            vm((rows, width), BF),
            vm((rows, width), F32),
            vm((nz,) + quarter, BF),
            vm((PARTS,) + quarter, BF),
            vm((2, 3) + quarter, BF),
            dma((nz + PARTS,)),
        ]
        + two(4) + two(pairs) + two(2, nz, 2) + two(2, nz) + two(2, nz - 1) + two() + two() + two() + two(2)
        + two(PARTS, nz) + two(PARTS, nz) + two(PARTS) + two(PARTS, 2) + two(PARTS, 4),
        compiler_params=params(cid),
        name="finish",
    )(xs, qkv, mixed, lse, whole, segments, hidden, probs, places, inner, gin, res, cot, attended, dw_half)


def spread_kernel(in_ref, out_ref):
    rows, experts_, k = out_ref.shape
    flat = rows * experts_
    at, of = iota((flat, flat), 0), iota((flat, flat), 1)
    move = (of == lax.rem(at, experts_) * rows + at // experts_).astype(F32).astype(BF)
    out_ref[...] = nn(move, in_ref[...].reshape(flat, k)).reshape(rows, experts_, k)


def spread_experts(parts):
    cores, experts_, r, k = parts.shape
    block = r // 8
    return pl.pallas_call(
        spread_kernel,
        grid=(cores, 8),
        out_shape=sds((cores * r, experts_, k), F32),
        in_specs=[pl.BlockSpec((None, experts_, block, k), lambda c, i: (c, 0, i, 0))],
        out_specs=pl.BlockSpec((block, experts_, k), lambda c, i: (c * 8 + i, 0, 0)),
        compiler_params=params(),
        name="spread",
    )(parts)


def shards(tokens, attn_in, attn_out, router, gains, expert_w, expert_ids, segments, cotangent):
    x = tokens[0]
    cot = cotangent[0]
    rows, width = x.shape
    nz = lax.axis_size("fsdp")
    group = 2 * rows
    prompt = group - segments.shape[1]
    capacity = 2 * rows // EXPERTS
    dp, sq = lax.axis_index("dp"), lax.axis_index("seq")
    core = lax.rem(dp, 2)
    mine = (dp // 2) * 2 + sq

    part = expert_w.shape[0] // 2
    piece = lax.dynamic_slice(expert_w, (core * part, mine, 0), (part, 1, 2 * width))[:, 0]
    xs, whole, qkv, mixed, lse, attended, raw, places_row, places_col, near = begin(
        x, attn_in, attn_out, router, gains, segments, expert_ids[0], cot, piece, prompt, nz, capacity, 0
    )
    hidden, probs, gin, res, inner, dw_half = experts(
        x, attended, whole, places_row, places_col, raw, near, capacity, nz, 1
    )
    block_out, d_tokens, d_in, d_out, d_route, d_gains, _, _, dw_all = finish(
        xs, qkv, mixed, lse, whole, segments, hidden, probs, places_col, inner, gin, res, cot, attended, dw_half,
        prompt, nz, capacity, 2,
    )
    d_expert = spread_experts(dw_all)
    return (
        block_out[None],
        d_tokens[None],
        d_in,
        d_out,
        d_route,
        d_gains,
        d_expert,
    )


def route(choose, capacity, experts_count):
    pair_expert = choose.reshape(-1)
    one_hot = (pair_expert[:, None] == jnp.arange(experts_count, dtype=jnp.int32)[None, :]).astype(
        jnp.int32
    )
    before = jnp.cumsum(one_hot, axis=0) - one_hot
    place = jnp.sum(before * one_hot, axis=1)
    kept = place < capacity
    slots = jnp.where(kept, pair_expert * capacity + place, experts_count * capacity)
    pair_count = pair_expert.shape[0]
    pair_of = (
        jnp.zeros((experts_count * capacity + 1,), jnp.int32)
        .at[slots]
        .set(jnp.arange(pair_count, dtype=jnp.int32))
    )
    filled = (
        jnp.zeros((experts_count * capacity + 1,), jnp.int32)
        .at[slots]
        .set(jnp.ones((pair_count,), jnp.int32))
    )
    return (slots, kept, pair_of[:-1], filled[:-1] > 0)


def expert_pre(expert_in, piece):
    width = piece.shape[2] // 2
    return jnp.einsum(
        "ecd,fed->ecf", expert_in, piece[:, :, :width], preferred_element_type=jnp.float32
    )


def expert_out(activity, piece):
    width = piece.shape[2] // 2
    return jnp.einsum(
        "ecf,fed->ecd", activity, piece[:, :, width:], preferred_element_type=jnp.float32
    )


def expert_back(grad_result, pre_rows, piece):
    width = piece.shape[2] // 2
    grad_act = jnp.einsum(
        "ecd,fed->ecf", grad_result, piece[:, :, width:], preferred_element_type=jnp.float32
    )
    grad_pre = jax.vjp(jax.nn.gelu, pre_rows)[1](grad_act)[0].astype(jnp.bfloat16)
    grad_in = jnp.einsum(
        "ecf,fed->ecd", grad_pre, piece[:, :, :width], preferred_element_type=jnp.float32
    )
    return (grad_pre, grad_in)


def general_shards(tokens, attn_in, attn_out, router, gains, expert_w, expert_ids, segments, cotangent):
    x_rows = tokens[0].astype(jnp.float32)
    tok_rows = x_rows.shape[0]
    width = x_rows.shape[1]
    seq_count = lax.axis_size("seq")
    scale = HEAD_DIM ** (-0.5)
    w_qkv, w_proj, w_route, gain_pair = (
        lax.all_gather(attn_in, "fsdp", axis=0, tiled=True),
        lax.all_gather(attn_out, "fsdp", axis=0, tiled=True),
        lax.all_gather(router, "fsdp", axis=0, tiled=True),
        lax.all_gather(gains, "fsdp", axis=0, tiled=True),
    )
    gain_f = gain_pair.astype(jnp.float32)
    r_one = lax.rsqrt(jnp.mean(x_rows * x_rows, axis=-1, keepdims=True) + EPSILON)
    normed_one = x_rows * r_one
    normed_low = (normed_one * gain_f[:, 0]).astype(jnp.bfloat16)
    projected = jnp.dot(normed_low, w_qkv, preferred_element_type=jnp.float32).astype(jnp.bfloat16)
    local_heads = HEADS // seq_count
    head_cols = local_heads * HEAD_DIM
    arrived = lax.all_to_all(
        projected.reshape(tok_rows, 3, seq_count, head_cols),
        "seq",
        split_axis=2,
        concat_axis=0,
        tiled=True,
    )
    group_len = arrived.shape[0]
    queries = arrived[:, 0, 0].reshape(group_len, local_heads, HEAD_DIM)
    keys = arrived[:, 1, 0].reshape(group_len, local_heads, HEAD_DIM)
    values = arrived[:, 2, 0].reshape(group_len, local_heads, HEAD_DIM)
    seg_full = jnp.concatenate([jnp.full((PROMPT,), -1, jnp.int32), segments[0]])
    block = min(512, group_len)
    key_place = jnp.arange(group_len, dtype=jnp.int32)
    begins = jnp.arange(group_len // block, dtype=jnp.int32) * block

    def block_scores(begin):
        query_block = lax.dynamic_slice_in_dim(queries, begin, block, 0)
        query_place = begin + jnp.arange(block, dtype=jnp.int32)
        query_seg = lax.dynamic_slice_in_dim(seg_full, begin, block, 0)
        raw = (
            jnp.einsum("qhd,khd->hqk", query_block, keys, preferred_element_type=jnp.float32)
            * scale
        )
        allowed = (key_place[None, :] <= query_place[:, None]) & (
            (seg_full[None, :] < 0) | (seg_full[None, :] == query_seg[:, None])
        )
        return (jnp.where(allowed[None], raw, NEGATIVE), query_block)

    def forward_block(begin):
        masked, query_block = block_scores(begin)
        row_max = jnp.max(masked, axis=-1, keepdims=True)
        expo = jnp.exp(masked - row_max)
        row_total = jnp.sum(expo, axis=-1, keepdims=True)
        probs = expo / row_total
        mixed_block = jnp.einsum(
            "hqk,khd->qhd", probs.astype(jnp.bfloat16), values, preferred_element_type=jnp.float32
        )
        return (mixed_block.astype(jnp.bfloat16), (row_max + jnp.log(row_total))[:, :, 0])

    mixed_blocks, log_totals = lax.map(forward_block, begins)
    mixed_heads = mixed_blocks.reshape(group_len, 1, head_cols)
    returned = lax.all_to_all(mixed_heads, "seq", split_axis=0, concat_axis=1, tiled=True)
    attended = returned.reshape(tok_rows, width)
    hidden = x_rows + jnp.dot(attended, w_proj, preferred_element_type=jnp.float32)
    r_two = lax.rsqrt(jnp.mean(hidden * hidden, axis=-1, keepdims=True) + EPSILON)
    normed_two = hidden * r_two
    routed_low = (normed_two * gain_f[:, 1]).astype(jnp.bfloat16)
    logits = jnp.dot(routed_low, w_route, preferred_element_type=jnp.float32)
    probs_r = jax.nn.softmax(logits, axis=-1)
    choose = expert_ids[0]
    choose_map = (choose[:, :, None] == jnp.arange(EXPERTS, dtype=jnp.int32)[None, None, :]).astype(
        jnp.float32
    )
    gates = jnp.sum(probs_r[:, None, :] * choose_map, axis=-1)
    capacity = 2 * tok_rows // EXPERTS
    slots, kept, pair_of, filled = route(choose, capacity, EXPERTS)
    token_of = pair_of // 2
    expert_in = jnp.where(
        filled[:, None], routed_low[token_of], jnp.zeros((), jnp.bfloat16)
    ).reshape(EXPERTS, capacity, width)
    piece = lax.all_gather(expert_w, "fsdp", axis=0, tiled=True)
    pre_rows = expert_pre(expert_in, piece)
    result = expert_out(jax.nn.gelu(pre_rows).astype(jnp.bfloat16), piece)
    padded = jnp.concatenate(
        [result.reshape(EXPERTS * capacity, width), jnp.zeros((1, width), jnp.float32)], axis=0
    )
    picked = padded[slots].reshape(tok_rows, 2, width)
    kept_f = kept.astype(jnp.float32).reshape(tok_rows, 2)
    weight_pair = gates * kept_f
    block_out = hidden + jnp.sum(weight_pair[..., None] * picked, axis=1)
    grad_out_rows = cotangent[0].astype(jnp.float32)
    grad_gates = kept_f * jnp.sum(grad_out_rows[:, None, :] * picked, axis=-1)
    grad_probs = jnp.sum(grad_gates[:, :, None] * choose_map, axis=1)
    grad_logits = probs_r * (grad_probs - jnp.sum(probs_r * grad_probs, axis=-1, keepdims=True))
    grad_route_w = jnp.dot(routed_low.astype(jnp.float32).T, grad_logits, precision=HIGH)
    grad_routed = jnp.dot(grad_logits, w_route.astype(jnp.float32).T, precision=HIGH)
    scaled = (weight_pair[:, :, None] * grad_out_rows[:, None, :]).reshape(2 * tok_rows, width)
    grad_result = (
        jnp.where(filled[:, None], scaled[pair_of], 0.0)
        .astype(jnp.bfloat16)
        .reshape(EXPERTS, capacity, width)
    )
    piece = lax.all_gather(expert_w, "fsdp", axis=0, tiled=True)
    pre_rows = expert_pre(expert_in, piece)
    act_rows = jax.nn.gelu(pre_rows).astype(jnp.bfloat16)
    grad_pre_rows, grad_in_rows = expert_back(grad_result, pre_rows, piece)
    act_store = act_rows
    pre_rows = grad_pre_rows
    act_rows = act_store
    grad_first = jnp.einsum("ecd,ecf->fed", expert_in, pre_rows, preferred_element_type=jnp.float32)
    grad_second = jnp.einsum(
        "ecf,ecd->fed", act_rows, grad_result, preferred_element_type=jnp.float32
    )
    expert_shard = lax.psum_scatter(
        jnp.concatenate([grad_first, grad_second], axis=2).astype(jnp.bfloat16),
        "fsdp",
        scatter_dimension=0,
        tiled=True,
    )
    padded_in = jnp.concatenate(
        [grad_in_rows.reshape(EXPERTS * capacity, width), jnp.zeros((1, width), jnp.float32)],
        axis=0,
    )
    grad_routed = grad_routed + jnp.sum(padded_in[slots].reshape(tok_rows, 2, width), axis=1)
    grad_gain_two = jnp.sum(grad_routed * normed_two, axis=0)
    scaled_two = grad_routed * gain_f[:, 1]
    grad_hidden = grad_out_rows + r_two * (
        scaled_two - normed_two * jnp.mean(scaled_two * normed_two, axis=-1, keepdims=True)
    )
    hid_low = grad_hidden.astype(jnp.bfloat16)
    grad_proj_w = jnp.dot(attended.T, hid_low, preferred_element_type=jnp.float32)
    grad_attended = jnp.dot(hid_low, w_proj.T, preferred_element_type=jnp.float32).astype(
        jnp.bfloat16
    )
    grad_heads = lax.all_to_all(
        grad_attended.reshape(tok_rows, seq_count, head_cols),
        "seq",
        split_axis=1,
        concat_axis=0,
        tiled=True,
    )
    grad_mixed = grad_heads.reshape(group_len, local_heads, HEAD_DIM)

    def back_block(carry, inputs):
        begin, log_rows = inputs
        masked, query_block = block_scores(begin)
        probs = jnp.exp(masked - log_rows[:, :, None])
        grad_block = lax.dynamic_slice_in_dim(grad_mixed, begin, block, 0)
        grad_p = jnp.einsum("qhd,khd->hqk", grad_block, values, preferred_element_type=jnp.float32)
        inner = jnp.sum(probs * grad_p, axis=-1, keepdims=True)
        grad_scores = (probs * (grad_p - inner)).astype(jnp.bfloat16)
        grad_query = (
            jnp.einsum("hqk,khd->qhd", grad_scores, keys, preferred_element_type=jnp.float32)
            * scale
        )
        grad_key = (
            carry[0]
            + jnp.einsum(
                "hqk,qhd->khd", grad_scores, query_block, preferred_element_type=jnp.float32
            )
            * scale
        )
        grad_value = carry[1] + jnp.einsum(
            "hqk,qhd->khd",
            probs.astype(jnp.bfloat16),
            grad_block,
            preferred_element_type=jnp.float32,
        )
        return ((grad_key, grad_value), grad_query)

    zero_heads = jnp.zeros((group_len, local_heads, HEAD_DIM), jnp.float32)
    (grad_keys, grad_values), grad_queries = lax.scan(
        back_block, (zero_heads, zero_heads), (begins, log_totals)
    )
    stacked = jnp.stack(
        [
            grad_queries.reshape(group_len, head_cols),
            grad_keys.reshape(group_len, head_cols),
            grad_values.reshape(group_len, head_cols),
        ],
        axis=1,
    )
    stacked = stacked.astype(jnp.bfloat16).reshape(group_len, 3, 1, head_cols)
    grad_back = lax.all_to_all(stacked, "seq", split_axis=0, concat_axis=2, tiled=True)
    grad_proj_rows = grad_back.reshape(tok_rows, 3 * width)
    grad_qkv_w = jnp.dot(normed_low.T, grad_proj_rows, preferred_element_type=jnp.float32)
    grad_normed = jnp.dot(grad_proj_rows, w_qkv.T, preferred_element_type=jnp.float32)
    grad_gain_one = jnp.sum(grad_normed * normed_one, axis=0)
    scaled_one = grad_normed * gain_f[:, 0]
    grad_x = grad_hidden + r_one * (
        scaled_one - normed_one * jnp.mean(scaled_one * normed_one, axis=-1, keepdims=True)
    )
    grad_gains = jnp.stack([grad_gain_one, grad_gain_two], axis=1)
    shard_qkv, shard_proj, shard_route, shard_gains = (
        lax.psum_scatter(
            grad_qkv_w.astype(jnp.bfloat16), "fsdp", scatter_dimension=0, tiled=True
        ).astype(jnp.float32),
        lax.psum_scatter(
            grad_proj_w.astype(jnp.bfloat16), "fsdp", scatter_dimension=0, tiled=True
        ).astype(jnp.float32),
        lax.psum_scatter(
            grad_route_w.astype(jnp.bfloat16), "fsdp", scatter_dimension=0, tiled=True
        ).astype(jnp.float32),
        lax.psum_scatter(
            grad_gains.astype(jnp.bfloat16), "fsdp", scatter_dimension=0, tiled=True
        ).astype(jnp.float32),
    )
    part_qkv, part_proj, part_expert = (
        lax.psum_scatter(
            shard_qkv.astype(jnp.bfloat16), ("dp", "seq"), scatter_dimension=1, tiled=True
        ).astype(jnp.float32),
        lax.psum_scatter(
            shard_proj.astype(jnp.bfloat16), ("dp", "seq"), scatter_dimension=1, tiled=True
        ).astype(jnp.float32),
        lax.psum_scatter(expert_shard, ("dp", "seq"), scatter_dimension=2, tiled=True).astype(
            jnp.float32
        ),
    )
    summed_qkv, summed_proj, summed_expert = (
        lax.all_gather(part_qkv.astype(jnp.bfloat16), ("dp", "seq"), axis=1, tiled=True).astype(
            part_qkv.dtype
        ),
        lax.all_gather(part_proj.astype(jnp.bfloat16), ("dp", "seq"), axis=1, tiled=True).astype(
            part_proj.dtype
        ),
        lax.all_gather(part_expert.astype(jnp.bfloat16), ("dp", "seq"), axis=2, tiled=True).astype(
            part_expert.dtype
        ),
    )
    summed_route, summed_gains = lax.psum((shard_route, shard_gains), ("dp", "seq"))
    return (
        block_out.astype(jnp.bfloat16)[None],
        grad_x.astype(jnp.bfloat16)[None],
        summed_qkv,
        summed_proj,
        summed_route,
        summed_gains,
        summed_expert,
    )


def fits(mesh):
    return mesh.shape["fsdp"] == 4 and mesh.shape["dp"] == 4 and mesh.shape["seq"] == 2


def solution(mesh):
    body = shards if fits(mesh) else general_shards
    in_specs = (
        P(("dp", "fsdp"), "seq", None),
        P("fsdp", None),
        P("fsdp", None),
        P("fsdp", None),
        P("fsdp", None),
        P("fsdp", None, None),
        P(("dp", "fsdp"), "seq", None),
        P(("dp", "fsdp"), None),
        P(("dp", "fsdp"), "seq", None),
    )
    out_specs = (
        P(("dp", "fsdp"), "seq", None),
        P(("dp", "fsdp"), "seq", None),
        P("fsdp", None),
        P("fsdp", None),
        P("fsdp", None),
        P("fsdp", None),
        P("fsdp", None, None),
    )
    return jax.shard_map(body, mesh=mesh, in_specs=in_specs, out_specs=out_specs, check_vma=False)
```

```python
import functools

import jax
import jax.numpy as jnp
from jax import lax
from jax.experimental import pallas as pl
from jax.experimental.pallas import tpu as pltpu
from jax.sharding import PartitionSpec as P

HEADS = 12
HEAD_DIM = 64
EXPERTS = 4
PROMPT = 1024
EPSILON = 1e-06
NEGATIVE = -1e30
HIGH = lax.Precision.HIGHEST
LOG2E = 1.4426950408889634
BF = jnp.bfloat16
F32 = jnp.float32
MESH = pl.DeviceIdType.MESH
VMEM_LIMIT = 60 << 20
QB = 256
ANY = pl.BlockSpec(memory_space=pl.ANY)
VM = pl.BlockSpec(memory_space=pltpu.VMEM)


def nn(a, b):
    return lax.dot_general(a, b, (((1,), (0,)), ((), ())), preferred_element_type=F32)


def nt(a, b):
    return lax.dot_general(a, b, (((1,), (1,)), ((), ())), preferred_element_type=F32)


def tn(a, b):
    return lax.dot_general(a, b, (((0,), (0,)), ((), ())), preferred_element_type=F32)


def iota(shape, dim):
    return lax.broadcasted_iota(jnp.int32, shape, dim)


def params(cid=None):
    if cid is None:
        return pltpu.CompilerParams(vmem_limit_bytes=VMEM_LIMIT)
    return pltpu.CompilerParams(
        vmem_limit_bytes=VMEM_LIMIT, collective_id=cid, has_side_effects=True
    )


def sds(shape, dtype):
    return jax.ShapeDtypeStruct(shape, dtype)


def place():
    dp, sq, z = lax.axis_index("dp"), lax.axis_index("seq"), lax.axis_index("fsdp")
    return dp, sq, z, dp // 2, lax.rem(dp, 2)


def greet(peers):
    barrier = pltpu.get_barrier_semaphore()
    for peer in peers:
        pl.semaphore_signal(barrier, inc=1, device_id=peer, device_id_type=MESH)
    pl.semaphore_wait(barrier, len(peers))


def remote(src, dst, send, recv, peer):
    return pltpu.make_async_remote_copy(
        src_ref=src, dst_ref=dst, send_sem=send, recv_sem=recv, device_id=peer, device_id_type=MESH
    )


def al(x):
    return pl.multiple_of(x, 128)


def allowed_tile(j, i, prompt, seg_col, seg_row):
    mask = None
    if i == j:
        mask = iota((QB, QB), 0) <= iota((QB, QB), 1)
    if j * QB >= prompt:
        keys, queries = j * QB - prompt, i * QB - prompt
        same = seg_col[keys : keys + QB, :] == seg_row[:, queries : queries + QB]
        mask = same if mask is None else mask & same
    return mask


def flip_chip(x, sq, fx, fy):
    px = 1 - x if fx else x
    py = 1 - sq if fy else sq
    return px, py


SOURCES = ((1, 0), (0, 1), (0, 0), (1, 1))
OWN = 2
AWAY = (0, 1, 3)


class Line:
    def __init__(self, nz, dp, sq, z, sources, target, sems):
        self.nz, self.dp, self.sq, self.z = nz, dp, sq, z
        self.sources, self.target, self.sems = sources, target, sems

    def copy(self, stage, up):
        nz, z = self.nz, self.z
        zone = z - (stage - 1) if up else z + (stage - 1)
        zone = lax.rem(zone + nz, nz)
        to = lax.rem(z + 1, nz) if up else lax.rem(z + nz - 1, nz)
        i = stage - 1
        send, recv = (self.sems[0], self.sems[1]) if up else (self.sems[2], self.sems[3])
        return remote(
            self.sources(stage, zone), self.target.at[zone], send.at[i], recv.at[i], (self.dp, self.sq, to)
        )

    def arrival(self, stage, up):
        nz, z = self.nz, self.z
        zone = lax.rem((z - stage if up else z + stage) + nz, nz)
        to = lax.rem(z + 1, nz) if up else lax.rem(z + nz - 1, nz)
        i = stage - 1
        send, recv = (self.sems[0], self.sems[1]) if up else (self.sems[2], self.sems[3])
        return remote(
            self.sources(stage, zone), self.target.at[zone], send.at[i], recv.at[i], (self.dp, self.sq, to)
        )

    def sends(self, stage, up):
        z, nz = self.z, self.nz
        return (z < nz - 1) & (z >= stage - 1) if up else (z > 0) & (z <= nz - stage)

    def gets(self, stage, up):
        return self.z >= stage if up else self.z <= self.nz - 1 - stage

    def start(self, stage):
        for up in (True, False):

            @pl.when(self.sends(stage, up))
            def _(up=up):
                self.copy(stage, up).start()

    def wait_recv(self, stage):
        for up in (True, False):

            @pl.when(self.gets(stage, up))
            def _(up=up):
                self.arrival(stage, up).wait_recv()

    def wait_send(self, stage):
        for up in (True, False):

            @pl.when(self.sends(stage, up))
            def _(up=up):
                self.copy(stage, up).wait_send()


def eighth(x, prompt):
    row = x.astype(F32)
    col = jnp.broadcast_to(row, (128, row.shape[1])).T[:, 0:1]
    return row, col


def begin_kernel(
    prompt, nz, capacity, x_ref, in_ref, out_ref, router_ref, gains_ref, seg_ref, ids_ref, cot_ref, piece_ref,
    xs_ref, w_ref, qkv_ref, mixed_ref, lse_ref, att_ref, raw_ref, row_ref, col_ref, near_ref,
    pack, vt, local, send_t, recv_t, send_z, recv_z, send_p, recv_p, send_c, recv_c, send_o, recv_o, *line_sems,
):
    dp, sq, z, x, core = place()
    rows, width = x_ref.shape
    shard = in_ref.shape[0]
    part = shard // 4
    half = width // 2
    pairs = half // 128
    own_cols = 3 * half
    lead = own_cols + 128
    sibling = (x * 2 + 1 - core, sq, z)
    partner = (dp, 1 - sq, z)
    across = ((1 - x) * 2 + core, sq, z)
    others = [(dp, sq, lax.rem(z + d, nz)) for d in range(1, nz)]
    base = pl.multiple_of(sq * rows, rows)
    there = pl.multiple_of((1 - sq) * rows, rows)
    groups = (pl.ds(0, lead), pl.ds(lead, width))

    packs = [
        pltpu.make_async_copy(
            in_ref.at[:, pl.ds(al(i * width + sq * half + p * 128), 128)],
            pack.at[:, pl.ds((3 * p + i) * 128, 128)],
            local.at[3 * p + i],
        )
        for p in range(pairs)
        for i in range(3)
    ]
    packs.append(pltpu.make_async_copy(out_ref, pack.at[:, groups[1]], local.at[3 * pairs]))
    for c in packs:
        c.start()
    lane = iota((1, 128), 1)
    small = jnp.zeros((shard, 128), F32)
    for e in range(EXPERTS):
        small = jnp.where(lane == e, router_ref[:, e : e + 1].astype(F32), small)
    for e in range(2):
        small = jnp.where(lane == EXPERTS + e, gains_ref[:, e : e + 1].astype(F32), small)
    pack[:, own_cols:lead] = small.astype(BF)
    greet([sibling, partner, across] + others)
    tokens = remote(x_ref, xs_ref.at[pl.ds(base, rows)], send_t, recv_t, partner)
    tokens.start()
    for c in packs:
        c.wait()

    def at(zs, px, co, g):
        return w_ref.at[pl.ds(pl.multiple_of(zs * shard + (px * 2 + co) * part, part), part), groups[g]]

    def along(d, g):
        src = pack.at[pl.ds(pl.multiple_of((x * 2 + core) * part, part), part), groups[g]]
        return remote(src, at(z, x, core, g), send_z.at[d - 1, g], recv_z.at[d - 1, g], others[d - 1])

    def source(d):
        return lax.rem(z + nz - d, nz)

    def over(d, g, px):
        ref = at(source(d), px, core, g)
        return remote(ref, ref, send_p.at[d - 1, g], recv_p.at[d - 1, g], across)

    def beside(d, g, i, co):
        ref = at(source(d), (x, 1 - x)[i], co, g)
        return remote(ref, ref, send_c.at[d - 1, g, i], recv_c.at[d - 1, g, i], sibling)

    for d in range(1, nz):
        along(d, 0).start()
    own = pltpu.make_async_copy(pack, w_ref.at[pl.ds(pl.multiple_of(z * shard, shard), shard)], local.at[3 * pairs + 1])
    own.start()
    xs_ref[pl.ds(base, rows), :] = x_ref[...]
    ids = ids_ref[...]
    chosen = jnp.where((ids[:, 0:1] == lane) | (ids[:, 1:2] == lane), 1.0, 0.0)
    earlier = (iota((rows, rows), 1) < iota((rows, rows), 0)).astype(F32).astype(BF)
    places = jnp.where(chosen > 0, nn(earlier, chosen.astype(BF)), -1.0)
    col_ref[...] = places
    places = places.T[0:8, :]
    row_ref[...] = places

    def gather(g):
        for d in range(1, nz):
            along(d, g).wait_recv()
            over(d, g, x).start()
            beside(d, g, 0, core).start()
        if g == 0:
            line.start(1)
            for d in range(1, nz):
                along(d, 1).start()
        for d in range(1, nz):
            over(d, g, 1 - x).wait_recv()
            beside(d, g, 1, core).start()

    def gathered(g):
        for d in range(1, nz):
            for i in range(2):
                beside(d, g, i, 1 - core).wait_recv()

    stay = pltpu.make_async_copy(piece_ref, near_ref.at[z], local.at[3 * pairs + 2])
    stay.start()
    line = Line(
        nz, dp, sq, z, lambda stage, zone: piece_ref if stage == 1 else near_ref.at[zone], near_ref, line_sems
    )
    gather(0)
    gathered(0)
    own.wait()
    tokens.wait_recv()

    gain = w_ref[:, own_cols:lead].astype(F32).T[EXPERTS : EXPERTS + 1, :]
    xf = xs_ref[...].astype(F32)
    normed = (xf * lax.rsqrt(jnp.mean(xf * xf, axis=1, keepdims=True) + EPSILON) * gain).astype(BF)
    for p in range(pairs):
        got = nn(normed, w_ref[:, p * 384 : (p + 1) * 384]).astype(BF)
        for i in range(3):
            qkv_ref[p, i] = got[:, i * 128 : (i + 1) * 128]

    blocks = 2 * rows // QB
    const = HEAD_DIM ** (-0.5) * LOG2E
    seg_row, seg_col = eighth(seg_ref[...], prompt)

    def back(p, own_side):
        src = mixed_ref.at[p, pl.ds(there, rows)]
        side = sq if own_side else 1 - sq
        return remote(
            src, att_ref.at[:, pl.ds(al(side * half + p * 128), 128)], send_o.at[p], recv_o.at[p], partner
        )

    @pl.loop(0, pairs)
    def _(p):
        vt[0:128, :] = qkv_ref[p, 2].T
        vt[128:144, :] = jnp.ones((16, vt.shape[1]), BF)
        for i in range(blocks):
            here = slice(i * QB, (i + 1) * QB)
            both = []
            for h in range(2):
                lanes = iota((1, 128), 1) // HEAD_DIM == h
                q = jnp.where(lanes, qkv_ref[p, 0, here, :], jnp.zeros((), BF))
                tiles = []
                for j in range(i + 1):
                    s = nt(qkv_ref[p, 1, j * QB : (j + 1) * QB, :], q)
                    mask = allowed_tile(j, i, prompt, seg_col, seg_row)
                    if mask is not None:
                        s = jnp.where(mask, s, NEGATIVE)
                    tiles.append(s)
                top = functools.reduce(
                    jnp.maximum, [jnp.max(s, axis=0, keepdims=True) for s in tiles]
                )
                top = top * const
                acc = None
                for j, s in enumerate(tiles):
                    pr = jnp.exp2(s * const - top).astype(BF)
                    add = nn(vt[:, j * QB : (j + 1) * QB], pr)
                    acc = add if acc is None else acc + add
                total = acc[128:129, :]
                lse_ref[p, h : h + 1, here] = top + jnp.log2(total)
                low = h * HEAD_DIM
                both.append(acc[low : low + HEAD_DIM, :] * (1.0 / total))
            mixed_ref[p, here, :] = jnp.concatenate(both, axis=0).T.astype(BF)
        back(p, True).start()
        att_ref[:, pl.ds(al(sq * half + p * 128), 128)] = mixed_ref[p, pl.ds(base, rows), :]

        @pl.when(p == 0)
        def _():
            line.wait_recv(1)
            line.start(2)
            gather(1)

    for j, (px, py) in enumerate([flip_chip(x, sq, *f) for f in SOURCES]):
        hot = hot_rows(pick_row(row_ref[...], px * 2 + py), capacity)
        raw_ref[j] = nn(hot, cot_ref[...]).astype(BF)
    for p in range(pairs):
        back(p, False).wait_recv()
        back(p, True).wait_send()
    gathered(1)
    tokens.wait_send()
    for g in range(2):
        for d in range(1, nz):
            along(d, g).wait_send()
            over(d, g, x).wait_send()
            for i in range(2):
                beside(d, g, i, core).wait_send()
    line.wait_recv(2)
    line.wait_send(1)
    line.wait_send(2)
    stay.wait()


def begin(x, attn_in, attn_out, router, gains, segments, ids, cot, piece, prompt, nz, capacity, cid):
    rows, width = x.shape
    shard = attn_in.shape[0]
    pairs = width // 256
    cols = 3 * width // 2 + 128 + width
    dma = pltpu.SemaphoreType.DMA
    two = lambda *shape: [dma(shape), dma(shape)]
    return pl.pallas_call(
        functools.partial(begin_kernel, prompt, nz, capacity),
        out_shape=(
            sds((2 * rows, width), BF),
            sds((shard * nz, cols), BF),
            sds((pairs, 3, 2 * rows, 128), BF),
            sds((pairs, 2 * rows, 128), BF),
            sds((pairs, 8, 2 * rows), F32),
            sds((rows, width), BF),
            sds((4, capacity, width), BF),
            sds((8, rows), F32),
            sds((rows, 128), F32),
            sds((nz,) + piece.shape, BF),
        ),
        in_specs=[VM, ANY, ANY, VM, VM, VM, VM, VM, ANY],
        out_specs=(VM,) * 9 + (ANY,),
        scratch_shapes=[
            pltpu.VMEM((shard, cols), BF),
            pltpu.VMEM((144, 2 * rows), BF),
            dma((3 * pairs + 3,)),
        ]
        + two() + two(nz - 1, 2) + two(nz - 1, 2) + two(nz - 1, 2, 2) + two(pairs) + two(2) + two(2),
        compiler_params=params(cid),
        name="begin",
    )(x, attn_in, attn_out, router, gains, segments, ids, cot, piece)


def softmax_lanes(logits):
    live = iota(logits.shape, 1) < EXPERTS
    logits = jnp.where(live, logits, NEGATIVE)
    expo = jnp.where(live, jnp.exp(logits - jnp.max(logits, axis=1, keepdims=True)), 0.0)
    return expo / jnp.sum(expo, axis=1, keepdims=True)


def pick_row(table, e):
    return jnp.sum(jnp.where(iota((8, 1), 0) == e, table, 0.0), axis=0, keepdims=True)


def pick_col(table, e):
    return jnp.sum(jnp.where(iota((1, 128), 1) == e, table, 0.0), axis=1, keepdims=True)


def hot_rows(row, capacity):
    return (row == iota((capacity, 1), 0).astype(F32)).astype(F32).astype(BF)


def hot_cols(col, capacity):
    return (col == iota((1, capacity), 1).astype(F32)).astype(F32).astype(BF)


GELU_A = 0.7978845608028654
GELU_B = GELU_A * 0.044715


def expert_step(x, g, w):
    width = x.shape[1]
    first, second = w[:, :width], w[:, width:]
    pre = nt(x, first)
    back = nt(g, second)
    square = pre * pre
    t = jnp.tanh(pre * (GELU_A + GELU_B * square))
    rise = 0.5 + 0.5 * t
    act = (pre * rise).astype(BF)
    slope = rise + (0.5 * pre) * (1.0 - t * t) * (GELU_A + (3.0 * GELU_B) * square)
    grad_pre = (back * slope).astype(BF)
    return nn(act, second), nn(grad_pre, first), tn(grad_pre, x), tn(act, g)


def experts_kernel(
    capacity, nz, x_ref, att_ref, w_hbm, places_row, places_col, raw_send, near_ref,
    hidden_ref, probs_ref, back_gin, out_res, back_dot, dw_ref,
    wp, send_in, got_in, send_gate, got_gate, own_w, theirs, grad, res_acc, gin_acc, out_gin, out_dot, dw_away, dw_got,
    raw_ref, local, send_x, recv_x, send_w, recv_w, send_i, recv_i, send_t, recv_t, send_r, recv_r, send_d, recv_d, send_v, recv_v, *line_sems,
):
    dp, sq, z, x, core = place()
    rows, width = x_ref.shape
    sibling = (x * 2 + 1 - core, sq, z)
    corner = [flip_chip(x, sq, *f) for f in SOURCES]
    plane = [(px * 2 + core, py, z) for px, py in corner]
    experts_of = [px * 2 + py for px, py in corner]
    beside_z = (dp, sq, z + 1 - 2 * lax.rem(z, 2))
    shift = jnp.where(z >= nz // 2, 1, 0)
    far_zone = jnp.where(z >= nz // 2, 0, nz - 1)
    at_end = (z == 0) | (z == nz - 1)
    near_peers = [sibling] + [plane[j] for j in AWAY]
    barrier = pltpu.get_barrier_semaphore()
    for peer in near_peers:
        pl.semaphore_signal(barrier, inc=1, device_id=peer, device_id_type=MESH)

    @pl.when(at_end)
    def _():
        pl.semaphore_signal(barrier, inc=1, device_id=beside_z, device_id_type=MESH)

    pl.semaphore_wait(barrier, len(near_peers) + jnp.where(at_end, 0, 1))
    line = Line(nz, dp, sq, z, lambda stage, zone: near_ref.at[zone], own_w, line_sems)
    line.start(nz - 1)

    def go_raw(j):
        return remote(raw_send.at[j], raw_ref.at[j], send_x.at[j], recv_x.at[j], plane[j])

    go_raw(0).start()
    go_raw(1).start()

    def weights(slot):
        if slot == nz - 1:
            return remote(own_w.at[far_zone], theirs.at[far_zone], send_w.at[slot], recv_w.at[slot], sibling)
        zone = slot + shift
        return remote(near_ref.at[zone], theirs.at[zone], send_w.at[slot], recv_w.at[slot], sibling)

    lifts = []
    for i in range(nz - 1):
        weights(i).start()
        lifts.append(pltpu.make_async_copy(near_ref.at[i + shift], own_w.at[i + shift], local.at[2 + i]))
    for c in lifts:
        c.start()
    far_lift = pltpu.make_async_copy(near_ref.at[far_zone], own_w.at[far_zone], local.at[1 + nz])

    @pl.when(jnp.logical_not(at_end))
    def _():
        far_lift.start()

    own_raw = pltpu.make_async_copy(raw_send.at[OWN], raw_ref.at[OWN], local.at[1])
    own_raw.start()
    load = pltpu.make_async_copy(w_hbm.at[:, 3 * width // 2 :], wp, local.at[0])
    load.start()
    load.wait()

    hidden = x_ref[...].astype(F32) + nn(att_ref[...], wp[:, 128:])
    hidden_ref[...] = hidden
    r_two = lax.rsqrt(jnp.mean(hidden * hidden, axis=1, keepdims=True) + EPSILON)
    small = wp[:, :128]
    gain = small.astype(F32).T[EXPERTS + 1 : EXPERTS + 2, :]
    routed = (hidden * r_two * gain).astype(BF)
    probs = softmax_lanes(nn(routed, small))
    probs_ref[...] = probs
    flat = probs.T[0:8, :]
    high = flat.astype(BF)
    rest = flat - high.astype(F32)
    mid = rest.astype(BF)
    low = (rest - mid.astype(F32)).astype(BF)
    split = jnp.concatenate([high.astype(F32), mid.astype(F32), low.astype(F32)], axis=0).astype(BF)

    def go_in(j):
        return remote(send_in.at[j], got_in.at[j], send_i.at[j], recv_i.at[j], plane[j])

    def go_gate(j):
        return remote(send_gate.at[j], got_gate.at[j], send_t.at[j], recv_t.at[j], plane[j])

    for j in range(4):
        e = experts_of[j]
        taken = nn(hot_rows(pick_row(places_row[...], e), capacity), routed).astype(BF)
        three = nn(split, hot_cols(pick_col(places_col[...], e), capacity))
        gate = three[0:8] + three[8:16] + three[16:24]
        gate = jnp.broadcast_to(pick_row(gate, e), gate.shape)
        if j != OWN:
            send_in[j] = taken
            send_gate[j] = gate
            go_gate(j).start()
        if j < OWN:
            go_in(j).start()
        if j == OWN:
            got_in[j] = taken
            got_gate[j] = gate
    own_raw.wait()
    for c in lifts:
        c.wait()
    for i in range(nz - 1):
        weights(i).wait_recv()

    def go_gin(j):
        return remote(out_gin.at[j], back_gin.at[j], send_r.at[j], recv_r.at[j], plane[j])

    def go_dot(j):
        return remote(out_dot.at[j], back_dot.at[j], send_d.at[j], recv_d.at[j], plane[j])

    def go_dw(n):
        return remote(dw_away.at[n], dw_got.at[n], send_v.at[n], recv_v.at[n], sibling)

    def arrive(lo, hi):
        for j in range(lo, hi):
            if j != OWN:
                go_raw(j).wait_recv()
                go_in(j).wait_recv()
                go_gate(j).wait_recv()
            gate = got_gate[j].T[:, 0:1]
            grad[j] = (raw_ref[j].astype(F32) * gate).astype(BF)

    def chunk(lo, hi, w_ref, dw, d, first, at):
        count = (hi - lo) * capacity
        xs = got_in[lo:hi].reshape(count, width)
        gs = grad[lo:hi].reshape(count, width)
        res, gin, d_first, d_second = expert_step(xs, gs, w_ref[d])
        here = slice(at * capacity, at * capacity + count)
        res_acc[here, :] += res
        gin_acc[here, :] += gin
        if first:
            dw[d, :, :width] = d_first.astype(BF)
            dw[d, :, width:] = d_second.astype(BF)
        else:
            dw[d, :, :width] = (dw[d, :, :width].astype(F32) + d_first).astype(BF)
            dw[d, :, width:] = (dw[d, :, width:].astype(F32) + d_second).astype(BF)

    def send_back(lo, hi, at):
        for j in range(lo, hi):
            here = slice((at + j - lo) * capacity, (at + j - lo + 1) * capacity)
            prod = res_acc[here, :] * raw_ref[j].astype(F32)
            narrow = functools.reduce(jnp.add, [prod[:, i : i + 128] for i in range(0, width, 128)])
            inner = jnp.broadcast_to(jnp.sum(narrow.T, axis=0, keepdims=True), (8, capacity))
            if j != OWN:
                out_gin[j] = gin_acc[here, :].astype(BF)
                out_dot[j] = inner
                go_gin(j).start()
                go_dot(j).start()
            else:
                back_gin[j] = gin_acc[here, :].astype(BF)
                back_dot[j] = inner
        for j in range(lo, hi):
            here = slice((at + j - lo) * capacity, (at + j - lo + 1) * capacity)
            out_res[j] = res_acc[here, :].astype(BF)

    both = ((theirs, dw_away), (own_w, dw_ref))
    res_acc[...] = jnp.zeros(res_acc.shape, F32)
    gin_acc[...] = jnp.zeros(gin_acc.shape, F32)
    arrive(OWN, OWN + 1)
    for w_ref, dw in both:

        @pl.loop(0, nz - 1)
        def _(i):
            chunk(OWN, OWN + 1, w_ref, dw, i + shift, True, OWN)

    arrive(0, OWN)
    go_raw(3).start()
    go_in(3).start()
    for w_ref, dw in both:

        @pl.loop(0, nz - 1)
        def _(i):
            chunk(0, OWN, w_ref, dw, i + shift, False, 0)

    @pl.when(jnp.logical_not(at_end))
    def _():
        far_lift.wait()

    line.wait_recv(nz - 1)
    weights(nz - 1).start()
    chunk(0, OWN + 1, own_w, dw_ref, far_zone, True, 0)
    weights(nz - 1).wait_recv()
    chunk(0, OWN + 1, theirs, dw_away, far_zone, True, 0)
    send_back(0, OWN + 1, 0)
    arrive(3, 4)
    res_acc[0:capacity, :] = jnp.zeros((capacity, width), F32)
    gin_acc[0:capacity, :] = jnp.zeros((capacity, width), F32)

    @pl.loop(0, nz)
    def _(d):
        chunk(3, 4, theirs, dw_away, d, False, 0)
        go_dw(d).start()

    @pl.loop(0, nz)
    def _(d):
        chunk(3, 4, own_w, dw_ref, d, False, 0)

    send_back(3, 4, 0)
    for n in range(nz):
        go_dw(n).wait_recv()
        dw_ref[n] = (dw_ref[n].astype(F32) + dw_got[n].astype(F32)).astype(BF)
    for j in AWAY:
        go_gin(j).wait_recv()
        go_dot(j).wait_recv()
    line.wait_send(nz - 1)
    for n in range(nz):
        weights(n).wait_send()
        go_dw(n).wait_send()
    for j in AWAY:
        for c in (go_raw(j), go_in(j), go_gate(j), go_gin(j), go_dot(j)):
            c.wait_send()


def experts(x, attended, whole, places_row, places_col, raw, near, capacity, nz, cid):
    rows, width = x.shape
    part = near.shape[1]
    slots = sds((4, capacity, width), BF)
    small = sds((4, 8, capacity), F32)
    dma = pltpu.SemaphoreType.DMA
    two = lambda *shape: [dma(shape), dma(shape)]
    vm = pltpu.VMEM
    return pl.pallas_call(
        functools.partial(experts_kernel, capacity, nz),
        out_shape=(
            sds((rows, width), F32),
            sds((rows, 128), F32),
            slots,
            slots,
            small,
            sds((nz, part, 2 * width), BF),
        ),
        in_specs=[VM, VM, ANY, VM, VM, ANY, ANY],
        out_specs=(VM,) * 6,
        scratch_shapes=[
            vm((rows, width + 128), BF),
            vm((4, capacity, width), BF),
            vm((4, capacity, width), BF),
            vm((4, 8, capacity), F32),
            vm((4, 8, capacity), F32),
            vm((nz, part, 2 * width), BF),
            vm((nz, part, 2 * width), BF),
            vm((4, capacity, width), BF),
            vm((3 * capacity, width), F32),
            vm((3 * capacity, width), F32),
            vm((4, capacity, width), BF),
            vm((4, 8, capacity), F32),
            vm((nz, part, 2 * width), BF),
            vm((nz, part, 2 * width), BF),
            vm((4, capacity, width), BF),
            dma((2 + nz,)),
        ]
        + two(4) + two(nz) + two(4) + two(4) + two(4) + two(4) + two(nz) + two(nz - 1) + two(nz - 1),
        compiler_params=params(cid),
        name="experts",
    )(x, attended, whole, places_row, places_col, raw, near)


PARTS = 4


def finish_kernel(
    prompt, nz, capacity, xs_ref, qkv_ref, mixed_ref, lse_ref, w_ref, seg_ref, hidden_ref, probs_ref, places_ref,
    dot_ref, gin_ref, res_ref, cot_ref, att_ref, part_ref,
    out_ref, dx_ref, din_out, dout_out, droute_out, dgains_out, got_up, got_down, dw_all,
    gh, gatt, got_res, grad, qm, dom, kt, dqt, dcat, norm_t, sums, got_c, got_x, got_z, mine, fin, got_f, total,
    send_dx, got_dx, own_gn, stage, dw_sum, ahead,
    local, send_r, recv_r, send_g, recv_g, send_c, recv_c, send_x, recv_x, send_z, recv_z, send_d, recv_d, send_f, recv_f,
    send_a, recv_a, send_b, recv_b, send_u, recv_u, send_l, recv_l, send_v, recv_v, send_h, recv_h, send_k, recv_k,
):
    dp, sq, z, x, core = place()
    rows, width = gatt.shape
    half = width // 2
    pairs = half // 128
    shard = width // nz
    part = shard // 4
    own_cols = 3 * half
    lead = own_cols + 128
    chip = x * 2 + sq
    chip_x, chip_y, chip_d = (1 - x) * 2 + sq, x * 2 + 1 - sq, (1 - x) * 2 + 1 - sq
    sibling = (x * 2 + 1 - core, sq, z)
    partner = (dp, 1 - sq, z)
    across = ((1 - x) * 2 + core, sq, z)
    others = [(dp, sq, lax.rem(z + d, nz)) for d in range(1, nz)]
    base = pl.multiple_of(sq * rows, rows)
    there = pl.multiple_of((1 - sq) * rows, rows)
    corner = [flip_chip(x, sq, *f) for f in SOURCES]
    plane = [(px * 2 + core, py, z) for px, py in corner]
    experts_of = [px * 2 + py for px, py in corner]
    greet([sibling] + [plane[j] for j in AWAY] + others)

    quarter = stage.shape[1]

    def rows_of(k):
        return pl.ds(k * quarter, quarter)

    def hop(k, t, up, src):
        to = lax.rem(z + 1, nz) if up else lax.rem(z + nz - 1, nz)
        got, send, recv = (got_up, send_u, recv_u) if up else (got_down, send_l, recv_l)
        return remote(src, got.at[k, t], send.at[k, t], recv.at[k, t], (dp, sq, to))

    def legs(slot):
        ups = (True, slot, list(range(nz - 1, slot, -1)))
        downs = (False, nz - 1 - slot, list(range(0, nz - 1 - slot)))
        return ups, downs

    def line_slot(k, slot):
        for up, sender, zones in legs(slot):

            @pl.when(z == sender)
            def _(up=up, zones=zones):
                if slot == 0:
                    for t in zones:
                        hop(k, t, up, part_ref.at[t, rows_of(k)]).start()
                    return
                got = got_up if up else got_down
                loads = []
                for i, t in enumerate(zones):
                    hop(k, t, up, ahead.at[k % 2, 0]).wait_recv()
                    loads.append(pltpu.make_async_copy(got.at[k, t], stage.at[2 * i], local.at[2 * i]))
                    loads.append(pltpu.make_async_copy(part_ref.at[t, rows_of(k)], stage.at[2 * i + 1], local.at[2 * i + 1]))
                for c in loads:
                    c.start()
                for i, t in enumerate(zones):
                    to = ahead.at[k % 2, i if slot == 1 else 2]
                    if k > 1:
                        hop(k - 2, t, up, to).wait_send()
                    loads[2 * i].wait()
                    loads[2 * i + 1].wait()
                    to[...] = (stage[2 * i].astype(F32) + stage[2 * i + 1].astype(F32)).astype(BF)
                    hop(k, t, up, to).start()

    def line_end():
        for slot in range(nz - 1):
            for up, sender, zones in legs(slot):

                @pl.when(z == sender)
                def _(up=up, zones=zones, slot=slot):
                    for k in range(PARTS) if slot == 0 else range(PARTS - 2, PARTS):
                        for i, t in enumerate(zones):
                            src = part_ref.at[t, rows_of(k)] if slot == 0 else ahead.at[k % 2, i if slot == 1 else 2]
                            hop(k, t, up, src).wait_send()

    def share(k, ch, send, recv, peer, own=False):
        at = dw_all.at[core, ch, pl.ds(k * quarter, quarter)]
        return remote(dw_sum.at[k] if own else at, at, send, recv, peer)

    def keep(k):
        return pltpu.make_async_copy(
            dw_sum.at[k], dw_all.at[core, chip, pl.ds(k * quarter, quarter)], local.at[nz + k]
        )

    def sum_part(k):
        own = pltpu.make_async_copy(part_ref.at[z, rows_of(k)], stage.at[2], local.at[2])
        own.start()
        for i, up in enumerate((True, False)):
            got = got_up if up else got_down
            has = z > 0 if up else z < nz - 1

            @pl.when(has)
            def _(i=i, up=up, got=got):
                hop(k, z, up, ahead.at[0, 0]).wait_recv()
                c = pltpu.make_async_copy(got.at[k, z], stage.at[i], local.at[i])
                c.start()
                c.wait()

            @pl.when(jnp.logical_not(has))
            def _(i=i):
                stage[i] = jnp.zeros(stage.shape[1:], BF)

        own.wait()
        dw_sum[k] = (stage[0].astype(F32) + stage[1].astype(F32) + stage[2].astype(F32)).astype(BF)
        share(k, chip, send_v.at[k], recv_v.at[k], partner, True).start()
        share(k, chip, send_h.at[k, 0], recv_h.at[k, 0], across, True).start()
        share(k, chip, send_k.at[k, 0], recv_k.at[k, 0], sibling, True).start()
        keep(k).start()

    def pass_part(k):
        share(k, chip_y, send_v.at[k], recv_v.at[k], partner).wait_recv()
        share(k, chip_y, send_h.at[k, 1], recv_h.at[k, 1], across).start()
        share(k, chip_y, send_k.at[k, 1], recv_k.at[k, 1], sibling).start()

    def last_part(k):
        share(k, chip_x, send_h.at[k, 0], recv_h.at[k, 0], across).wait_recv()
        share(k, chip_x, send_k.at[k, 2], recv_k.at[k, 2], sibling).start()
        share(k, chip_d, send_h.at[k, 1], recv_h.at[k, 1], across).wait_recv()
        share(k, chip_d, send_k.at[k, 3], recv_k.at[k, 3], sibling).start()

    others_of = [chip, chip_y, chip_x, chip_d]

    def end_parts():
        for k in range(PARTS):
            for i in range(4):
                at = dw_all.at[1 - core, others_of[i], rows_of(k)]
                remote(at, at, send_k.at[k, i], recv_k.at[k, i], sibling).wait_recv()
                share(k, others_of[i], send_k.at[k, i], recv_k.at[k, i], sibling, i == 0).wait_send()
            share(k, chip, send_v.at[k], recv_v.at[k], partner, True).wait_send()
            share(k, chip, send_h.at[k, 0], recv_h.at[k, 0], across, True).wait_send()
            share(k, chip_y, send_h.at[k, 1], recv_h.at[k, 1], across).wait_send()
            keep(k).wait()
        line_end()

    spans = [((pairs - 1) * 384, lead), (lead, lead + width)] + [(p * 384, (p + 1) * 384) for p in range(pairs - 1)]
    groups = [pl.ds(lo, hi - lo) for lo, hi in spans]
    order = [lax.rem(z + d, nz) for d in range(1, nz + 1)]

    def piece(zz, px, co):
        return pl.ds(pl.multiple_of(zz * shard + (px * 2 + co) * part, part), part)

    def to_core(g, n, i):
        src = sums.at[piece(order[n], (1 - x, x)[i], 1 - core), groups[g]]
        return remote(src, got_c.at[n, i, :, groups[g]], send_c.at[g, n, i], recv_c.at[g, n, i], sibling)

    def to_x(g, n):
        src = sums.at[piece(order[n], 1 - x, core), groups[g]]
        return remote(src, got_x.at[n, :, groups[g]], send_x.at[g, n], recv_x.at[g, n], across)

    def to_z(g, n):
        return remote(
            mine.at[n, :, groups[g]], got_z.at[n, :, groups[g]], send_z.at[g, n], recv_z.at[g, n], others[n]
        )

    def cols_of(g):
        return slice(*spans[g])

    def reduce_core(g, n):
        cols = cols_of(g)
        for i in range(2):
            to_core(g, n, i).wait_recv()
            at = piece(order[n], (1 - x, x)[i], core)
            sums[at, cols] = (sums[at, cols].astype(F32) + got_c[n, i, :, cols].astype(F32)).astype(BF)
            if i == 0:
                to_x(g, n).start()

    def reduce_x(g, n):
        cols = cols_of(g)
        to_x(g, n).wait_recv()
        acc = sums[piece(order[n], x, core), cols].astype(F32) + got_x[n, :, cols].astype(F32)
        if n < nz - 1:
            mine[n, :, cols] = acc.astype(BF)
            to_z(g, n).start()
        return acc

    def reduce_z(g, acc):
        cols = cols_of(g)
        for n in range(nz - 1):
            to_z(g, n).wait_recv()
            acc = acc + got_z[n, :, cols].astype(F32)
        fin[:, cols] = acc.astype(BF)

    line_slot(0, 0)
    fetch = [pltpu.make_async_copy(gin_ref.at[j], dcat.at[pl.ds(j * capacity, capacity), 0:width], local.at[j]) for j in range(4)]
    fetch.append(pltpu.make_async_copy(cot_ref, send_dx, local.at[4]))
    fetch.append(pltpu.make_async_copy(att_ref, norm_t.at[:, 0:rows], local.at[5]))
    fetch.append(pltpu.make_async_copy(res_ref.at[OWN], got_res.at[OWN], local.at[6]))
    for c in fetch:
        c.start()
    results = {j: remote(res_ref.at[j], got_res.at[j], send_r.at[j], recv_r.at[j], plane[j]) for j in AWAY}
    for j in range(OWN):
        results[j].start()
    for c in fetch:
        c.wait()
    hidden = hidden_ref[...]
    probs = probs_ref[...]
    small = w_ref[:, own_cols:lead]
    gain_two = small.astype(F32).T[EXPERTS + 1 : EXPERTS + 2, :]
    lane = iota(probs.shape, 1)
    back = None
    grad_probs = jnp.zeros_like(probs)
    for j in range(4):
        pick = hot_cols(pick_col(places_ref[...], experts_of[j]), capacity)
        add = nn(pick, dcat[j * capacity : (j + 1) * capacity, 0:width])
        back = add if back is None else back + add
        inner = jnp.sum(pick.astype(F32) * dot_ref[j][0:1, :], axis=1, keepdims=True)
        grad_probs = jnp.where(lane == experts_of[j], inner, grad_probs)
    mixed = jnp.sum(probs * grad_probs, axis=1, keepdims=True)
    low = (probs * (grad_probs - mixed)).astype(BF)
    r_two = lax.rsqrt(jnp.mean(hidden * hidden, axis=1, keepdims=True) + EPSILON)
    h_norm = hidden * r_two
    routed = (h_norm * gain_two).astype(BF)
    grad_routed = back + nt(low, small)
    dg_two = jnp.sum(grad_routed * h_norm, axis=0, keepdims=True)
    u = grad_routed * gain_two
    grad_hidden = send_dx[...].astype(F32) + r_two * (
        u - h_norm * jnp.mean(u * h_norm, axis=1, keepdims=True)
    )
    gh[...] = grad_hidden
    hid_low = grad_hidden.astype(BF)
    gatt[...] = nt(hid_low, w_ref[:, lead:]).astype(BF)

    def give(p, to):
        return remote(
            gatt.at[:, pl.ds(al((1 - sq) * half + p * 128), 128)],
            grad.at[p, pl.ds(to, rows)],
            send_g.at[p],
            recv_g.at[p],
            partner,
        )

    for p in range(pairs):
        give(p, base).start()
    line_slot(1, 0)
    for p in range(pairs):
        grad[p, pl.ds(base, rows), :] = gatt[:, pl.ds(al(sq * half + p * 128), 128)]
    d_route = tn(routed, low)
    sums[:, cols_of(1)] = tn(norm_t[:, 0:rows], hid_low).astype(BF)
    for n in range(nz):
        for i in range(2):
            to_core(1, n, i).start()
    seg_row, seg_col = eighth(seg_ref[...], prompt)
    gain = w_ref[:, own_cols:lead].astype(F32).T[EXPERTS : EXPERTS + 1, :]

    def norm_of(at):
        xf = xs_ref[at, :].astype(F32)
        r_one = lax.rsqrt(jnp.mean(xf * xf, axis=1, keepdims=True) + EPSILON)
        return xf * r_one, r_one

    for i in range(2):
        at = slice(i * rows, (i + 1) * rows)
        norm_t[:, at] = (norm_of(at)[0] * gain).astype(BF).T

    line_slot(0, 1)
    def weight_grad(g, p):
        cols = slice(p * 384, (p + 1) * 384)
        for n in range(nz):
            zone = pl.ds(pl.multiple_of(order[n] * shard, shard), shard)
            sums[zone, cols] = nn(norm_t[zone, :], dcat[:, cols]).astype(BF)
            for i in range(2):
                to_core(g, n, i).start()

    blocks = 2 * rows // QB
    scale = HEAD_DIM ** (-0.5)
    zero = jnp.zeros((), BF)

    @pl.loop(0, pairs)
    def _(p):
        give(p, there).wait_recv()
        kt[...] = qkv_ref[p, 1].T
        prod = (grad[p].astype(F32) * mixed_ref[p].astype(F32)).T
        delta = []
        for h in range(2):
            lanes = iota((1, 128), 1) // HEAD_DIM == h
            qm[h] = jnp.where(lanes, qkv_ref[p, 0], zero) * jnp.asarray(scale, BF)
            dom[h] = jnp.where(lanes, grad[p], zero)
            low = h * HEAD_DIM
            delta.append(jnp.sum(prod[low : low + HEAD_DIM, :], axis=0, keepdims=True))
        for j in range(blocks):
            keys = slice(j * QB, (j + 1) * QB)
            k, v = qkv_ref[p, 1, keys, :], qkv_ref[p, 2, keys, :]
            dk = dv = None
            for i in range(j, blocks):
                at = slice(i * QB, (i + 1) * QB)
                mask = allowed_tile(j, i, prompt, seg_col, seg_row)
                for h in range(2):
                    s = nt(k, qm[h, at, :])
                    dpr = nt(v, dom[h, at, :])
                    pr = jnp.exp2(s * LOG2E - lse_ref[p, h : h + 1, at])
                    if mask is not None:
                        pr = jnp.where(mask, pr, 0.0)
                    ds = (pr * (dpr - delta[h][:, at])).astype(BF)
                    a = nn(pr.astype(BF), dom[h, at, :])
                    b = nn(ds, qm[h, at, :])
                    c = nn(kt[h * HEAD_DIM : (h + 1) * HEAD_DIM, keys], ds)
                    dv = a if dv is None else dv + a
                    dk = b if dk is None else dk + b
                    to = slice(h * HEAD_DIM, (h + 1) * HEAD_DIM)
                    dqt[to, at] = c if j == 0 else dqt[to, at] + c
            dcat[keys, pl.ds(al(p * 384 + 128), 128)] = dk.astype(BF)
            dcat[keys, pl.ds(al(p * 384 + 256), 128)] = dv.astype(BF)
        dcat[:, pl.ds(al(p * 384), 128)] = (dqt[...] * scale).T.astype(BF)

        @pl.when(p == 0)
        def _():
            weight_grad(2, 0)
            line_slot(2, 0)
            results[3].start()
            line_slot(0, 2)
            for n in range(nz):
                reduce_core(1, n)

        @pl.when(p == 1)
        def _():
            weight_grad(3, 1)
            line_slot(3, 0)
            line_slot(1, 1)
            sum_part(0)
            for n in range(nz - 1):
                reduce_x(1, n)
            for n in range(nz):
                reduce_core(2, n)

        @pl.when(p == 2)
        def _():
            line_slot(1, 2)
            line_slot(2, 1)
            pass_part(0)
            for n in range(nz):
                reduce_core(3, n)
            for n in range(nz - 1):
                reduce_x(2, n)

    partial = nt(dcat[pl.ds(there, rows), :], w_ref[:, 0:own_cols])
    send_dx[...] = partial.astype(BF)
    to_dx = remote(send_dx, got_dx, send_d, recv_d, partner)
    to_dx.start()
    dg_one = jnp.sum(partial * norm_of(pl.ds(there, rows))[0], axis=0, keepdims=True)
    partial = nt(dcat[pl.ds(base, rows), :], w_ref[:, 0:own_cols])
    own_gn[...] = partial
    dg_one = dg_one + jnp.sum(partial * norm_of(pl.ds(base, rows))[0], axis=0, keepdims=True)
    stacked = jnp.concatenate([dg_one, dg_two, jnp.zeros((126, width), F32)], axis=0).T
    lane = iota((1, 128), 1)
    small = jnp.where(lane < EXPERTS, d_route, 0.0)
    for i in range(2):
        small = jnp.where(lane == EXPERTS + i, stacked[:, i : i + 1], small)
    sums[:, own_cols:lead] = small.astype(BF)
    weight_grad(0, pairs - 1)
    reduce_core(0, 0)
    for n in range(1, nz):
        reduce_core(0, n)
        if n == 1:
            line_slot(2, 2)
            sum_part(1)
        reduce_x(0, n - 1)
    for n in range(nz - 1):
        reduce_x(3, n)
    line_slot(3, 1)
    last_part(0)
    pass_part(1)
    for g in (1, 2):
        reduce_z(g, reduce_x(g, nz - 1))
    total_out = hidden_ref[...]
    for j in (OWN,) + AWAY:
        if j != OWN:
            results[j].wait_recv()
        pick = hot_cols(pick_col(places_ref[...], experts_of[j]), capacity)
        total_out = total_out + pick_col(probs_ref[...], experts_of[j]) * nn(pick, got_res[j])
    out_ref[...] = total_out.astype(BF)
    sum_part(2)
    line_slot(3, 2)
    reduce_z(3, reduce_x(3, nz - 1))
    reduce_z(0, reduce_x(0, nz - 1))
    to_f = remote(fin, got_f, send_f, recv_f, partner)
    to_f.start()
    to_dx.wait_recv()
    grad_n = own_gn[...] + got_dx[...].astype(F32)
    x_norm, r_one = norm_of(pl.ds(base, rows))
    u = grad_n * gain
    dx = gh[...] + r_one * (u - x_norm * jnp.mean(u * x_norm, axis=1, keepdims=True))
    dx_ref[...] = dx.astype(BF)
    last_part(1)
    pass_part(2)
    to_f.wait_recv()

    def spot(px, co):
        return pl.ds(pl.multiple_of((px * 2 + co) * part, part), part)

    here = spot(x, core)
    for p in range(pairs):
        for i in range(3):
            cols = slice((3 * p + i) * 128, (3 * p + i + 1) * 128)
            total[here, pl.ds(al(i * width + sq * half + p * 128), 128)] = fin[:, cols]
            total[here, pl.ds(al(i * width + (1 - sq) * half + p * 128), 128)] = got_f[:, cols]
    total[here, 3 * width :] = (fin[:, own_cols:].astype(F32) + got_f[:, own_cols:].astype(F32)).astype(BF)

    def pass_on(px, co, send, recv, peer):
        return remote(total.at[spot(px, co)], total.at[spot(px, co)], send, recv, peer)

    pass_on(x, core, send_a, recv_a, across).start()
    pass_on(x, core, send_b.at[0], recv_b.at[0], sibling).start()
    sum_part(3)
    last_part(2)
    pass_part(3)
    pass_on(1 - x, core, send_a, recv_a, across).wait_recv()
    pass_on(1 - x, core, send_b.at[1], recv_b.at[1], sibling).start()
    pass_on(x, 1 - core, send_b.at[0], recv_b.at[0], sibling).wait_recv()
    pass_on(1 - x, 1 - core, send_b.at[1], recv_b.at[1], sibling).wait_recv()
    din_out[...] = total[:, 0 : 3 * width].astype(F32)
    small = total[:, 3 * width : 3 * width + 128].astype(F32)
    droute_out[...] = small[:, 0:EXPERTS]
    dgains_out[...] = small[:, EXPERTS : EXPERTS + 2]
    dout_out[...] = total[:, 3 * width + 128 :].astype(F32)
    last_part(3)
    end_parts()
    for c in results.values():
        c.wait_send()
    pass_on(x, core, send_a, recv_a, across).wait_send()
    pass_on(x, core, send_b.at[0], recv_b.at[0], sibling).wait_send()
    pass_on(1 - x, core, send_b.at[1], recv_b.at[1], sibling).wait_send()
    to_f.wait_send()
    to_dx.wait_send()
    for g in range(len(spans)):
        for n in range(nz):
            for i in range(2):
                to_core(g, n, i).wait_send()
            to_x(g, n).wait_send()
            if n < nz - 1:
                to_z(g, n).wait_send()
    for p in range(pairs):
        give(p, base).wait_send()


def finish(
    xs, qkv, mixed, lse, whole, segments, hidden, probs, places, inner, gin, res, cot, attended, dw_half,
    prompt, nz, capacity, cid,
):
    rows, width = cot.shape
    pairs = width // 256
    cols = whole.shape[1]
    shard = width // nz
    part = shard // 4
    group = 2 * rows
    deep = dw_half.shape[1]
    quarter = (deep // PARTS, dw_half.shape[2])
    dma = pltpu.SemaphoreType.DMA
    two = lambda *shape: [dma(shape), dma(shape)]
    vm = pltpu.VMEM
    return pl.pallas_call(
        functools.partial(finish_kernel, prompt, nz, capacity),
        out_shape=(
            sds((rows, width), BF),
            sds((rows, width), BF),
            sds((shard, 3 * width), F32),
            sds((shard, width), F32),
            sds((shard, EXPERTS), F32),
            sds((shard, 2), F32),
            sds((PARTS, nz) + quarter, BF),
            sds((PARTS, nz) + quarter, BF),
            sds((2, 4) + dw_half.shape[1:], BF),
        ),
        in_specs=[VM] * 10 + [ANY] * 5,
        out_specs=(VM,) * 6 + (ANY,) * 3,
        scratch_shapes=[
            vm((rows, width), F32),
            vm((rows, width), BF),
            vm((4, capacity, width), BF),
            vm((pairs, group, 128), BF),
            vm((2, group, 128), BF),
            vm((2, group, 128), BF),
            vm((128, group), BF),
            vm((128, group), F32),
            vm((group, 3 * width // 2), BF),
            vm((width, group), BF),
            vm((width, cols), BF),
            vm((nz, 2, part, cols), BF),
            vm((nz, part, cols), BF),
            vm((nz - 1, part, cols), BF),
            vm((nz - 1, part, cols), BF),
            vm((part, cols), BF),
            vm((part, cols), BF),
            vm((shard, 4 * width + 128), BF),
            vm((rows, width), BF),
            vm((rows, width), BF),
            vm((rows, width), F32),
            vm((nz,) + quarter, BF),
            vm((PARTS,) + quarter, BF),
            vm((2, 3) + quarter, BF),
            dma((nz + PARTS,)),
        ]
        + two(4) + two(pairs) + two(pairs + 1, nz, 2) + two(pairs + 1, nz) + two(pairs + 1, nz - 1) + two() + two() + two() + two(2)
        + two(PARTS, nz) + two(PARTS, nz) + two(PARTS) + two(PARTS, 2) + two(PARTS, 4),
        compiler_params=params(cid),
        name="finish",
    )(xs, qkv, mixed, lse, whole, segments, hidden, probs, places, inner, gin, res, cot, attended, dw_half)


def spread_kernel(in_ref, out_ref):
    for e in range(EXPERTS):
        out_ref[:, e, :] = in_ref[e].astype(F32)


def spread_experts(parts):
    cores, experts_, r, k = parts.shape
    block = r // 2
    return pl.pallas_call(
        spread_kernel,
        grid=(cores, r // block),
        out_shape=sds((cores * r, experts_, k), F32),
        in_specs=[pl.BlockSpec((None, experts_, block, k), lambda c, i: (c, 0, i, 0))],
        out_specs=pl.BlockSpec((block, experts_, k), lambda c, i: (c * (r // block) + i, 0, 0)),
        compiler_params=params(),
        name="spread",
    )(parts)


def shards(tokens, attn_in, attn_out, router, gains, expert_w, expert_ids, segments, cotangent):
    x = tokens[0]
    cot = cotangent[0]
    rows, width = x.shape
    nz = lax.axis_size("fsdp")
    group = 2 * rows
    prompt = group - segments.shape[1]
    capacity = 2 * rows // EXPERTS
    dp, sq = lax.axis_index("dp"), lax.axis_index("seq")
    core = lax.rem(dp, 2)
    mine = (dp // 2) * 2 + sq

    part = expert_w.shape[0] // 2
    piece = lax.dynamic_slice(expert_w, (core * part, mine, 0), (part, 1, 2 * width))[:, 0]
    xs, whole, qkv, mixed, lse, attended, raw, places_row, places_col, near = begin(
        x, attn_in, attn_out, router, gains, segments, expert_ids[0], cot, piece, prompt, nz, capacity, 0
    )
    hidden, probs, gin, res, inner, dw_half = experts(
        x, attended, whole, places_row, places_col, raw, near, capacity, nz, 1
    )
    block_out, d_tokens, d_in, d_out, d_route, d_gains, _, _, dw_all = finish(
        xs, qkv, mixed, lse, whole, segments, hidden, probs, places_col, inner, gin, res, cot, attended, dw_half,
        prompt, nz, capacity, 2,
    )
    d_expert = spread_experts(dw_all)
    return (
        block_out[None],
        d_tokens[None],
        d_in,
        d_out,
        d_route,
        d_gains,
        d_expert,
    )


def route(choose, capacity, experts_count):
    pair_expert = choose.reshape(-1)
    one_hot = (pair_expert[:, None] == jnp.arange(experts_count, dtype=jnp.int32)[None, :]).astype(
        jnp.int32
    )
    before = jnp.cumsum(one_hot, axis=0) - one_hot
    place = jnp.sum(before * one_hot, axis=1)
    kept = place < capacity
    slots = jnp.where(kept, pair_expert * capacity + place, experts_count * capacity)
    pair_count = pair_expert.shape[0]
    pair_of = (
        jnp.zeros((experts_count * capacity + 1,), jnp.int32)
        .at[slots]
        .set(jnp.arange(pair_count, dtype=jnp.int32))
    )
    filled = (
        jnp.zeros((experts_count * capacity + 1,), jnp.int32)
        .at[slots]
        .set(jnp.ones((pair_count,), jnp.int32))
    )
    return (slots, kept, pair_of[:-1], filled[:-1] > 0)


def expert_pre(expert_in, piece):
    width = piece.shape[2] // 2
    return jnp.einsum(
        "ecd,fed->ecf", expert_in, piece[:, :, :width], preferred_element_type=jnp.float32
    )


def expert_out(activity, piece):
    width = piece.shape[2] // 2
    return jnp.einsum(
        "ecf,fed->ecd", activity, piece[:, :, width:], preferred_element_type=jnp.float32
    )


def expert_back(grad_result, pre_rows, piece):
    width = piece.shape[2] // 2
    grad_act = jnp.einsum(
        "ecd,fed->ecf", grad_result, piece[:, :, width:], preferred_element_type=jnp.float32
    )
    grad_pre = jax.vjp(jax.nn.gelu, pre_rows)[1](grad_act)[0].astype(jnp.bfloat16)
    grad_in = jnp.einsum(
        "ecf,fed->ecd", grad_pre, piece[:, :, :width], preferred_element_type=jnp.float32
    )
    return (grad_pre, grad_in)


def general_shards(tokens, attn_in, attn_out, router, gains, expert_w, expert_ids, segments, cotangent):
    x_rows = tokens[0].astype(jnp.float32)
    tok_rows = x_rows.shape[0]
    width = x_rows.shape[1]
    seq_count = lax.axis_size("seq")
    scale = HEAD_DIM ** (-0.5)
    w_qkv, w_proj, w_route, gain_pair = (
        lax.all_gather(attn_in, "fsdp", axis=0, tiled=True),
        lax.all_gather(attn_out, "fsdp", axis=0, tiled=True),
        lax.all_gather(router, "fsdp", axis=0, tiled=True),
        lax.all_gather(gains, "fsdp", axis=0, tiled=True),
    )
    gain_f = gain_pair.astype(jnp.float32)
    r_one = lax.rsqrt(jnp.mean(x_rows * x_rows, axis=-1, keepdims=True) + EPSILON)
    normed_one = x_rows * r_one
    normed_low = (normed_one * gain_f[:, 0]).astype(jnp.bfloat16)
    projected = jnp.dot(normed_low, w_qkv, preferred_element_type=jnp.float32).astype(jnp.bfloat16)
    local_heads = HEADS // seq_count
    head_cols = local_heads * HEAD_DIM
    arrived = lax.all_to_all(
        projected.reshape(tok_rows, 3, seq_count, head_cols),
        "seq",
        split_axis=2,
        concat_axis=0,
        tiled=True,
    )
    group_len = arrived.shape[0]
    queries = arrived[:, 0, 0].reshape(group_len, local_heads, HEAD_DIM)
    keys = arrived[:, 1, 0].reshape(group_len, local_heads, HEAD_DIM)
    values = arrived[:, 2, 0].reshape(group_len, local_heads, HEAD_DIM)
    seg_full = jnp.concatenate([jnp.full((PROMPT,), -1, jnp.int32), segments[0]])
    block = min(512, group_len)
    key_place = jnp.arange(group_len, dtype=jnp.int32)
    begins = jnp.arange(group_len // block, dtype=jnp.int32) * block

    def block_scores(begin):
        query_block = lax.dynamic_slice_in_dim(queries, begin, block, 0)
        query_place = begin + jnp.arange(block, dtype=jnp.int32)
        query_seg = lax.dynamic_slice_in_dim(seg_full, begin, block, 0)
        raw = (
            jnp.einsum("qhd,khd->hqk", query_block, keys, preferred_element_type=jnp.float32)
            * scale
        )
        allowed = (key_place[None, :] <= query_place[:, None]) & (
            (seg_full[None, :] < 0) | (seg_full[None, :] == query_seg[:, None])
        )
        return (jnp.where(allowed[None], raw, NEGATIVE), query_block)

    def forward_block(begin):
        masked, query_block = block_scores(begin)
        row_max = jnp.max(masked, axis=-1, keepdims=True)
        expo = jnp.exp(masked - row_max)
        row_total = jnp.sum(expo, axis=-1, keepdims=True)
        probs = expo / row_total
        mixed_block = jnp.einsum(
            "hqk,khd->qhd", probs.astype(jnp.bfloat16), values, preferred_element_type=jnp.float32
        )
        return (mixed_block.astype(jnp.bfloat16), (row_max + jnp.log(row_total))[:, :, 0])

    mixed_blocks, log_totals = lax.map(forward_block, begins)
    mixed_heads = mixed_blocks.reshape(group_len, 1, head_cols)
    returned = lax.all_to_all(mixed_heads, "seq", split_axis=0, concat_axis=1, tiled=True)
    attended = returned.reshape(tok_rows, width)
    hidden = x_rows + jnp.dot(attended, w_proj, preferred_element_type=jnp.float32)
    r_two = lax.rsqrt(jnp.mean(hidden * hidden, axis=-1, keepdims=True) + EPSILON)
    normed_two = hidden * r_two
    routed_low = (normed_two * gain_f[:, 1]).astype(jnp.bfloat16)
    logits = jnp.dot(routed_low, w_route, preferred_element_type=jnp.float32)
    probs_r = jax.nn.softmax(logits, axis=-1)
    choose = expert_ids[0]
    choose_map = (choose[:, :, None] == jnp.arange(EXPERTS, dtype=jnp.int32)[None, None, :]).astype(
        jnp.float32
    )
    gates = jnp.sum(probs_r[:, None, :] * choose_map, axis=-1)
    capacity = 2 * tok_rows // EXPERTS
    slots, kept, pair_of, filled = route(choose, capacity, EXPERTS)
    token_of = pair_of // 2
    expert_in = jnp.where(
        filled[:, None], routed_low[token_of], jnp.zeros((), jnp.bfloat16)
    ).reshape(EXPERTS, capacity, width)
    piece = lax.all_gather(expert_w, "fsdp", axis=0, tiled=True)
    pre_rows = expert_pre(expert_in, piece)
    result = expert_out(jax.nn.gelu(pre_rows).astype(jnp.bfloat16), piece)
    padded = jnp.concatenate(
        [result.reshape(EXPERTS * capacity, width), jnp.zeros((1, width), jnp.float32)], axis=0
    )
    picked = padded[slots].reshape(tok_rows, 2, width)
    kept_f = kept.astype(jnp.float32).reshape(tok_rows, 2)
    weight_pair = gates * kept_f
    block_out = hidden + jnp.sum(weight_pair[..., None] * picked, axis=1)
    grad_out_rows = cotangent[0].astype(jnp.float32)
    grad_gates = kept_f * jnp.sum(grad_out_rows[:, None, :] * picked, axis=-1)
    grad_probs = jnp.sum(grad_gates[:, :, None] * choose_map, axis=1)
    grad_logits = probs_r * (grad_probs - jnp.sum(probs_r * grad_probs, axis=-1, keepdims=True))
    grad_route_w = jnp.dot(routed_low.astype(jnp.float32).T, grad_logits, precision=HIGH)
    grad_routed = jnp.dot(grad_logits, w_route.astype(jnp.float32).T, precision=HIGH)
    scaled = (weight_pair[:, :, None] * grad_out_rows[:, None, :]).reshape(2 * tok_rows, width)
    grad_result = (
        jnp.where(filled[:, None], scaled[pair_of], 0.0)
        .astype(jnp.bfloat16)
        .reshape(EXPERTS, capacity, width)
    )
    piece = lax.all_gather(expert_w, "fsdp", axis=0, tiled=True)
    pre_rows = expert_pre(expert_in, piece)
    act_rows = jax.nn.gelu(pre_rows).astype(jnp.bfloat16)
    grad_pre_rows, grad_in_rows = expert_back(grad_result, pre_rows, piece)
    act_store = act_rows
    pre_rows = grad_pre_rows
    act_rows = act_store
    grad_first = jnp.einsum("ecd,ecf->fed", expert_in, pre_rows, preferred_element_type=jnp.float32)
    grad_second = jnp.einsum(
        "ecf,ecd->fed", act_rows, grad_result, preferred_element_type=jnp.float32
    )
    expert_shard = lax.psum_scatter(
        jnp.concatenate([grad_first, grad_second], axis=2).astype(jnp.bfloat16),
        "fsdp",
        scatter_dimension=0,
        tiled=True,
    )
    padded_in = jnp.concatenate(
        [grad_in_rows.reshape(EXPERTS * capacity, width), jnp.zeros((1, width), jnp.float32)],
        axis=0,
    )
    grad_routed = grad_routed + jnp.sum(padded_in[slots].reshape(tok_rows, 2, width), axis=1)
    grad_gain_two = jnp.sum(grad_routed * normed_two, axis=0)
    scaled_two = grad_routed * gain_f[:, 1]
    grad_hidden = grad_out_rows + r_two * (
        scaled_two - normed_two * jnp.mean(scaled_two * normed_two, axis=-1, keepdims=True)
    )
    hid_low = grad_hidden.astype(jnp.bfloat16)
    grad_proj_w = jnp.dot(attended.T, hid_low, preferred_element_type=jnp.float32)
    grad_attended = jnp.dot(hid_low, w_proj.T, preferred_element_type=jnp.float32).astype(
        jnp.bfloat16
    )
    grad_heads = lax.all_to_all(
        grad_attended.reshape(tok_rows, seq_count, head_cols),
        "seq",
        split_axis=1,
        concat_axis=0,
        tiled=True,
    )
    grad_mixed = grad_heads.reshape(group_len, local_heads, HEAD_DIM)

    def back_block(carry, inputs):
        begin, log_rows = inputs
        masked, query_block = block_scores(begin)
        probs = jnp.exp(masked - log_rows[:, :, None])
        grad_block = lax.dynamic_slice_in_dim(grad_mixed, begin, block, 0)
        grad_p = jnp.einsum("qhd,khd->hqk", grad_block, values, preferred_element_type=jnp.float32)
        inner = jnp.sum(probs * grad_p, axis=-1, keepdims=True)
        grad_scores = (probs * (grad_p - inner)).astype(jnp.bfloat16)
        grad_query = (
            jnp.einsum("hqk,khd->qhd", grad_scores, keys, preferred_element_type=jnp.float32)
            * scale
        )
        grad_key = (
            carry[0]
            + jnp.einsum(
                "hqk,qhd->khd", grad_scores, query_block, preferred_element_type=jnp.float32
            )
            * scale
        )
        grad_value = carry[1] + jnp.einsum(
            "hqk,qhd->khd",
            probs.astype(jnp.bfloat16),
            grad_block,
            preferred_element_type=jnp.float32,
        )
        return ((grad_key, grad_value), grad_query)

    zero_heads = jnp.zeros((group_len, local_heads, HEAD_DIM), jnp.float32)
    (grad_keys, grad_values), grad_queries = lax.scan(
        back_block, (zero_heads, zero_heads), (begins, log_totals)
    )
    stacked = jnp.stack(
        [
            grad_queries.reshape(group_len, head_cols),
            grad_keys.reshape(group_len, head_cols),
            grad_values.reshape(group_len, head_cols),
        ],
        axis=1,
    )
    stacked = stacked.astype(jnp.bfloat16).reshape(group_len, 3, 1, head_cols)
    grad_back = lax.all_to_all(stacked, "seq", split_axis=0, concat_axis=2, tiled=True)
    grad_proj_rows = grad_back.reshape(tok_rows, 3 * width)
    grad_qkv_w = jnp.dot(normed_low.T, grad_proj_rows, preferred_element_type=jnp.float32)
    grad_normed = jnp.dot(grad_proj_rows, w_qkv.T, preferred_element_type=jnp.float32)
    grad_gain_one = jnp.sum(grad_normed * normed_one, axis=0)
    scaled_one = grad_normed * gain_f[:, 0]
    grad_x = grad_hidden + r_one * (
        scaled_one - normed_one * jnp.mean(scaled_one * normed_one, axis=-1, keepdims=True)
    )
    grad_gains = jnp.stack([grad_gain_one, grad_gain_two], axis=1)
    shard_qkv, shard_proj, shard_route, shard_gains = (
        lax.psum_scatter(
            grad_qkv_w.astype(jnp.bfloat16), "fsdp", scatter_dimension=0, tiled=True
        ).astype(jnp.float32),
        lax.psum_scatter(
            grad_proj_w.astype(jnp.bfloat16), "fsdp", scatter_dimension=0, tiled=True
        ).astype(jnp.float32),
        lax.psum_scatter(
            grad_route_w.astype(jnp.bfloat16), "fsdp", scatter_dimension=0, tiled=True
        ).astype(jnp.float32),
        lax.psum_scatter(
            grad_gains.astype(jnp.bfloat16), "fsdp", scatter_dimension=0, tiled=True
        ).astype(jnp.float32),
    )
    part_qkv, part_proj, part_expert = (
        lax.psum_scatter(
            shard_qkv.astype(jnp.bfloat16), ("dp", "seq"), scatter_dimension=1, tiled=True
        ).astype(jnp.float32),
        lax.psum_scatter(
            shard_proj.astype(jnp.bfloat16), ("dp", "seq"), scatter_dimension=1, tiled=True
        ).astype(jnp.float32),
        lax.psum_scatter(expert_shard, ("dp", "seq"), scatter_dimension=2, tiled=True).astype(
            jnp.float32
        ),
    )
    summed_qkv, summed_proj, summed_expert = (
        lax.all_gather(part_qkv.astype(jnp.bfloat16), ("dp", "seq"), axis=1, tiled=True).astype(
            part_qkv.dtype
        ),
        lax.all_gather(part_proj.astype(jnp.bfloat16), ("dp", "seq"), axis=1, tiled=True).astype(
            part_proj.dtype
        ),
        lax.all_gather(part_expert.astype(jnp.bfloat16), ("dp", "seq"), axis=2, tiled=True).astype(
            part_expert.dtype
        ),
    )
    summed_route, summed_gains = lax.psum((shard_route, shard_gains), ("dp", "seq"))
    return (
        block_out.astype(jnp.bfloat16)[None],
        grad_x.astype(jnp.bfloat16)[None],
        summed_qkv,
        summed_proj,
        summed_route,
        summed_gains,
        summed_expert,
    )


def fits(mesh):
    return mesh.shape["fsdp"] == 4 and mesh.shape["dp"] == 4 and mesh.shape["seq"] == 2


def solution(mesh):
    body = shards if fits(mesh) else general_shards
    in_specs = (
        P(("dp", "fsdp"), "seq", None),
        P("fsdp", None),
        P("fsdp", None),
        P("fsdp", None),
        P("fsdp", None),
        P("fsdp", None, None),
        P(("dp", "fsdp"), "seq", None),
        P(("dp", "fsdp"), None),
        P(("dp", "fsdp"), "seq", None),
    )
    out_specs = (
        P(("dp", "fsdp"), "seq", None),
        P(("dp", "fsdp"), "seq", None),
        P("fsdp", None),
        P("fsdp", None),
        P("fsdp", None),
        P("fsdp", None),
        P("fsdp", None, None),
    )
    return jax.shard_map(body, mesh=mesh, in_specs=in_specs, out_specs=out_specs, check_vma=False)
```

```python
import functools

import jax
import jax.numpy as jnp
from jax import lax
from jax.experimental import pallas as pl
from jax.experimental.pallas import tpu as pltpu
from jax.sharding import PartitionSpec as P

HEADS = 12
HEAD_DIM = 64
EXPERTS = 4
PROMPT = 1024
EPSILON = 1e-06
NEGATIVE = -1e30
HIGH = lax.Precision.HIGHEST
LOG2E = 1.4426950408889634
BF = jnp.bfloat16
F32 = jnp.float32
MESH = pl.DeviceIdType.MESH
VMEM_LIMIT = 60 << 20
QB = 256
ANY = pl.BlockSpec(memory_space=pl.ANY)
VM = pl.BlockSpec(memory_space=pltpu.VMEM)


def nn(a, b):
    return lax.dot_general(a, b, (((1,), (0,)), ((), ())), preferred_element_type=F32)


def nt(a, b):
    return lax.dot_general(a, b, (((1,), (1,)), ((), ())), preferred_element_type=F32)


def tn(a, b):
    return lax.dot_general(a, b, (((0,), (0,)), ((), ())), preferred_element_type=F32)


def iota(shape, dim):
    return lax.broadcasted_iota(jnp.int32, shape, dim)


def params(cid=None):
    if cid is None:
        return pltpu.CompilerParams(vmem_limit_bytes=VMEM_LIMIT)
    return pltpu.CompilerParams(
        vmem_limit_bytes=VMEM_LIMIT, collective_id=cid, has_side_effects=True
    )


def sds(shape, dtype):
    return jax.ShapeDtypeStruct(shape, dtype)


def place():
    dp, sq, z = lax.axis_index("dp"), lax.axis_index("seq"), lax.axis_index("fsdp")
    return dp, sq, z, dp // 2, lax.rem(dp, 2)


def greet(peers):
    barrier = pltpu.get_barrier_semaphore()
    for peer in peers:
        pl.semaphore_signal(barrier, inc=1, device_id=peer, device_id_type=MESH)
    pl.semaphore_wait(barrier, len(peers))


def remote(src, dst, send, recv, peer):
    return pltpu.make_async_remote_copy(
        src_ref=src, dst_ref=dst, send_sem=send, recv_sem=recv, device_id=peer, device_id_type=MESH
    )


def al(x):
    return pl.multiple_of(x, 128)


def allowed_tile(j, i, prompt, seg_col, seg_row):
    mask = None
    if i == j:
        mask = iota((QB, QB), 0) <= iota((QB, QB), 1)
    if j * QB >= prompt:
        keys, queries = j * QB - prompt, i * QB - prompt
        same = seg_col[keys : keys + QB, :] == seg_row[:, queries : queries + QB]
        mask = same if mask is None else mask & same
    return mask


def flip_chip(x, sq, fx, fy):
    px = 1 - x if fx else x
    py = 1 - sq if fy else sq
    return px, py


SOURCES = ((1, 0), (0, 1), (0, 0), (1, 1))
OWN = 2
AWAY = (0, 1, 3)


class Line:
    def __init__(self, nz, dp, sq, z, sources, target, sems):
        self.nz, self.dp, self.sq, self.z = nz, dp, sq, z
        self.sources, self.target, self.sems = sources, target, sems

    def copy(self, stage, up):
        nz, z = self.nz, self.z
        zone = z - (stage - 1) if up else z + (stage - 1)
        zone = lax.rem(zone + nz, nz)
        to = lax.rem(z + 1, nz) if up else lax.rem(z + nz - 1, nz)
        i = stage - 1
        send, recv = (self.sems[0], self.sems[1]) if up else (self.sems[2], self.sems[3])
        return remote(
            self.sources(stage, zone), self.target.at[zone], send.at[i], recv.at[i], (self.dp, self.sq, to)
        )

    def arrival(self, stage, up):
        nz, z = self.nz, self.z
        zone = lax.rem((z - stage if up else z + stage) + nz, nz)
        to = lax.rem(z + 1, nz) if up else lax.rem(z + nz - 1, nz)
        i = stage - 1
        send, recv = (self.sems[0], self.sems[1]) if up else (self.sems[2], self.sems[3])
        return remote(
            self.sources(stage, zone), self.target.at[zone], send.at[i], recv.at[i], (self.dp, self.sq, to)
        )

    def sends(self, stage, up):
        z, nz = self.z, self.nz
        return (z < nz - 1) & (z >= stage - 1) if up else (z > 0) & (z <= nz - stage)

    def gets(self, stage, up):
        return self.z >= stage if up else self.z <= self.nz - 1 - stage

    def start(self, stage):
        for up in (True, False):

            @pl.when(self.sends(stage, up))
            def _(up=up):
                self.copy(stage, up).start()

    def wait_recv(self, stage):
        for up in (True, False):

            @pl.when(self.gets(stage, up))
            def _(up=up):
                self.arrival(stage, up).wait_recv()

    def wait_send(self, stage):
        for up in (True, False):

            @pl.when(self.sends(stage, up))
            def _(up=up):
                self.copy(stage, up).wait_send()


def eighth(x, prompt):
    row = x.astype(F32)
    col = jnp.broadcast_to(row, (128, row.shape[1])).T[:, 0:1]
    return row, col


def begin_kernel(
    prompt, nz, capacity, x_ref, in_ref, out_ref, router_ref, gains_ref, seg_ref, ids_ref, cot_ref, piece_ref,
    xs_ref, w_ref, qkv_ref, mixed_ref, lse_ref, att_ref, raw_ref, row_ref, col_ref, near_ref,
    pack, vt, local, send_t, recv_t, send_z, recv_z, send_p, recv_p, send_c, recv_c, send_o, recv_o, *line_sems,
):
    dp, sq, z, x, core = place()
    rows, width = x_ref.shape
    shard = in_ref.shape[0]
    part = shard // 4
    half = width // 2
    pairs = half // 128
    own_cols = 3 * half
    lead = own_cols + 128
    sibling = (x * 2 + 1 - core, sq, z)
    partner = (dp, 1 - sq, z)
    across = ((1 - x) * 2 + core, sq, z)
    others = [(dp, sq, lax.rem(z + d, nz)) for d in range(1, nz)]
    base = pl.multiple_of(sq * rows, rows)
    there = pl.multiple_of((1 - sq) * rows, rows)
    groups = (pl.ds(0, lead), pl.ds(lead, width))

    packs = [
        pltpu.make_async_copy(
            in_ref.at[:, pl.ds(al(i * width + sq * half + p * 128), 128)],
            pack.at[:, pl.ds((3 * p + i) * 128, 128)],
            local.at[3 * p + i],
        )
        for p in range(pairs)
        for i in range(3)
    ]
    packs.append(pltpu.make_async_copy(out_ref, pack.at[:, groups[1]], local.at[3 * pairs]))
    for c in packs:
        c.start()
    lane = iota((1, 128), 1)
    small = jnp.zeros((shard, 128), F32)
    for e in range(EXPERTS):
        small = jnp.where(lane == e, router_ref[:, e : e + 1].astype(F32), small)
    for e in range(2):
        small = jnp.where(lane == EXPERTS + e, gains_ref[:, e : e + 1].astype(F32), small)
    pack[:, own_cols:lead] = small.astype(BF)
    greet([sibling, partner, across] + others)
    tokens = remote(x_ref, xs_ref.at[pl.ds(base, rows)], send_t, recv_t, partner)
    tokens.start()
    for c in packs:
        c.wait()

    def at(zs, px, co, g):
        return w_ref.at[pl.ds(pl.multiple_of(zs * shard + (px * 2 + co) * part, part), part), groups[g]]

    def along(d, g):
        src = pack.at[pl.ds(pl.multiple_of((x * 2 + core) * part, part), part), groups[g]]
        return remote(src, at(z, x, core, g), send_z.at[d - 1, g], recv_z.at[d - 1, g], others[d - 1])

    def source(d):
        return lax.rem(z + nz - d, nz)

    def over(d, g, px):
        ref = at(source(d), px, core, g)
        return remote(ref, ref, send_p.at[d - 1, g], recv_p.at[d - 1, g], across)

    def beside(d, g, i, co):
        ref = at(source(d), (x, 1 - x)[i], co, g)
        return remote(ref, ref, send_c.at[d - 1, g, i], recv_c.at[d - 1, g, i], sibling)

    for d in range(1, nz):
        along(d, 0).start()
    own = pltpu.make_async_copy(pack, w_ref.at[pl.ds(pl.multiple_of(z * shard, shard), shard)], local.at[3 * pairs + 1])
    own.start()
    xs_ref[pl.ds(base, rows), :] = x_ref[...]
    ids = ids_ref[...]
    chosen = jnp.where((ids[:, 0:1] == lane) | (ids[:, 1:2] == lane), 1.0, 0.0)
    earlier = (iota((rows, rows), 1) < iota((rows, rows), 0)).astype(F32).astype(BF)
    places = jnp.where(chosen > 0, nn(earlier, chosen.astype(BF)), -1.0)
    col_ref[...] = places
    places = places.T[0:8, :]
    row_ref[...] = places

    def gather(g):
        for d in range(1, nz):
            along(d, g).wait_recv()
            over(d, g, x).start()
            beside(d, g, 0, core).start()
        if g == 0:
            line.start(1)
            for d in range(1, nz):
                along(d, 1).start()
        for d in range(1, nz):
            over(d, g, 1 - x).wait_recv()
            beside(d, g, 1, core).start()

    def gathered(g):
        for d in range(1, nz):
            for i in range(2):
                beside(d, g, i, 1 - core).wait_recv()

    stay = pltpu.make_async_copy(piece_ref, near_ref.at[z], local.at[3 * pairs + 2])
    stay.start()
    line = Line(
        nz, dp, sq, z, lambda stage, zone: piece_ref if stage == 1 else near_ref.at[zone], near_ref, line_sems
    )
    gather(0)
    gathered(0)
    own.wait()
    tokens.wait_recv()

    gain = w_ref[:, own_cols:lead].astype(F32).T[EXPERTS : EXPERTS + 1, :]
    xf = xs_ref[...].astype(F32)
    normed = (xf * lax.rsqrt(jnp.mean(xf * xf, axis=1, keepdims=True) + EPSILON) * gain).astype(BF)
    for p in range(pairs):
        got = nn(normed, w_ref[:, p * 384 : (p + 1) * 384]).astype(BF)
        for i in range(3):
            qkv_ref[p, i] = got[:, i * 128 : (i + 1) * 128]

    blocks = 2 * rows // QB
    const = HEAD_DIM ** (-0.5) * LOG2E
    seg_row, seg_col = eighth(seg_ref[...], prompt)

    def back(p, own_side):
        src = mixed_ref.at[p, pl.ds(there, rows)]
        side = sq if own_side else 1 - sq
        return remote(
            src, att_ref.at[:, pl.ds(al(side * half + p * 128), 128)], send_o.at[p], recv_o.at[p], partner
        )

    @pl.loop(0, pairs)
    def _(p):
        vt[0:128, :] = qkv_ref[p, 2].T
        vt[128:144, :] = jnp.ones((16, vt.shape[1]), BF)
        for i in range(blocks):
            here = slice(i * QB, (i + 1) * QB)
            both = []
            for h in range(2):
                lanes = iota((1, 128), 1) // HEAD_DIM == h
                q = jnp.where(lanes, qkv_ref[p, 0, here, :], jnp.zeros((), BF))
                tiles = []
                for j in range(i + 1):
                    s = nt(qkv_ref[p, 1, j * QB : (j + 1) * QB, :], q)
                    mask = allowed_tile(j, i, prompt, seg_col, seg_row)
                    if mask is not None:
                        s = jnp.where(mask, s, NEGATIVE)
                    tiles.append(s)
                top = functools.reduce(
                    jnp.maximum, [jnp.max(s, axis=0, keepdims=True) for s in tiles]
                )
                top = top * const
                acc = None
                for j, s in enumerate(tiles):
                    pr = jnp.exp2(s * const - top).astype(BF)
                    add = nn(vt[:, j * QB : (j + 1) * QB], pr)
                    acc = add if acc is None else acc + add
                total = acc[128:129, :]
                lse_ref[p, h : h + 1, here] = top + jnp.log2(total)
                low = h * HEAD_DIM
                both.append(acc[low : low + HEAD_DIM, :] * (1.0 / total))
            mixed_ref[p, here, :] = jnp.concatenate(both, axis=0).T.astype(BF)
        back(p, True).start()
        att_ref[:, pl.ds(al(sq * half + p * 128), 128)] = mixed_ref[p, pl.ds(base, rows), :]

        @pl.when(p == 0)
        def _():
            line.wait_recv(1)
            line.start(2)
            gather(1)

    for j, (px, py) in enumerate([flip_chip(x, sq, *f) for f in SOURCES]):
        hot = hot_rows(pick_row(row_ref[...], px * 2 + py), capacity)
        raw_ref[j] = nn(hot, cot_ref[...]).astype(BF)
    for p in range(pairs):
        back(p, False).wait_recv()
        back(p, True).wait_send()
    gathered(1)
    tokens.wait_send()
    for g in range(2):
        for d in range(1, nz):
            along(d, g).wait_send()
            over(d, g, x).wait_send()
            for i in range(2):
                beside(d, g, i, core).wait_send()
    line.wait_recv(2)
    line.wait_send(1)
    line.wait_send(2)
    stay.wait()


def begin(x, attn_in, attn_out, router, gains, segments, ids, cot, piece, prompt, nz, capacity, cid):
    rows, width = x.shape
    shard = attn_in.shape[0]
    pairs = width // 256
    cols = 3 * width // 2 + 128 + width
    dma = pltpu.SemaphoreType.DMA
    two = lambda *shape: [dma(shape), dma(shape)]
    return pl.pallas_call(
        functools.partial(begin_kernel, prompt, nz, capacity),
        out_shape=(
            sds((2 * rows, width), BF),
            sds((shard * nz, cols), BF),
            sds((pairs, 3, 2 * rows, 128), BF),
            sds((pairs, 2 * rows, 128), BF),
            sds((pairs, 8, 2 * rows), F32),
            sds((rows, width), BF),
            sds((4, capacity, width), BF),
            sds((8, rows), F32),
            sds((rows, 128), F32),
            sds((nz,) + piece.shape, BF),
        ),
        in_specs=[VM, ANY, ANY, VM, VM, VM, VM, VM, ANY],
        out_specs=(VM,) * 9 + (ANY,),
        scratch_shapes=[
            pltpu.VMEM((shard, cols), BF),
            pltpu.VMEM((144, 2 * rows), BF),
            dma((3 * pairs + 3,)),
        ]
        + two() + two(nz - 1, 2) + two(nz - 1, 2) + two(nz - 1, 2, 2) + two(pairs) + two(2) + two(2),
        compiler_params=params(cid),
        name="begin",
    )(x, attn_in, attn_out, router, gains, segments, ids, cot, piece)


def softmax_lanes(logits):
    live = iota(logits.shape, 1) < EXPERTS
    logits = jnp.where(live, logits, NEGATIVE)
    expo = jnp.where(live, jnp.exp(logits - jnp.max(logits, axis=1, keepdims=True)), 0.0)
    return expo / jnp.sum(expo, axis=1, keepdims=True)


def pick_row(table, e):
    return jnp.sum(jnp.where(iota((8, 1), 0) == e, table, 0.0), axis=0, keepdims=True)


def pick_col(table, e):
    return jnp.sum(jnp.where(iota((1, 128), 1) == e, table, 0.0), axis=1, keepdims=True)


def hot_rows(row, capacity):
    return (row == iota((capacity, 1), 0).astype(F32)).astype(F32).astype(BF)


def hot_cols(col, capacity):
    return (col == iota((1, capacity), 1).astype(F32)).astype(F32).astype(BF)


GELU_A = 0.7978845608028654
GELU_B = GELU_A * 0.044715


def expert_step(x, g, w):
    width = x.shape[1]
    first, second = w[:, :width], w[:, width:]
    pre = nt(x, first)
    back = nt(g, second)
    square = pre * pre
    t = jnp.tanh(pre * (GELU_A + GELU_B * square))
    rise = 0.5 + 0.5 * t
    act = (pre * rise).astype(BF)
    slope = rise + (0.5 * pre) * (1.0 - t * t) * (GELU_A + (3.0 * GELU_B) * square)
    grad_pre = (back * slope).astype(BF)
    return nn(act, second), nn(grad_pre, first), tn(grad_pre, x), tn(act, g)


def experts_kernel(
    capacity, nz, x_ref, att_ref, w_hbm, places_row, places_col, raw_send, near_ref,
    hidden_ref, probs_ref, back_gin, out_res, back_dot, dw_ref,
    wp, send_in, got_in, send_gate, got_gate, own_w, theirs, grad, res_acc, gin_acc, out_gin, out_dot, dw_away, dw_got,
    raw_ref, local, send_x, recv_x, send_w, recv_w, send_i, recv_i, send_t, recv_t, send_r, recv_r, send_d, recv_d, send_v, recv_v, *line_sems,
):
    dp, sq, z, x, core = place()
    rows, width = x_ref.shape
    sibling = (x * 2 + 1 - core, sq, z)
    corner = [flip_chip(x, sq, *f) for f in SOURCES]
    plane = [(px * 2 + core, py, z) for px, py in corner]
    experts_of = [px * 2 + py for px, py in corner]
    beside_z = (dp, sq, z + 1 - 2 * lax.rem(z, 2))
    shift = jnp.where(z >= nz // 2, 1, 0)
    far_zone = jnp.where(z >= nz // 2, 0, nz - 1)
    at_end = (z == 0) | (z == nz - 1)
    near_peers = [sibling] + [plane[j] for j in AWAY]
    barrier = pltpu.get_barrier_semaphore()
    for peer in near_peers:
        pl.semaphore_signal(barrier, inc=1, device_id=peer, device_id_type=MESH)

    @pl.when(at_end)
    def _():
        pl.semaphore_signal(barrier, inc=1, device_id=beside_z, device_id_type=MESH)

    pl.semaphore_wait(barrier, len(near_peers) + jnp.where(at_end, 0, 1))
    line = Line(nz, dp, sq, z, lambda stage, zone: near_ref.at[zone], own_w, line_sems)
    line.start(nz - 1)

    def go_raw(j):
        return remote(raw_send.at[j], raw_ref.at[j], send_x.at[j], recv_x.at[j], plane[j])

    go_raw(0).start()
    go_raw(1).start()

    def weights(slot):
        if slot == nz - 1:
            return remote(own_w.at[far_zone], theirs.at[far_zone], send_w.at[slot], recv_w.at[slot], sibling)
        zone = slot + shift
        return remote(near_ref.at[zone], theirs.at[zone], send_w.at[slot], recv_w.at[slot], sibling)

    lifts = []
    for i in range(nz - 1):
        weights(i).start()
        lifts.append(pltpu.make_async_copy(near_ref.at[i + shift], own_w.at[i + shift], local.at[2 + i]))
    for c in lifts:
        c.start()
    far_lift = pltpu.make_async_copy(near_ref.at[far_zone], own_w.at[far_zone], local.at[1 + nz])

    @pl.when(jnp.logical_not(at_end))
    def _():
        far_lift.start()

    own_raw = pltpu.make_async_copy(raw_send.at[OWN], raw_ref.at[OWN], local.at[1])
    own_raw.start()
    load = pltpu.make_async_copy(w_hbm.at[:, 3 * width // 2 :], wp, local.at[0])
    load.start()
    load.wait()

    hidden = x_ref[...].astype(F32) + nn(att_ref[...], wp[:, 128:])
    hidden_ref[...] = hidden
    r_two = lax.rsqrt(jnp.mean(hidden * hidden, axis=1, keepdims=True) + EPSILON)
    small = wp[:, :128]
    gain = small.astype(F32).T[EXPERTS + 1 : EXPERTS + 2, :]
    routed = (hidden * r_two * gain).astype(BF)
    probs = softmax_lanes(nn(routed, small))
    probs_ref[...] = probs
    flat = probs.T[0:8, :]
    high = flat.astype(BF)
    rest = flat - high.astype(F32)
    mid = rest.astype(BF)
    low = (rest - mid.astype(F32)).astype(BF)
    split = jnp.concatenate([high.astype(F32), mid.astype(F32), low.astype(F32)], axis=0).astype(BF)

    def go_in(j):
        return remote(send_in.at[j], got_in.at[j], send_i.at[j], recv_i.at[j], plane[j])

    def go_gate(j):
        return remote(send_gate.at[j], got_gate.at[j], send_t.at[j], recv_t.at[j], plane[j])

    for j in range(4):
        e = experts_of[j]
        taken = nn(hot_rows(pick_row(places_row[...], e), capacity), routed).astype(BF)
        three = nn(split, hot_cols(pick_col(places_col[...], e), capacity))
        gate = three[0:8] + three[8:16] + three[16:24]
        gate = jnp.broadcast_to(pick_row(gate, e), gate.shape)
        if j != OWN:
            send_in[j] = taken
            send_gate[j] = gate
            go_gate(j).start()
        if j < OWN:
            go_in(j).start()
        if j == OWN:
            got_in[j] = taken
            got_gate[j] = gate
    own_raw.wait()
    for c in lifts:
        c.wait()
    for i in range(nz - 1):
        weights(i).wait_recv()

    def go_gin(j):
        return remote(out_gin.at[j], back_gin.at[j], send_r.at[j], recv_r.at[j], plane[j])

    def go_dot(j):
        return remote(out_dot.at[j], back_dot.at[j], send_d.at[j], recv_d.at[j], plane[j])

    def go_dw(n):
        return remote(dw_away.at[n], dw_got.at[n], send_v.at[n], recv_v.at[n], sibling)

    def arrive(lo, hi):
        for j in range(lo, hi):
            if j != OWN:
                go_raw(j).wait_recv()
                go_in(j).wait_recv()
                go_gate(j).wait_recv()
            gate = got_gate[j].T[:, 0:1]
            grad[j] = (raw_ref[j].astype(F32) * gate).astype(BF)

    def chunk(lo, hi, w_ref, dw, d, first, at):
        count = (hi - lo) * capacity
        xs = got_in[lo:hi].reshape(count, width)
        gs = grad[lo:hi].reshape(count, width)
        res, gin, d_first, d_second = expert_step(xs, gs, w_ref[d])
        here = slice(at * capacity, at * capacity + count)
        res_acc[here, :] += res
        gin_acc[here, :] += gin
        if first:
            dw[d, :, :width] = d_first.astype(BF)
            dw[d, :, width:] = d_second.astype(BF)
        else:
            dw[d, :, :width] = (dw[d, :, :width].astype(F32) + d_first).astype(BF)
            dw[d, :, width:] = (dw[d, :, width:].astype(F32) + d_second).astype(BF)

    def send_back(lo, hi, at):
        for j in range(lo, hi):
            here = slice((at + j - lo) * capacity, (at + j - lo + 1) * capacity)
            prod = res_acc[here, :] * raw_ref[j].astype(F32)
            narrow = functools.reduce(jnp.add, [prod[:, i : i + 128] for i in range(0, width, 128)])
            inner = jnp.broadcast_to(jnp.sum(narrow.T, axis=0, keepdims=True), (8, capacity))
            if j != OWN:
                out_gin[j] = gin_acc[here, :].astype(BF)
                out_dot[j] = inner
                go_gin(j).start()
                go_dot(j).start()
            else:
                back_gin[j] = gin_acc[here, :].astype(BF)
                back_dot[j] = inner
        for j in range(lo, hi):
            here = slice((at + j - lo) * capacity, (at + j - lo + 1) * capacity)
            out_res[j] = res_acc[here, :].astype(BF)

    both = ((theirs, dw_away), (own_w, dw_ref))
    res_acc[...] = jnp.zeros(res_acc.shape, F32)
    gin_acc[...] = jnp.zeros(gin_acc.shape, F32)
    arrive(OWN, OWN + 1)
    for w_ref, dw in both:

        @pl.loop(0, nz - 1)
        def _(i):
            chunk(OWN, OWN + 1, w_ref, dw, i + shift, True, OWN)

    arrive(0, OWN)
    go_raw(3).start()
    go_in(3).start()
    for w_ref, dw in both:

        @pl.loop(0, nz - 1)
        def _(i):
            chunk(0, OWN, w_ref, dw, i + shift, False, 0)

    @pl.when(jnp.logical_not(at_end))
    def _():
        far_lift.wait()

    line.wait_recv(nz - 1)
    weights(nz - 1).start()
    chunk(0, OWN + 1, own_w, dw_ref, far_zone, True, 0)
    weights(nz - 1).wait_recv()
    chunk(0, OWN + 1, theirs, dw_away, far_zone, True, 0)
    send_back(0, OWN + 1, 0)
    arrive(3, 4)
    res_acc[0:capacity, :] = jnp.zeros((capacity, width), F32)
    gin_acc[0:capacity, :] = jnp.zeros((capacity, width), F32)

    @pl.loop(0, nz)
    def _(d):
        chunk(3, 4, theirs, dw_away, d, False, 0)
        go_dw(d).start()

    @pl.loop(0, nz)
    def _(d):
        chunk(3, 4, own_w, dw_ref, d, False, 0)

    send_back(3, 4, 0)
    for n in range(nz):
        go_dw(n).wait_recv()
        dw_ref[n] = (dw_ref[n].astype(F32) + dw_got[n].astype(F32)).astype(BF)
    for j in AWAY:
        go_gin(j).wait_recv()
        go_dot(j).wait_recv()
    line.wait_send(nz - 1)
    for n in range(nz):
        weights(n).wait_send()
        go_dw(n).wait_send()
    for j in AWAY:
        for c in (go_raw(j), go_in(j), go_gate(j), go_gin(j), go_dot(j)):
            c.wait_send()


def experts(x, attended, whole, places_row, places_col, raw, near, capacity, nz, cid):
    rows, width = x.shape
    part = near.shape[1]
    slots = sds((4, capacity, width), BF)
    small = sds((4, 8, capacity), F32)
    dma = pltpu.SemaphoreType.DMA
    two = lambda *shape: [dma(shape), dma(shape)]
    vm = pltpu.VMEM
    return pl.pallas_call(
        functools.partial(experts_kernel, capacity, nz),
        out_shape=(
            sds((rows, width), F32),
            sds((rows, 128), F32),
            slots,
            slots,
            small,
            sds((nz, part, 2 * width), BF),
        ),
        in_specs=[VM, VM, ANY, VM, VM, ANY, ANY],
        out_specs=(VM,) * 6,
        scratch_shapes=[
            vm((rows, width + 128), BF),
            vm((4, capacity, width), BF),
            vm((4, capacity, width), BF),
            vm((4, 8, capacity), F32),
            vm((4, 8, capacity), F32),
            vm((nz, part, 2 * width), BF),
            vm((nz, part, 2 * width), BF),
            vm((4, capacity, width), BF),
            vm((3 * capacity, width), F32),
            vm((3 * capacity, width), F32),
            vm((4, capacity, width), BF),
            vm((4, 8, capacity), F32),
            vm((nz, part, 2 * width), BF),
            vm((nz, part, 2 * width), BF),
            vm((4, capacity, width), BF),
            dma((2 + nz,)),
        ]
        + two(4) + two(nz) + two(4) + two(4) + two(4) + two(4) + two(nz) + two(nz - 1) + two(nz - 1),
        compiler_params=params(cid),
        name="experts",
    )(x, attended, whole, places_row, places_col, raw, near)


PARTS = 4


def finish_kernel(
    prompt, nz, capacity, xs_ref, lse_ref, w_ref, seg_ref, hidden_ref, probs_ref, places_ref,
    dot_ref, qkv_hbm, mixed_hbm, gin_ref, res_ref, cot_ref, att_ref, part_ref,
    out_ref, dx_ref, din_out, dout_out, droute_out, dgains_out, dw_all,
    gh, gatt, got_res, qkv_ref, mixed_ref, grad, qm, dom, kt, dqt, dcat, norm_t, sums, got_c, got_x, got_z, mine, fin, got_f, total,
    send_dx, got_dx, own_gn, stage, dw_sum, ahead, got_up, got_down,
    local, send_r, recv_r, send_g, recv_g, send_c, recv_c, send_x, recv_x, send_z, recv_z, send_d, recv_d, send_f, recv_f,
    send_a, recv_a, send_b, recv_b, send_u, recv_u, send_l, recv_l, send_v, recv_v, send_h, recv_h, send_k, recv_k,
):
    dp, sq, z, x, core = place()
    rows, width = gatt.shape
    half = width // 2
    pairs = half // 128
    shard = width // nz
    part = shard // 4
    own_cols = 3 * half
    lead = own_cols + 128
    chip = x * 2 + sq
    chip_x, chip_y, chip_d = (1 - x) * 2 + sq, x * 2 + 1 - sq, (1 - x) * 2 + 1 - sq
    sibling = (x * 2 + 1 - core, sq, z)
    partner = (dp, 1 - sq, z)
    across = ((1 - x) * 2 + core, sq, z)
    others = [(dp, sq, lax.rem(z + d, nz)) for d in range(1, nz)]
    base = pl.multiple_of(sq * rows, rows)
    there = pl.multiple_of((1 - sq) * rows, rows)
    corner = [flip_chip(x, sq, *f) for f in SOURCES]
    plane = [(px * 2 + core, py, z) for px, py in corner]
    experts_of = [px * 2 + py for px, py in corner]
    greet([sibling] + [plane[j] for j in AWAY] + others)

    quarter = stage.shape[1]

    def rows_of(k):
        return pl.ds(k * quarter, quarter)

    def hop(k, t, up, src):
        to = lax.rem(z + 1, nz) if up else lax.rem(z + nz - 1, nz)
        got, send, recv = (got_up, send_u, recv_u) if up else (got_down, send_l, recv_l)
        return remote(src, got.at[k, t - 1 if up else t], send.at[k, t], recv.at[k, t], (dp, sq, to))

    def legs(slot):
        ups = (True, slot, list(range(nz - 1, slot, -1)))
        downs = (False, nz - 1 - slot, list(range(0, nz - 1 - slot)))
        return ups, downs

    def line_slot(k, slot):
        for up, sender, zones in legs(slot):

            @pl.when(z == sender)
            def _(up=up, zones=zones):
                if slot == 0:
                    for t in zones:
                        hop(k, t, up, part_ref.at[t, rows_of(k)]).start()
                    return
                loads = [
                    pltpu.make_async_copy(part_ref.at[t, rows_of(k)], stage.at[i], local.at[i])
                    for i, t in enumerate(zones)
                ]
                for c in loads:
                    c.start()
                for i, t in enumerate(zones):
                    to = ahead.at[k % 2, i if slot == 1 else 2]
                    if k > 1:
                        hop(k - 2, t, up, to).wait_send()
                    hop(k, t, up, to).wait_recv()
                    loads[i].wait()
                    got = got_up[k, t - 1] if up else got_down[k, t]
                    to[...] = (stage[i].astype(F32) + got.astype(F32)).astype(BF)
                    hop(k, t, up, to).start()

    def line_end():
        for slot in range(nz - 1):
            for up, sender, zones in legs(slot):

                @pl.when(z == sender)
                def _(up=up, zones=zones, slot=slot):
                    for k in range(PARTS) if slot == 0 else range(PARTS - 2, PARTS):
                        for i, t in enumerate(zones):
                            src = part_ref.at[t, rows_of(k)] if slot == 0 else ahead.at[k % 2, i if slot == 1 else 2]
                            hop(k, t, up, src).wait_send()

    def share(k, ch, send, recv, peer, own=False):
        at = dw_all.at[core, ch, pl.ds(k * quarter, quarter)]
        return remote(dw_sum.at[k] if own else at, at, send, recv, peer)

    def keep(k):
        return pltpu.make_async_copy(
            dw_sum.at[k], dw_all.at[core, chip, pl.ds(k * quarter, quarter)], local.at[nz + k]
        )

    def sum_part(k):
        own = pltpu.make_async_copy(part_ref.at[z, rows_of(k)], stage.at[2], local.at[2])
        own.start()
        above_zero, below_top = z > 0, z < nz - 1

        @pl.when(above_zero)
        def _():
            hop(k, z, True, ahead.at[0, 0]).wait_recv()
            stage[0] = got_up[k, z - 1]

        @pl.when(below_top)
        def _():
            hop(k, z, False, ahead.at[0, 0]).wait_recv()
            stage[1] = got_down[k, z]

        own.wait()
        acc = stage[2].astype(F32)
        acc = acc + jnp.where(above_zero, stage[0].astype(F32), 0.0)
        acc = acc + jnp.where(below_top, stage[1].astype(F32), 0.0)
        dw_sum[k] = acc.astype(BF)
        share(k, chip, send_v.at[k], recv_v.at[k], partner, True).start()
        share(k, chip, send_h.at[k, 0], recv_h.at[k, 0], across, True).start()
        share(k, chip, send_k.at[k, 0], recv_k.at[k, 0], sibling, True).start()
        keep(k).start()

    def pass_part(k):
        share(k, chip_y, send_v.at[k], recv_v.at[k], partner).wait_recv()
        share(k, chip_y, send_h.at[k, 1], recv_h.at[k, 1], across).start()
        share(k, chip_y, send_k.at[k, 1], recv_k.at[k, 1], sibling).start()

    def last_part(k):
        share(k, chip_x, send_h.at[k, 0], recv_h.at[k, 0], across).wait_recv()
        share(k, chip_x, send_k.at[k, 2], recv_k.at[k, 2], sibling).start()
        share(k, chip_d, send_h.at[k, 1], recv_h.at[k, 1], across).wait_recv()
        share(k, chip_d, send_k.at[k, 3], recv_k.at[k, 3], sibling).start()

    others_of = [chip, chip_y, chip_x, chip_d]

    def end_parts():
        for k in range(PARTS):
            for i in range(4):
                at = dw_all.at[1 - core, others_of[i], rows_of(k)]
                remote(at, at, send_k.at[k, i], recv_k.at[k, i], sibling).wait_recv()
                share(k, others_of[i], send_k.at[k, i], recv_k.at[k, i], sibling, i == 0).wait_send()
            share(k, chip, send_v.at[k], recv_v.at[k], partner, True).wait_send()
            share(k, chip, send_h.at[k, 0], recv_h.at[k, 0], across, True).wait_send()
            share(k, chip_y, send_h.at[k, 1], recv_h.at[k, 1], across).wait_send()
            keep(k).wait()
        line_end()

    spans = [((pairs - 1) * 384, lead), (lead, lead + width)] + [(p * 384, (p + 1) * 384) for p in range(pairs - 1)]
    groups = [pl.ds(lo, hi - lo) for lo, hi in spans]
    order = [lax.rem(z + d, nz) for d in range(1, nz + 1)]

    def piece(zz, px, co):
        return pl.ds(pl.multiple_of(zz * shard + (px * 2 + co) * part, part), part)

    def to_core(g, n, i):
        src = sums.at[piece(order[n], (1 - x, x)[i], 1 - core), groups[g]]
        return remote(src, got_c.at[n, i, :, groups[g]], send_c.at[g, n, i], recv_c.at[g, n, i], sibling)

    def to_x(g, n):
        src = sums.at[piece(order[n], 1 - x, core), groups[g]]
        return remote(src, got_x.at[n, :, groups[g]], send_x.at[g, n], recv_x.at[g, n], across)

    def to_z(g, n):
        return remote(
            mine.at[n, :, groups[g]], got_z.at[n, :, groups[g]], send_z.at[g, n], recv_z.at[g, n], others[n]
        )

    def cols_of(g):
        return slice(*spans[g])

    def reduce_core(g, n):
        cols = cols_of(g)
        for i in range(2):
            to_core(g, n, i).wait_recv()
            at = piece(order[n], (1 - x, x)[i], core)
            sums[at, cols] = (sums[at, cols].astype(F32) + got_c[n, i, :, cols].astype(F32)).astype(BF)
            if i == 0:
                to_x(g, n).start()

    def reduce_x(g, n):
        cols = cols_of(g)
        to_x(g, n).wait_recv()
        acc = sums[piece(order[n], x, core), cols].astype(F32) + got_x[n, :, cols].astype(F32)
        if n < nz - 1:
            mine[n, :, cols] = acc.astype(BF)
            to_z(g, n).start()
        return acc

    def reduce_z(g, acc):
        cols = cols_of(g)
        for n in range(nz - 1):
            to_z(g, n).wait_recv()
            acc = acc + got_z[n, :, cols].astype(F32)
        fin[:, cols] = acc.astype(BF)

    def pair_loads(p):
        return (
            pltpu.make_async_copy(qkv_hbm.at[p], qkv_ref, local.at[nz + PARTS]),
            pltpu.make_async_copy(mixed_hbm.at[p], mixed_ref, local.at[nz + PARTS + 1]),
        )

    for c in pair_loads(0):
        c.start()
    line_slot(0, 0)
    fetch = [pltpu.make_async_copy(gin_ref.at[j], dcat.at[pl.ds(j * capacity, capacity), 0:width], local.at[j]) for j in range(4)]
    fetch.append(pltpu.make_async_copy(cot_ref, send_dx, local.at[4]))
    fetch.append(pltpu.make_async_copy(att_ref, norm_t.at[:, 0:rows], local.at[5]))
    fetch.append(pltpu.make_async_copy(res_ref.at[OWN], got_res.at[OWN], local.at[6]))
    for c in fetch:
        c.start()
    results = {j: remote(res_ref.at[j], got_res.at[j], send_r.at[j], recv_r.at[j], plane[j]) for j in AWAY}
    for j in range(OWN):
        results[j].start()
    for c in fetch:
        c.wait()
    hidden = hidden_ref[...]
    probs = probs_ref[...]
    small = w_ref[:, own_cols:lead]
    gain_two = small.astype(F32).T[EXPERTS + 1 : EXPERTS + 2, :]
    lane = iota(probs.shape, 1)
    back = None
    grad_probs = jnp.zeros_like(probs)
    for j in range(4):
        pick = hot_cols(pick_col(places_ref[...], experts_of[j]), capacity)
        add = nn(pick, dcat[j * capacity : (j + 1) * capacity, 0:width])
        back = add if back is None else back + add
        inner = jnp.sum(pick.astype(F32) * dot_ref[j][0:1, :], axis=1, keepdims=True)
        grad_probs = jnp.where(lane == experts_of[j], inner, grad_probs)
    mixed = jnp.sum(probs * grad_probs, axis=1, keepdims=True)
    low = (probs * (grad_probs - mixed)).astype(BF)
    r_two = lax.rsqrt(jnp.mean(hidden * hidden, axis=1, keepdims=True) + EPSILON)
    h_norm = hidden * r_two
    routed = (h_norm * gain_two).astype(BF)
    grad_routed = back + nt(low, small)
    dg_two = jnp.sum(grad_routed * h_norm, axis=0, keepdims=True)
    u = grad_routed * gain_two
    grad_hidden = send_dx[...].astype(F32) + r_two * (
        u - h_norm * jnp.mean(u * h_norm, axis=1, keepdims=True)
    )
    gh[...] = grad_hidden
    hid_low = grad_hidden.astype(BF)
    gatt[...] = nt(hid_low, w_ref[:, lead:]).astype(BF)

    def give(p, to):
        return remote(
            gatt.at[:, pl.ds(al((1 - sq) * half + p * 128), 128)],
            grad.at[p, pl.ds(to, rows)],
            send_g.at[p],
            recv_g.at[p],
            partner,
        )

    for p in range(pairs):
        give(p, base).start()
    line_slot(1, 0)
    for p in range(pairs):
        grad[p, pl.ds(base, rows), :] = gatt[:, pl.ds(al(sq * half + p * 128), 128)]
    d_route = tn(routed, low)
    sums[:, cols_of(1)] = tn(norm_t[:, 0:rows], hid_low).astype(BF)
    for n in range(nz):
        for i in range(2):
            to_core(1, n, i).start()
    seg_row, seg_col = eighth(seg_ref[...], prompt)
    gain = w_ref[:, own_cols:lead].astype(F32).T[EXPERTS : EXPERTS + 1, :]

    def norm_of(at):
        xf = xs_ref[at, :].astype(F32)
        r_one = lax.rsqrt(jnp.mean(xf * xf, axis=1, keepdims=True) + EPSILON)
        return xf * r_one, r_one

    for i in range(2):
        at = slice(i * rows, (i + 1) * rows)
        norm_t[:, at] = (norm_of(at)[0] * gain).astype(BF).T

    line_slot(0, 1)
    def weight_grad(g, p):
        cols = slice(p * 384, (p + 1) * 384)
        for n in range(nz):
            zone = pl.ds(pl.multiple_of(order[n] * shard, shard), shard)
            sums[zone, cols] = nn(norm_t[zone, :], dcat[:, cols]).astype(BF)
            for i in range(2):
                to_core(g, n, i).start()

    blocks = 2 * rows // QB
    scale = HEAD_DIM ** (-0.5)
    zero = jnp.zeros((), BF)

    @pl.loop(0, pairs)
    def _(p):
        give(p, there).wait_recv()
        for c in pair_loads(p):
            c.wait()
        kt[...] = qkv_ref[1].T
        prod = (grad[p].astype(F32) * mixed_ref[...].astype(F32)).T
        delta = []
        for h in range(2):
            lanes = iota((1, 128), 1) // HEAD_DIM == h
            qm[h] = jnp.where(lanes, qkv_ref[0], zero) * jnp.asarray(scale, BF)
            dom[h] = jnp.where(lanes, grad[p], zero)
            low = h * HEAD_DIM
            delta.append(jnp.sum(prod[low : low + HEAD_DIM, :], axis=0, keepdims=True))
        for j in range(blocks):
            keys = slice(j * QB, (j + 1) * QB)
            k, v = qkv_ref[1, keys, :], qkv_ref[2, keys, :]
            dk = dv = None
            for i in range(j, blocks):
                at = slice(i * QB, (i + 1) * QB)
                mask = allowed_tile(j, i, prompt, seg_col, seg_row)
                for h in range(2):
                    s = nt(k, qm[h, at, :])
                    dpr = nt(v, dom[h, at, :])
                    pr = jnp.exp2(s * LOG2E - lse_ref[p, h : h + 1, at])
                    if mask is not None:
                        pr = jnp.where(mask, pr, 0.0)
                    ds = (pr * (dpr - delta[h][:, at])).astype(BF)
                    a = nn(pr.astype(BF), dom[h, at, :])
                    b = nn(ds, qm[h, at, :])
                    c = nn(kt[h * HEAD_DIM : (h + 1) * HEAD_DIM, keys], ds)
                    dv = a if dv is None else dv + a
                    dk = b if dk is None else dk + b
                    to = slice(h * HEAD_DIM, (h + 1) * HEAD_DIM)
                    dqt[to, at] = c if j == 0 else dqt[to, at] + c
            dcat[keys, pl.ds(al(p * 384 + 128), 128)] = dk.astype(BF)
            dcat[keys, pl.ds(al(p * 384 + 256), 128)] = dv.astype(BF)
        dcat[:, pl.ds(al(p * 384), 128)] = (dqt[...] * scale).T.astype(BF)

        @pl.when(p < pairs - 1)
        def _():
            for c in pair_loads(p + 1):
                c.start()

        @pl.when(p == 0)
        def _():
            weight_grad(2, 0)
            line_slot(2, 0)
            results[3].start()
            line_slot(0, 2)
            for n in range(nz):
                reduce_core(1, n)

        @pl.when(p == 1)
        def _():
            weight_grad(3, 1)
            line_slot(3, 0)
            line_slot(1, 1)
            sum_part(0)
            for n in range(nz - 1):
                reduce_x(1, n)
            for n in range(nz):
                reduce_core(2, n)

        @pl.when(p == 2)
        def _():
            line_slot(1, 2)
            line_slot(2, 1)
            pass_part(0)
            for n in range(nz):
                reduce_core(3, n)
            for n in range(nz - 1):
                reduce_x(2, n)

    partial = nt(dcat[pl.ds(there, rows), :], w_ref[:, 0:own_cols])
    send_dx[...] = partial.astype(BF)
    to_dx = remote(send_dx, got_dx, send_d, recv_d, partner)
    to_dx.start()
    dg_one = jnp.sum(partial * norm_of(pl.ds(there, rows))[0], axis=0, keepdims=True)
    partial = nt(dcat[pl.ds(base, rows), :], w_ref[:, 0:own_cols])
    own_gn[...] = partial
    dg_one = dg_one + jnp.sum(partial * norm_of(pl.ds(base, rows))[0], axis=0, keepdims=True)
    stacked = jnp.concatenate([dg_one, dg_two, jnp.zeros((126, width), F32)], axis=0).T
    lane = iota((1, 128), 1)
    small = jnp.where(lane < EXPERTS, d_route, 0.0)
    for i in range(2):
        small = jnp.where(lane == EXPERTS + i, stacked[:, i : i + 1], small)
    sums[:, own_cols:lead] = small.astype(BF)
    weight_grad(0, pairs - 1)
    reduce_core(0, 0)
    for n in range(1, nz):
        reduce_core(0, n)
        if n == 1:
            line_slot(2, 2)
            sum_part(1)
        reduce_x(0, n - 1)
    for n in range(nz - 1):
        reduce_x(3, n)
    line_slot(3, 1)
    last_part(0)
    pass_part(1)
    for g in (1, 2):
        reduce_z(g, reduce_x(g, nz - 1))
    total_out = hidden_ref[...]
    for j in (OWN,) + AWAY:
        if j != OWN:
            results[j].wait_recv()
        pick = hot_cols(pick_col(places_ref[...], experts_of[j]), capacity)
        total_out = total_out + pick_col(probs_ref[...], experts_of[j]) * nn(pick, got_res[j])
    out_ref[...] = total_out.astype(BF)
    sum_part(2)
    line_slot(3, 2)
    reduce_z(3, reduce_x(3, nz - 1))
    reduce_z(0, reduce_x(0, nz - 1))
    to_f = remote(fin, got_f, send_f, recv_f, partner)
    to_f.start()
    to_dx.wait_recv()
    grad_n = own_gn[...] + got_dx[...].astype(F32)
    x_norm, r_one = norm_of(pl.ds(base, rows))
    u = grad_n * gain
    dx = gh[...] + r_one * (u - x_norm * jnp.mean(u * x_norm, axis=1, keepdims=True))
    dx_ref[...] = dx.astype(BF)
    last_part(1)
    pass_part(2)
    to_f.wait_recv()

    def spot(px, co):
        return pl.ds(pl.multiple_of((px * 2 + co) * part, part), part)

    here = spot(x, core)
    for p in range(pairs):
        for i in range(3):
            cols = slice((3 * p + i) * 128, (3 * p + i + 1) * 128)
            total[here, pl.ds(al(i * width + sq * half + p * 128), 128)] = fin[:, cols]
            total[here, pl.ds(al(i * width + (1 - sq) * half + p * 128), 128)] = got_f[:, cols]
    total[here, 3 * width :] = (fin[:, own_cols:].astype(F32) + got_f[:, own_cols:].astype(F32)).astype(BF)

    def pass_on(px, co, send, recv, peer):
        return remote(total.at[spot(px, co)], total.at[spot(px, co)], send, recv, peer)

    pass_on(x, core, send_a, recv_a, across).start()
    pass_on(x, core, send_b.at[0], recv_b.at[0], sibling).start()
    sum_part(3)
    last_part(2)
    pass_part(3)
    pass_on(1 - x, core, send_a, recv_a, across).wait_recv()
    pass_on(1 - x, core, send_b.at[1], recv_b.at[1], sibling).start()
    pass_on(x, 1 - core, send_b.at[0], recv_b.at[0], sibling).wait_recv()
    pass_on(1 - x, 1 - core, send_b.at[1], recv_b.at[1], sibling).wait_recv()
    din_out[...] = total[:, 0 : 3 * width].astype(F32)
    small = total[:, 3 * width : 3 * width + 128].astype(F32)
    droute_out[...] = small[:, 0:EXPERTS]
    dgains_out[...] = small[:, EXPERTS : EXPERTS + 2]
    dout_out[...] = total[:, 3 * width + 128 :].astype(F32)
    last_part(3)
    end_parts()
    for c in results.values():
        c.wait_send()
    pass_on(x, core, send_a, recv_a, across).wait_send()
    pass_on(x, core, send_b.at[0], recv_b.at[0], sibling).wait_send()
    pass_on(1 - x, core, send_b.at[1], recv_b.at[1], sibling).wait_send()
    to_f.wait_send()
    to_dx.wait_send()
    for g in range(len(spans)):
        for n in range(nz):
            for i in range(2):
                to_core(g, n, i).wait_send()
            to_x(g, n).wait_send()
            if n < nz - 1:
                to_z(g, n).wait_send()
    for p in range(pairs):
        give(p, base).wait_send()


def finish(
    xs, qkv, mixed, lse, whole, segments, hidden, probs, places, inner, gin, res, cot, attended, dw_half,
    prompt, nz, capacity, cid,
):
    rows, width = cot.shape
    pairs = width // 256
    cols = whole.shape[1]
    shard = width // nz
    part = shard // 4
    group = 2 * rows
    deep = dw_half.shape[1]
    quarter = (deep // PARTS, dw_half.shape[2])
    dma = pltpu.SemaphoreType.DMA
    two = lambda *shape: [dma(shape), dma(shape)]
    vm = pltpu.VMEM
    return pl.pallas_call(
        functools.partial(finish_kernel, prompt, nz, capacity),
        out_shape=(
            sds((rows, width), BF),
            sds((rows, width), BF),
            sds((shard, 3 * width), F32),
            sds((shard, width), F32),
            sds((shard, EXPERTS), F32),
            sds((shard, 2), F32),
            sds((2, 4) + dw_half.shape[1:], BF),
        ),
        in_specs=[VM] * 8 + [ANY] * 7,
        out_specs=(VM,) * 6 + (ANY,),
        scratch_shapes=[
            vm((rows, width), F32),
            vm((rows, width), BF),
            vm((4, capacity, width), BF),
            vm((3, group, 128), BF),
            vm((group, 128), BF),
            vm((pairs, group, 128), BF),
            vm((2, group, 128), BF),
            vm((2, group, 128), BF),
            vm((128, group), BF),
            vm((128, group), F32),
            vm((group, 3 * width // 2), BF),
            vm((width, group), BF),
            vm((width, cols), BF),
            vm((nz, 2, part, cols), BF),
            vm((nz, part, cols), BF),
            vm((nz - 1, part, cols), BF),
            vm((nz - 1, part, cols), BF),
            vm((part, cols), BF),
            vm((part, cols), BF),
            vm((shard, 4 * width + 128), BF),
            vm((rows, width), BF),
            vm((rows, width), BF),
            vm((rows, width), F32),
            vm((nz,) + quarter, BF),
            vm((PARTS,) + quarter, BF),
            vm((2, 3) + quarter, BF),
            vm((PARTS, nz - 1) + quarter, BF),
            vm((PARTS, nz - 1) + quarter, BF),
            dma((nz + PARTS + 2,)),
        ]
        + two(4) + two(pairs) + two(pairs + 1, nz, 2) + two(pairs + 1, nz) + two(pairs + 1, nz - 1) + two() + two() + two() + two(2)
        + two(PARTS, nz) + two(PARTS, nz) + two(PARTS) + two(PARTS, 2) + two(PARTS, 4),
        compiler_params=params(cid),
        name="finish",
    )(xs, lse, whole, segments, hidden, probs, places, inner, qkv, mixed, gin, res, cot, attended, dw_half)


def spread_kernel(in_ref, out_ref):
    for e in range(EXPERTS):
        out_ref[:, e, :] = in_ref[e].astype(F32)


def spread_experts(parts):
    cores, experts_, r, k = parts.shape
    block = r // 2
    return pl.pallas_call(
        spread_kernel,
        grid=(cores, r // block),
        out_shape=sds((cores * r, experts_, k), F32),
        in_specs=[pl.BlockSpec((None, experts_, block, k), lambda c, i: (c, 0, i, 0))],
        out_specs=pl.BlockSpec((block, experts_, k), lambda c, i: (c * (r // block) + i, 0, 0)),
        compiler_params=params(),
        name="spread",
    )(parts)


def shards(tokens, attn_in, attn_out, router, gains, expert_w, expert_ids, segments, cotangent):
    x = tokens[0]
    cot = cotangent[0]
    rows, width = x.shape
    nz = lax.axis_size("fsdp")
    group = 2 * rows
    prompt = group - segments.shape[1]
    capacity = 2 * rows // EXPERTS
    dp, sq = lax.axis_index("dp"), lax.axis_index("seq")
    core = lax.rem(dp, 2)
    mine = (dp // 2) * 2 + sq

    part = expert_w.shape[0] // 2
    piece = lax.dynamic_slice(expert_w, (core * part, mine, 0), (part, 1, 2 * width))[:, 0]
    xs, whole, qkv, mixed, lse, attended, raw, places_row, places_col, near = begin(
        x, attn_in, attn_out, router, gains, segments, expert_ids[0], cot, piece, prompt, nz, capacity, 0
    )
    hidden, probs, gin, res, inner, dw_half = experts(
        x, attended, whole, places_row, places_col, raw, near, capacity, nz, 1
    )
    block_out, d_tokens, d_in, d_out, d_route, d_gains, dw_all = finish(
        xs, qkv, mixed, lse, whole, segments, hidden, probs, places_col, inner, gin, res, cot, attended, dw_half,
        prompt, nz, capacity, 2,
    )
    d_expert = spread_experts(dw_all)
    return (
        block_out[None],
        d_tokens[None],
        d_in,
        d_out,
        d_route,
        d_gains,
        d_expert,
    )


def route(choose, capacity, experts_count):
    pair_expert = choose.reshape(-1)
    one_hot = (pair_expert[:, None] == jnp.arange(experts_count, dtype=jnp.int32)[None, :]).astype(
        jnp.int32
    )
    before = jnp.cumsum(one_hot, axis=0) - one_hot
    place = jnp.sum(before * one_hot, axis=1)
    kept = place < capacity
    slots = jnp.where(kept, pair_expert * capacity + place, experts_count * capacity)
    pair_count = pair_expert.shape[0]
    pair_of = (
        jnp.zeros((experts_count * capacity + 1,), jnp.int32)
        .at[slots]
        .set(jnp.arange(pair_count, dtype=jnp.int32))
    )
    filled = (
        jnp.zeros((experts_count * capacity + 1,), jnp.int32)
        .at[slots]
        .set(jnp.ones((pair_count,), jnp.int32))
    )
    return (slots, kept, pair_of[:-1], filled[:-1] > 0)


def expert_pre(expert_in, piece):
    width = piece.shape[2] // 2
    return jnp.einsum(
        "ecd,fed->ecf", expert_in, piece[:, :, :width], preferred_element_type=jnp.float32
    )


def expert_out(activity, piece):
    width = piece.shape[2] // 2
    return jnp.einsum(
        "ecf,fed->ecd", activity, piece[:, :, width:], preferred_element_type=jnp.float32
    )


def expert_back(grad_result, pre_rows, piece):
    width = piece.shape[2] // 2
    grad_act = jnp.einsum(
        "ecd,fed->ecf", grad_result, piece[:, :, width:], preferred_element_type=jnp.float32
    )
    grad_pre = jax.vjp(jax.nn.gelu, pre_rows)[1](grad_act)[0].astype(jnp.bfloat16)
    grad_in = jnp.einsum(
        "ecf,fed->ecd", grad_pre, piece[:, :, :width], preferred_element_type=jnp.float32
    )
    return (grad_pre, grad_in)


def general_shards(tokens, attn_in, attn_out, router, gains, expert_w, expert_ids, segments, cotangent):
    x_rows = tokens[0].astype(jnp.float32)
    tok_rows = x_rows.shape[0]
    width = x_rows.shape[1]
    seq_count = lax.axis_size("seq")
    scale = HEAD_DIM ** (-0.5)
    w_qkv, w_proj, w_route, gain_pair = (
        lax.all_gather(attn_in, "fsdp", axis=0, tiled=True),
        lax.all_gather(attn_out, "fsdp", axis=0, tiled=True),
        lax.all_gather(router, "fsdp", axis=0, tiled=True),
        lax.all_gather(gains, "fsdp", axis=0, tiled=True),
    )
    gain_f = gain_pair.astype(jnp.float32)
    r_one = lax.rsqrt(jnp.mean(x_rows * x_rows, axis=-1, keepdims=True) + EPSILON)
    normed_one = x_rows * r_one
    normed_low = (normed_one * gain_f[:, 0]).astype(jnp.bfloat16)
    projected = jnp.dot(normed_low, w_qkv, preferred_element_type=jnp.float32).astype(jnp.bfloat16)
    local_heads = HEADS // seq_count
    head_cols = local_heads * HEAD_DIM
    arrived = lax.all_to_all(
        projected.reshape(tok_rows, 3, seq_count, head_cols),
        "seq",
        split_axis=2,
        concat_axis=0,
        tiled=True,
    )
    group_len = arrived.shape[0]
    queries = arrived[:, 0, 0].reshape(group_len, local_heads, HEAD_DIM)
    keys = arrived[:, 1, 0].reshape(group_len, local_heads, HEAD_DIM)
    values = arrived[:, 2, 0].reshape(group_len, local_heads, HEAD_DIM)
    seg_full = jnp.concatenate([jnp.full((PROMPT,), -1, jnp.int32), segments[0]])
    block = min(512, group_len)
    key_place = jnp.arange(group_len, dtype=jnp.int32)
    begins = jnp.arange(group_len // block, dtype=jnp.int32) * block

    def block_scores(begin):
        query_block = lax.dynamic_slice_in_dim(queries, begin, block, 0)
        query_place = begin + jnp.arange(block, dtype=jnp.int32)
        query_seg = lax.dynamic_slice_in_dim(seg_full, begin, block, 0)
        raw = (
            jnp.einsum("qhd,khd->hqk", query_block, keys, preferred_element_type=jnp.float32)
            * scale
        )
        allowed = (key_place[None, :] <= query_place[:, None]) & (
            (seg_full[None, :] < 0) | (seg_full[None, :] == query_seg[:, None])
        )
        return (jnp.where(allowed[None], raw, NEGATIVE), query_block)

    def forward_block(begin):
        masked, query_block = block_scores(begin)
        row_max = jnp.max(masked, axis=-1, keepdims=True)
        expo = jnp.exp(masked - row_max)
        row_total = jnp.sum(expo, axis=-1, keepdims=True)
        probs = expo / row_total
        mixed_block = jnp.einsum(
            "hqk,khd->qhd", probs.astype(jnp.bfloat16), values, preferred_element_type=jnp.float32
        )
        return (mixed_block.astype(jnp.bfloat16), (row_max + jnp.log(row_total))[:, :, 0])

    mixed_blocks, log_totals = lax.map(forward_block, begins)
    mixed_heads = mixed_blocks.reshape(group_len, 1, head_cols)
    returned = lax.all_to_all(mixed_heads, "seq", split_axis=0, concat_axis=1, tiled=True)
    attended = returned.reshape(tok_rows, width)
    hidden = x_rows + jnp.dot(attended, w_proj, preferred_element_type=jnp.float32)
    r_two = lax.rsqrt(jnp.mean(hidden * hidden, axis=-1, keepdims=True) + EPSILON)
    normed_two = hidden * r_two
    routed_low = (normed_two * gain_f[:, 1]).astype(jnp.bfloat16)
    logits = jnp.dot(routed_low, w_route, preferred_element_type=jnp.float32)
    probs_r = jax.nn.softmax(logits, axis=-1)
    choose = expert_ids[0]
    choose_map = (choose[:, :, None] == jnp.arange(EXPERTS, dtype=jnp.int32)[None, None, :]).astype(
        jnp.float32
    )
    gates = jnp.sum(probs_r[:, None, :] * choose_map, axis=-1)
    capacity = 2 * tok_rows // EXPERTS
    slots, kept, pair_of, filled = route(choose, capacity, EXPERTS)
    token_of = pair_of // 2
    expert_in = jnp.where(
        filled[:, None], routed_low[token_of], jnp.zeros((), jnp.bfloat16)
    ).reshape(EXPERTS, capacity, width)
    piece = lax.all_gather(expert_w, "fsdp", axis=0, tiled=True)
    pre_rows = expert_pre(expert_in, piece)
    result = expert_out(jax.nn.gelu(pre_rows).astype(jnp.bfloat16), piece)
    padded = jnp.concatenate(
        [result.reshape(EXPERTS * capacity, width), jnp.zeros((1, width), jnp.float32)], axis=0
    )
    picked = padded[slots].reshape(tok_rows, 2, width)
    kept_f = kept.astype(jnp.float32).reshape(tok_rows, 2)
    weight_pair = gates * kept_f
    block_out = hidden + jnp.sum(weight_pair[..., None] * picked, axis=1)
    grad_out_rows = cotangent[0].astype(jnp.float32)
    grad_gates = kept_f * jnp.sum(grad_out_rows[:, None, :] * picked, axis=-1)
    grad_probs = jnp.sum(grad_gates[:, :, None] * choose_map, axis=1)
    grad_logits = probs_r * (grad_probs - jnp.sum(probs_r * grad_probs, axis=-1, keepdims=True))
    grad_route_w = jnp.dot(routed_low.astype(jnp.float32).T, grad_logits, precision=HIGH)
    grad_routed = jnp.dot(grad_logits, w_route.astype(jnp.float32).T, precision=HIGH)
    scaled = (weight_pair[:, :, None] * grad_out_rows[:, None, :]).reshape(2 * tok_rows, width)
    grad_result = (
        jnp.where(filled[:, None], scaled[pair_of], 0.0)
        .astype(jnp.bfloat16)
        .reshape(EXPERTS, capacity, width)
    )
    piece = lax.all_gather(expert_w, "fsdp", axis=0, tiled=True)
    pre_rows = expert_pre(expert_in, piece)
    act_rows = jax.nn.gelu(pre_rows).astype(jnp.bfloat16)
    grad_pre_rows, grad_in_rows = expert_back(grad_result, pre_rows, piece)
    act_store = act_rows
    pre_rows = grad_pre_rows
    act_rows = act_store
    grad_first = jnp.einsum("ecd,ecf->fed", expert_in, pre_rows, preferred_element_type=jnp.float32)
    grad_second = jnp.einsum(
        "ecf,ecd->fed", act_rows, grad_result, preferred_element_type=jnp.float32
    )
    expert_shard = lax.psum_scatter(
        jnp.concatenate([grad_first, grad_second], axis=2).astype(jnp.bfloat16),
        "fsdp",
        scatter_dimension=0,
        tiled=True,
    )
    padded_in = jnp.concatenate(
        [grad_in_rows.reshape(EXPERTS * capacity, width), jnp.zeros((1, width), jnp.float32)],
        axis=0,
    )
    grad_routed = grad_routed + jnp.sum(padded_in[slots].reshape(tok_rows, 2, width), axis=1)
    grad_gain_two = jnp.sum(grad_routed * normed_two, axis=0)
    scaled_two = grad_routed * gain_f[:, 1]
    grad_hidden = grad_out_rows + r_two * (
        scaled_two - normed_two * jnp.mean(scaled_two * normed_two, axis=-1, keepdims=True)
    )
    hid_low = grad_hidden.astype(jnp.bfloat16)
    grad_proj_w = jnp.dot(attended.T, hid_low, preferred_element_type=jnp.float32)
    grad_attended = jnp.dot(hid_low, w_proj.T, preferred_element_type=jnp.float32).astype(
        jnp.bfloat16
    )
    grad_heads = lax.all_to_all(
        grad_attended.reshape(tok_rows, seq_count, head_cols),
        "seq",
        split_axis=1,
        concat_axis=0,
        tiled=True,
    )
    grad_mixed = grad_heads.reshape(group_len, local_heads, HEAD_DIM)

    def back_block(carry, inputs):
        begin, log_rows = inputs
        masked, query_block = block_scores(begin)
        probs = jnp.exp(masked - log_rows[:, :, None])
        grad_block = lax.dynamic_slice_in_dim(grad_mixed, begin, block, 0)
        grad_p = jnp.einsum("qhd,khd->hqk", grad_block, values, preferred_element_type=jnp.float32)
        inner = jnp.sum(probs * grad_p, axis=-1, keepdims=True)
        grad_scores = (probs * (grad_p - inner)).astype(jnp.bfloat16)
        grad_query = (
            jnp.einsum("hqk,khd->qhd", grad_scores, keys, preferred_element_type=jnp.float32)
            * scale
        )
        grad_key = (
            carry[0]
            + jnp.einsum(
                "hqk,qhd->khd", grad_scores, query_block, preferred_element_type=jnp.float32
            )
            * scale
        )
        grad_value = carry[1] + jnp.einsum(
            "hqk,qhd->khd",
            probs.astype(jnp.bfloat16),
            grad_block,
            preferred_element_type=jnp.float32,
        )
        return ((grad_key, grad_value), grad_query)

    zero_heads = jnp.zeros((group_len, local_heads, HEAD_DIM), jnp.float32)
    (grad_keys, grad_values), grad_queries = lax.scan(
        back_block, (zero_heads, zero_heads), (begins, log_totals)
    )
    stacked = jnp.stack(
        [
            grad_queries.reshape(group_len, head_cols),
            grad_keys.reshape(group_len, head_cols),
            grad_values.reshape(group_len, head_cols),
        ],
        axis=1,
    )
    stacked = stacked.astype(jnp.bfloat16).reshape(group_len, 3, 1, head_cols)
    grad_back = lax.all_to_all(stacked, "seq", split_axis=0, concat_axis=2, tiled=True)
    grad_proj_rows = grad_back.reshape(tok_rows, 3 * width)
    grad_qkv_w = jnp.dot(normed_low.T, grad_proj_rows, preferred_element_type=jnp.float32)
    grad_normed = jnp.dot(grad_proj_rows, w_qkv.T, preferred_element_type=jnp.float32)
    grad_gain_one = jnp.sum(grad_normed * normed_one, axis=0)
    scaled_one = grad_normed * gain_f[:, 0]
    grad_x = grad_hidden + r_one * (
        scaled_one - normed_one * jnp.mean(scaled_one * normed_one, axis=-1, keepdims=True)
    )
    grad_gains = jnp.stack([grad_gain_one, grad_gain_two], axis=1)
    shard_qkv, shard_proj, shard_route, shard_gains = (
        lax.psum_scatter(
            grad_qkv_w.astype(jnp.bfloat16), "fsdp", scatter_dimension=0, tiled=True
        ).astype(jnp.float32),
        lax.psum_scatter(
            grad_proj_w.astype(jnp.bfloat16), "fsdp", scatter_dimension=0, tiled=True
        ).astype(jnp.float32),
        lax.psum_scatter(
            grad_route_w.astype(jnp.bfloat16), "fsdp", scatter_dimension=0, tiled=True
        ).astype(jnp.float32),
        lax.psum_scatter(
            grad_gains.astype(jnp.bfloat16), "fsdp", scatter_dimension=0, tiled=True
        ).astype(jnp.float32),
    )
    part_qkv, part_proj, part_expert = (
        lax.psum_scatter(
            shard_qkv.astype(jnp.bfloat16), ("dp", "seq"), scatter_dimension=1, tiled=True
        ).astype(jnp.float32),
        lax.psum_scatter(
            shard_proj.astype(jnp.bfloat16), ("dp", "seq"), scatter_dimension=1, tiled=True
        ).astype(jnp.float32),
        lax.psum_scatter(expert_shard, ("dp", "seq"), scatter_dimension=2, tiled=True).astype(
            jnp.float32
        ),
    )
    summed_qkv, summed_proj, summed_expert = (
        lax.all_gather(part_qkv.astype(jnp.bfloat16), ("dp", "seq"), axis=1, tiled=True).astype(
            part_qkv.dtype
        ),
        lax.all_gather(part_proj.astype(jnp.bfloat16), ("dp", "seq"), axis=1, tiled=True).astype(
            part_proj.dtype
        ),
        lax.all_gather(part_expert.astype(jnp.bfloat16), ("dp", "seq"), axis=2, tiled=True).astype(
            part_expert.dtype
        ),
    )
    summed_route, summed_gains = lax.psum((shard_route, shard_gains), ("dp", "seq"))
    return (
        block_out.astype(jnp.bfloat16)[None],
        grad_x.astype(jnp.bfloat16)[None],
        summed_qkv,
        summed_proj,
        summed_route,
        summed_gains,
        summed_expert,
    )


def fits(mesh):
    return mesh.shape["fsdp"] == 4 and mesh.shape["dp"] == 4 and mesh.shape["seq"] == 2


def solution(mesh):
    body = shards if fits(mesh) else general_shards
    in_specs = (
        P(("dp", "fsdp"), "seq", None),
        P("fsdp", None),
        P("fsdp", None),
        P("fsdp", None),
        P("fsdp", None),
        P("fsdp", None, None),
        P(("dp", "fsdp"), "seq", None),
        P(("dp", "fsdp"), None),
        P(("dp", "fsdp"), "seq", None),
    )
    out_specs = (
        P(("dp", "fsdp"), "seq", None),
        P(("dp", "fsdp"), "seq", None),
        P("fsdp", None),
        P("fsdp", None),
        P("fsdp", None),
        P("fsdp", None),
        P("fsdp", None, None),
    )
    return jax.shard_map(body, mesh=mesh, in_specs=in_specs, out_specs=out_specs, check_vma=False)
```

```python
import functools

import jax
import jax.numpy as jnp
from jax import lax
from jax.experimental import pallas as pl
from jax.experimental.pallas import tpu as pltpu
from jax.sharding import PartitionSpec as P

HEADS = 12
HEAD_DIM = 64
EXPERTS = 4
PROMPT = 1024
EPSILON = 1e-06
NEGATIVE = -1e30
HIGH = lax.Precision.HIGHEST
LOG2E = 1.4426950408889634
BF = jnp.bfloat16
F32 = jnp.float32
MESH = pl.DeviceIdType.MESH
VMEM_LIMIT = 60 << 20
QB = 256
ANY = pl.BlockSpec(memory_space=pl.ANY)
VM = pl.BlockSpec(memory_space=pltpu.VMEM)


def nn(a, b):
    return lax.dot_general(a, b, (((1,), (0,)), ((), ())), preferred_element_type=F32)


def nt(a, b):
    return lax.dot_general(a, b, (((1,), (1,)), ((), ())), preferred_element_type=F32)


def tn(a, b):
    return lax.dot_general(a, b, (((0,), (0,)), ((), ())), preferred_element_type=F32)


def iota(shape, dim):
    return lax.broadcasted_iota(jnp.int32, shape, dim)


def params(cid=None):
    if cid is None:
        return pltpu.CompilerParams(vmem_limit_bytes=VMEM_LIMIT)
    return pltpu.CompilerParams(
        vmem_limit_bytes=VMEM_LIMIT, collective_id=cid, has_side_effects=True
    )


def sds(shape, dtype):
    return jax.ShapeDtypeStruct(shape, dtype)


def place():
    dp, sq, z = lax.axis_index("dp"), lax.axis_index("seq"), lax.axis_index("fsdp")
    return dp, sq, z, dp // 2, lax.rem(dp, 2)


def greet(peers):
    barrier = pltpu.get_barrier_semaphore()
    for peer in peers:
        pl.semaphore_signal(barrier, inc=1, device_id=peer, device_id_type=MESH)
    pl.semaphore_wait(barrier, len(peers))


def remote(src, dst, send, recv, peer):
    return pltpu.make_async_remote_copy(
        src_ref=src, dst_ref=dst, send_sem=send, recv_sem=recv, device_id=peer, device_id_type=MESH
    )


def al(x):
    return pl.multiple_of(x, 128)


def allowed_tile(j, i, prompt, seg_col, seg_row):
    mask = None
    if i == j:
        mask = iota((QB, QB), 0) <= iota((QB, QB), 1)
    if j * QB >= prompt:
        keys, queries = j * QB - prompt, i * QB - prompt
        same = seg_col[keys : keys + QB, :] == seg_row[:, queries : queries + QB]
        mask = same if mask is None else mask & same
    return mask


def flip_chip(x, sq, fx, fy):
    px = 1 - x if fx else x
    py = 1 - sq if fy else sq
    return px, py


SOURCES = ((1, 0), (0, 1), (0, 0), (1, 1))
OWN = 2
AWAY = (0, 1, 3)


class Line:
    def __init__(self, nz, dp, sq, z, sources, target, sems):
        self.nz, self.dp, self.sq, self.z = nz, dp, sq, z
        self.sources, self.target, self.sems = sources, target, sems

    def copy(self, stage, up):
        nz, z = self.nz, self.z
        zone = z - (stage - 1) if up else z + (stage - 1)
        zone = lax.rem(zone + nz, nz)
        to = lax.rem(z + 1, nz) if up else lax.rem(z + nz - 1, nz)
        i = stage - 1
        send, recv = (self.sems[0], self.sems[1]) if up else (self.sems[2], self.sems[3])
        return remote(
            self.sources(stage, zone), self.target.at[zone], send.at[i], recv.at[i], (self.dp, self.sq, to)
        )

    def arrival(self, stage, up):
        nz, z = self.nz, self.z
        zone = lax.rem((z - stage if up else z + stage) + nz, nz)
        to = lax.rem(z + 1, nz) if up else lax.rem(z + nz - 1, nz)
        i = stage - 1
        send, recv = (self.sems[0], self.sems[1]) if up else (self.sems[2], self.sems[3])
        return remote(
            self.sources(stage, zone), self.target.at[zone], send.at[i], recv.at[i], (self.dp, self.sq, to)
        )

    def sends(self, stage, up):
        z, nz = self.z, self.nz
        return (z < nz - 1) & (z >= stage - 1) if up else (z > 0) & (z <= nz - stage)

    def gets(self, stage, up):
        return self.z >= stage if up else self.z <= self.nz - 1 - stage

    def start(self, stage):
        for up in (True, False):

            @pl.when(self.sends(stage, up))
            def _(up=up):
                self.copy(stage, up).start()

    def wait_recv(self, stage):
        for up in (True, False):

            @pl.when(self.gets(stage, up))
            def _(up=up):
                self.arrival(stage, up).wait_recv()

    def wait_send(self, stage):
        for up in (True, False):

            @pl.when(self.sends(stage, up))
            def _(up=up):
                self.copy(stage, up).wait_send()


def eighth(x, prompt):
    row = x.astype(F32)
    col = jnp.broadcast_to(row, (128, row.shape[1])).T[:, 0:1]
    return row, col


def upright(rows, count):
    wide = -(-count // 128) * 128
    few = rows.astype(F32)
    few = jnp.concatenate([few, jnp.zeros((8 - few.shape[0], count), F32)], axis=0)
    if wide > count:
        few = jnp.concatenate([few, jnp.zeros((8, wide - count), F32)], axis=1)
    return few.T[0:count, :]


def begin_kernel(
    prompt, nz, capacity, x_ref, in_ref, out_ref, router_ref, gains_ref, seg_ref, ids_ref, cot_ref, piece_ref,
    xs_ref, w_ref, qkv_ref, mixed_ref, lse_ref, att_ref, raw_ref, row_ref, col_ref, near_ref,
    pack, vt, local, send_t, recv_t, send_z, recv_z, send_p, recv_p, send_c, recv_c, send_o, recv_o, *line_sems,
):
    dp, sq, z, x, core = place()
    rows, width = x_ref.shape
    shard = in_ref.shape[0]
    part = shard // 4
    half = width // 2
    pairs = half // 128
    own_cols = 3 * half
    lead = own_cols + 128
    sibling = (x * 2 + 1 - core, sq, z)
    partner = (dp, 1 - sq, z)
    across = ((1 - x) * 2 + core, sq, z)
    others = [(dp, sq, lax.rem(z + d, nz)) for d in range(1, nz)]
    base = pl.multiple_of(sq * rows, rows)
    there = pl.multiple_of((1 - sq) * rows, rows)
    groups = (pl.ds(0, lead), pl.ds(lead, width))

    packs = [
        pltpu.make_async_copy(
            in_ref.at[:, pl.ds(al(i * width + sq * half + p * 128), 128)],
            pack.at[:, pl.ds((3 * p + i) * 128, 128)],
            local.at[3 * p + i],
        )
        for p in range(pairs)
        for i in range(3)
    ]
    packs.append(pltpu.make_async_copy(out_ref, pack.at[:, groups[1]], local.at[3 * pairs]))
    for c in packs:
        c.start()
    lane = iota((1, 128), 1)
    small = jnp.zeros((shard, 128), F32)
    router_cols, gain_cols = upright(router_ref[...], shard), upright(gains_ref[...], shard)
    for e in range(EXPERTS):
        small = jnp.where(lane == e, router_cols[:, e : e + 1], small)
    for e in range(2):
        small = jnp.where(lane == EXPERTS + e, gain_cols[:, e : e + 1], small)
    pack[:, own_cols:lead] = small.astype(BF)
    greet([sibling, partner, across] + others)
    tokens = remote(x_ref, xs_ref.at[pl.ds(base, rows)], send_t, recv_t, partner)
    tokens.start()
    for c in packs:
        c.wait()

    def at(zs, px, co, g):
        return w_ref.at[pl.ds(pl.multiple_of(zs * shard + (px * 2 + co) * part, part), part), groups[g]]

    def along(d, g):
        src = pack.at[pl.ds(pl.multiple_of((x * 2 + core) * part, part), part), groups[g]]
        return remote(src, at(z, x, core, g), send_z.at[d - 1, g], recv_z.at[d - 1, g], others[d - 1])

    def source(d):
        return lax.rem(z + nz - d, nz)

    def over(d, g, px):
        ref = at(source(d), px, core, g)
        return remote(ref, ref, send_p.at[d - 1, g], recv_p.at[d - 1, g], across)

    def beside(d, g, i, co):
        ref = at(source(d), (x, 1 - x)[i], co, g)
        return remote(ref, ref, send_c.at[d - 1, g, i], recv_c.at[d - 1, g, i], sibling)

    for d in range(1, nz):
        along(d, 0).start()
    own = pltpu.make_async_copy(pack, w_ref.at[pl.ds(pl.multiple_of(z * shard, shard), shard)], local.at[3 * pairs + 1])
    own.start()
    xs_ref[pl.ds(base, rows), :] = x_ref[...]
    ids = upright(ids_ref[...], rows)
    lanes_f = lane.astype(F32)
    chosen = jnp.where((ids[:, 0:1] == lanes_f) | (ids[:, 1:2] == lanes_f), 1.0, 0.0)
    earlier = (iota((rows, rows), 1) < iota((rows, rows), 0)).astype(F32).astype(BF)
    places = jnp.where(chosen > 0, nn(earlier, chosen.astype(BF)), -1.0)
    col_ref[...] = places
    places = places.T[0:8, :]
    row_ref[...] = places

    def gather(g):
        for d in range(1, nz):
            along(d, g).wait_recv()
            over(d, g, x).start()
            beside(d, g, 0, core).start()
        if g == 0:
            for d in range(1, nz):
                along(d, 1).start()
        for d in range(1, nz):
            over(d, g, 1 - x).wait_recv()
            beside(d, g, 1, core).start()

    def gathered(g):
        for d in range(1, nz):
            for i in range(2):
                beside(d, g, i, 1 - core).wait_recv()

    stay = pltpu.make_async_copy(piece_ref, near_ref.at[z], local.at[3 * pairs + 2])
    stay.start()
    line = Line(
        nz, dp, sq, z, lambda stage, zone: piece_ref if stage == 1 else near_ref.at[zone], near_ref, line_sems
    )
    line.start(1)
    gather(0)
    gathered(0)
    own.wait()
    tokens.wait_recv()

    gain = w_ref[:, own_cols:lead].astype(F32).T[EXPERTS : EXPERTS + 1, :]
    xf = xs_ref[...].astype(F32)
    normed = (xf * lax.rsqrt(jnp.mean(xf * xf, axis=1, keepdims=True) + EPSILON) * gain).astype(BF)
    for p in range(pairs):
        got = nn(normed, w_ref[:, p * 384 : (p + 1) * 384]).astype(BF)
        for i in range(3):
            qkv_ref[p, i] = got[:, i * 128 : (i + 1) * 128]

    blocks = 2 * rows // QB
    const = HEAD_DIM ** (-0.5) * LOG2E
    seg_row, seg_col = eighth(seg_ref[...], prompt)

    def back(p, own_side):
        src = mixed_ref.at[p, pl.ds(there, rows)]
        side = sq if own_side else 1 - sq
        return remote(
            src, att_ref.at[:, pl.ds(al(side * half + p * 128), 128)], send_o.at[p], recv_o.at[p], partner
        )

    line.wait_recv(1)
    line.start(2)

    @pl.loop(0, pairs)
    def _(p):
        vt[0:128, :] = qkv_ref[p, 2].T
        vt[128:144, :] = jnp.ones((16, vt.shape[1]), BF)
        for i in range(blocks):
            here = slice(i * QB, (i + 1) * QB)
            both = []
            for h in range(2):
                lanes = iota((1, 128), 1) // HEAD_DIM == h
                q = jnp.where(lanes, qkv_ref[p, 0, here, :], jnp.zeros((), BF))
                tiles = []
                for j in range(i + 1):
                    s = nt(qkv_ref[p, 1, j * QB : (j + 1) * QB, :], q)
                    mask = allowed_tile(j, i, prompt, seg_col, seg_row)
                    if mask is not None:
                        s = jnp.where(mask, s, NEGATIVE)
                    tiles.append(s)
                top = functools.reduce(
                    jnp.maximum, [jnp.max(s, axis=0, keepdims=True) for s in tiles]
                )
                top = top * const
                acc = None
                for j, s in enumerate(tiles):
                    pr = jnp.exp2(s * const - top).astype(BF)
                    add = nn(vt[:, j * QB : (j + 1) * QB], pr)
                    acc = add if acc is None else acc + add
                total = acc[128:129, :]
                lse_ref[p, h : h + 1, here] = top + jnp.log2(total)
                low = h * HEAD_DIM
                both.append(acc[low : low + HEAD_DIM, :] * (1.0 / total))
            mixed_ref[p, here, :] = jnp.concatenate(both, axis=0).T.astype(BF)
        back(p, True).start()
        att_ref[:, pl.ds(al(sq * half + p * 128), 128)] = mixed_ref[p, pl.ds(base, rows), :]

        @pl.when(p == 0)
        def _():
            gather(1)

    for j, (px, py) in enumerate([flip_chip(x, sq, *f) for f in SOURCES]):
        hot = hot_rows(pick_row(row_ref[...], px * 2 + py), capacity)
        raw_ref[j] = nn(hot, cot_ref[...]).astype(BF)
    for p in range(pairs):
        back(p, False).wait_recv()
        back(p, True).wait_send()
    gathered(1)
    tokens.wait_send()
    for g in range(2):
        for d in range(1, nz):
            along(d, g).wait_send()
            over(d, g, x).wait_send()
            for i in range(2):
                beside(d, g, i, core).wait_send()
    line.wait_recv(2)
    line.wait_send(1)
    line.wait_send(2)
    stay.wait()


def begin(x, attn_in, attn_out, router, gains, segments, ids, cot, piece, prompt, nz, capacity, cid):
    rows, width = x.shape
    shard = attn_in.shape[0]
    pairs = width // 256
    cols = 3 * width // 2 + 128 + width
    dma = pltpu.SemaphoreType.DMA
    two = lambda *shape: [dma(shape), dma(shape)]
    return pl.pallas_call(
        functools.partial(begin_kernel, prompt, nz, capacity),
        out_shape=(
            sds((2 * rows, width), BF),
            sds((shard * nz, cols), BF),
            sds((pairs, 3, 2 * rows, 128), BF),
            sds((pairs, 2 * rows, 128), BF),
            sds((pairs, 8, 2 * rows), F32),
            sds((rows, width), BF),
            sds((4, capacity, width), BF),
            sds((8, rows), F32),
            sds((rows, 128), F32),
            sds((nz,) + piece.shape, BF),
        ),
        in_specs=[VM, ANY, ANY, VM, VM, VM, VM, VM, ANY],
        out_specs=(VM,) * 9 + (ANY,),
        scratch_shapes=[
            pltpu.VMEM((shard, cols), BF),
            pltpu.VMEM((144, 2 * rows), BF),
            dma((3 * pairs + 3,)),
        ]
        + two() + two(nz - 1, 2) + two(nz - 1, 2) + two(nz - 1, 2, 2) + two(pairs) + two(2) + two(2),
        compiler_params=params(cid),
        name="begin",
    )(x, attn_in, attn_out, router, gains, segments, ids, cot, piece)


def softmax_lanes(logits):
    live = iota(logits.shape, 1) < EXPERTS
    logits = jnp.where(live, logits, NEGATIVE)
    expo = jnp.where(live, jnp.exp(logits - jnp.max(logits, axis=1, keepdims=True)), 0.0)
    return expo / jnp.sum(expo, axis=1, keepdims=True)


def pick_row(table, e):
    return jnp.sum(jnp.where(iota((8, 1), 0) == e, table, 0.0), axis=0, keepdims=True)


def pick_col(table, e):
    return jnp.sum(jnp.where(iota((1, 128), 1) == e, table, 0.0), axis=1, keepdims=True)


def hot_rows(row, capacity):
    return (row == iota((capacity, 1), 0).astype(F32)).astype(F32).astype(BF)


def hot_cols(col, capacity):
    return (col == iota((1, capacity), 1).astype(F32)).astype(F32).astype(BF)


GELU_A = 0.7978845608028654
GELU_B = GELU_A * 0.044715


def expert_step(x, g, w):
    width = x.shape[1]
    first, second = w[:, :width], w[:, width:]
    pre = nt(x, first)
    back = nt(g, second)
    square = pre * pre
    t = jnp.tanh(pre * (GELU_A + GELU_B * square))
    rise = 0.5 + 0.5 * t
    act = (pre * rise).astype(BF)
    slope = rise + (0.5 * pre) * (1.0 - t * t) * (GELU_A + (3.0 * GELU_B) * square)
    grad_pre = (back * slope).astype(BF)
    return nn(act, second), nn(grad_pre, first), tn(grad_pre, x), tn(act, g)


def experts_kernel(
    capacity, nz, x_ref, att_ref, w_hbm, places_row, places_col, raw_send, near_ref,
    hidden_ref, probs_ref, back_gin, out_res, back_dot, dw_ref,
    wp, send_in, got_in, send_gate, got_gate, own_w, theirs, grad, res_acc, gin_acc, out_gin, out_dot, dw_away, dw_got,
    raw_ref, local, send_x, recv_x, send_w, recv_w, send_i, recv_i, send_t, recv_t, send_r, recv_r, send_d, recv_d, send_v, recv_v, *line_sems,
):
    dp, sq, z, x, core = place()
    rows, width = x_ref.shape
    sibling = (x * 2 + 1 - core, sq, z)
    corner = [flip_chip(x, sq, *f) for f in SOURCES]
    plane = [(px * 2 + core, py, z) for px, py in corner]
    experts_of = [px * 2 + py for px, py in corner]
    beside_z = (dp, sq, z + 1 - 2 * lax.rem(z, 2))
    shift = jnp.where(z >= nz // 2, 1, 0)
    far_zone = jnp.where(z >= nz // 2, 0, nz - 1)
    at_end = (z == 0) | (z == nz - 1)
    near_peers = [sibling] + [plane[j] for j in AWAY]
    barrier = pltpu.get_barrier_semaphore()
    for peer in near_peers:
        pl.semaphore_signal(barrier, inc=1, device_id=peer, device_id_type=MESH)

    @pl.when(at_end)
    def _():
        pl.semaphore_signal(barrier, inc=1, device_id=beside_z, device_id_type=MESH)

    pl.semaphore_wait(barrier, len(near_peers) + jnp.where(at_end, 0, 1))
    line = Line(nz, dp, sq, z, lambda stage, zone: near_ref.at[zone], own_w, line_sems)
    line.start(nz - 1)

    def go_raw(j):
        return remote(raw_send.at[j], raw_ref.at[j], send_x.at[j], recv_x.at[j], plane[j])

    go_raw(0).start()
    go_raw(1).start()

    def weights(slot):
        if slot == nz - 1:
            return remote(own_w.at[far_zone], theirs.at[far_zone], send_w.at[slot], recv_w.at[slot], sibling)
        zone = slot + shift
        return remote(near_ref.at[zone], theirs.at[zone], send_w.at[slot], recv_w.at[slot], sibling)

    lifts = []
    for i in range(nz - 1):
        weights(i).start()
        lifts.append(pltpu.make_async_copy(near_ref.at[i + shift], own_w.at[i + shift], local.at[2 + i]))
    for c in lifts:
        c.start()
    far_lift = pltpu.make_async_copy(near_ref.at[far_zone], own_w.at[far_zone], local.at[1 + nz])

    @pl.when(jnp.logical_not(at_end))
    def _():
        far_lift.start()

    own_raw = pltpu.make_async_copy(raw_send.at[OWN], raw_ref.at[OWN], local.at[1])
    own_raw.start()
    load = pltpu.make_async_copy(w_hbm.at[:, 3 * width // 2 :], wp, local.at[0])
    load.start()
    load.wait()

    hidden = x_ref[...].astype(F32) + nn(att_ref[...], wp[:, 128:])
    hidden_ref[...] = hidden
    r_two = lax.rsqrt(jnp.mean(hidden * hidden, axis=1, keepdims=True) + EPSILON)
    small = wp[:, :128]
    gain = small.astype(F32).T[EXPERTS + 1 : EXPERTS + 2, :]
    routed = (hidden * r_two * gain).astype(BF)
    probs = softmax_lanes(nn(routed, small))
    probs_ref[...] = probs
    flat = probs.T[0:8, :]
    high = flat.astype(BF)
    rest = flat - high.astype(F32)
    mid = rest.astype(BF)
    low = (rest - mid.astype(F32)).astype(BF)
    split = jnp.concatenate([high.astype(F32), mid.astype(F32), low.astype(F32)], axis=0).astype(BF)

    def go_in(j):
        return remote(send_in.at[j], got_in.at[j], send_i.at[j], recv_i.at[j], plane[j])

    def go_gate(j):
        return remote(send_gate.at[j], got_gate.at[j], send_t.at[j], recv_t.at[j], plane[j])

    for j in range(4):
        e = experts_of[j]
        taken = nn(hot_rows(pick_row(places_row[...], e), capacity), routed).astype(BF)
        three = nn(split, hot_cols(pick_col(places_col[...], e), capacity))
        gate = three[0:8] + three[8:16] + three[16:24]
        gate = jnp.broadcast_to(pick_row(gate, e), gate.shape)
        if j != OWN:
            send_in[j] = taken
            send_gate[j] = gate
            go_gate(j).start()
        if j < OWN:
            go_in(j).start()
        if j == OWN:
            got_in[j] = taken
            got_gate[j] = gate
    own_raw.wait()
    for c in lifts:
        c.wait()
    for i in range(nz - 1):
        weights(i).wait_recv()

    def go_gin(j):
        return remote(out_gin.at[j], back_gin.at[j], send_r.at[j], recv_r.at[j], plane[j])

    def go_dot(j):
        return remote(out_dot.at[j], back_dot.at[j], send_d.at[j], recv_d.at[j], plane[j])

    def go_dw(n):
        return remote(dw_away.at[n], dw_got.at[n], send_v.at[n], recv_v.at[n], sibling)

    def arrive(lo, hi):
        for j in range(lo, hi):
            if j != OWN:
                go_raw(j).wait_recv()
                go_in(j).wait_recv()
                go_gate(j).wait_recv()
            gate = got_gate[j].T[:, 0:1]
            grad[j] = (raw_ref[j].astype(F32) * gate).astype(BF)

    def chunk(lo, hi, w_ref, dw, d, first, at):
        count = (hi - lo) * capacity
        xs = got_in[lo:hi].reshape(count, width)
        gs = grad[lo:hi].reshape(count, width)
        res, gin, d_first, d_second = expert_step(xs, gs, w_ref[d])
        here = slice(at * capacity, at * capacity + count)
        res_acc[here, :] += res
        gin_acc[here, :] += gin
        if first:
            dw[d, :, :width] = d_first.astype(BF)
            dw[d, :, width:] = d_second.astype(BF)
        else:
            dw[d, :, :width] = (dw[d, :, :width].astype(F32) + d_first).astype(BF)
            dw[d, :, width:] = (dw[d, :, width:].astype(F32) + d_second).astype(BF)

    def send_back(lo, hi, at):
        for j in range(lo, hi):
            here = slice((at + j - lo) * capacity, (at + j - lo + 1) * capacity)
            prod = res_acc[here, :] * raw_ref[j].astype(F32)
            narrow = functools.reduce(jnp.add, [prod[:, i : i + 128] for i in range(0, width, 128)])
            inner = jnp.broadcast_to(jnp.sum(narrow.T, axis=0, keepdims=True), (8, capacity))
            if j != OWN:
                out_gin[j] = gin_acc[here, :].astype(BF)
                out_dot[j] = inner
                go_gin(j).start()
                go_dot(j).start()
            else:
                back_gin[j] = gin_acc[here, :].astype(BF)
                back_dot[j] = inner
        for j in range(lo, hi):
            here = slice((at + j - lo) * capacity, (at + j - lo + 1) * capacity)
            out_res[j] = res_acc[here, :].astype(BF)

    both = ((theirs, dw_away), (own_w, dw_ref))
    res_acc[...] = jnp.zeros(res_acc.shape, F32)
    gin_acc[...] = jnp.zeros(gin_acc.shape, F32)
    arrive(OWN, OWN + 1)
    for w_ref, dw in both:

        @pl.loop(0, nz - 1)
        def _(i):
            chunk(OWN, OWN + 1, w_ref, dw, i + shift, True, OWN)

    arrive(0, OWN)
    go_raw(3).start()
    go_in(3).start()
    for w_ref, dw in both:

        @pl.loop(0, nz - 1)
        def _(i):
            chunk(0, OWN, w_ref, dw, i + shift, False, 0)

    @pl.when(jnp.logical_not(at_end))
    def _():
        far_lift.wait()

    line.wait_recv(nz - 1)
    weights(nz - 1).start()
    chunk(0, OWN + 1, own_w, dw_ref, far_zone, True, 0)
    weights(nz - 1).wait_recv()
    chunk(0, OWN + 1, theirs, dw_away, far_zone, True, 0)
    send_back(0, OWN + 1, 0)
    arrive(3, 4)
    res_acc[0:capacity, :] = jnp.zeros((capacity, width), F32)
    gin_acc[0:capacity, :] = jnp.zeros((capacity, width), F32)

    @pl.loop(0, nz)
    def _(d):
        chunk(3, 4, theirs, dw_away, d, False, 0)
        go_dw(d).start()

    @pl.loop(0, nz)
    def _(d):
        chunk(3, 4, own_w, dw_ref, d, False, 0)

    send_back(3, 4, 0)
    for n in range(nz):
        go_dw(n).wait_recv()
        dw_ref[n] = (dw_ref[n].astype(F32) + dw_got[n].astype(F32)).astype(BF)
    for j in AWAY:
        go_gin(j).wait_recv()
        go_dot(j).wait_recv()
    line.wait_send(nz - 1)
    for n in range(nz):
        weights(n).wait_send()
        go_dw(n).wait_send()
    for j in AWAY:
        for c in (go_raw(j), go_in(j), go_gate(j), go_gin(j), go_dot(j)):
            c.wait_send()


def experts(x, attended, whole, places_row, places_col, raw, near, capacity, nz, cid):
    rows, width = x.shape
    part = near.shape[1]
    slots = sds((4, capacity, width), BF)
    small = sds((4, 8, capacity), F32)
    dma = pltpu.SemaphoreType.DMA
    two = lambda *shape: [dma(shape), dma(shape)]
    vm = pltpu.VMEM
    return pl.pallas_call(
        functools.partial(experts_kernel, capacity, nz),
        out_shape=(
            sds((rows, width), F32),
            sds((rows, 128), F32),
            slots,
            slots,
            small,
            sds((nz, part, 2 * width), BF),
        ),
        in_specs=[VM, VM, ANY, VM, VM, ANY, ANY],
        out_specs=(VM,) * 6,
        scratch_shapes=[
            vm((rows, width + 128), BF),
            vm((4, capacity, width), BF),
            vm((4, capacity, width), BF),
            vm((4, 8, capacity), F32),
            vm((4, 8, capacity), F32),
            vm((nz, part, 2 * width), BF),
            vm((nz, part, 2 * width), BF),
            vm((4, capacity, width), BF),
            vm((3 * capacity, width), F32),
            vm((3 * capacity, width), F32),
            vm((4, capacity, width), BF),
            vm((4, 8, capacity), F32),
            vm((nz, part, 2 * width), BF),
            vm((nz, part, 2 * width), BF),
            vm((4, capacity, width), BF),
            dma((2 + nz,)),
        ]
        + two(4) + two(nz) + two(4) + two(4) + two(4) + two(4) + two(nz) + two(nz - 1) + two(nz - 1),
        compiler_params=params(cid),
        name="experts",
    )(x, attended, whole, places_row, places_col, raw, near)


PARTS = 4


def finish_kernel(
    prompt, nz, capacity, xs_ref, lse_ref, w_ref, seg_ref, hidden_ref, probs_ref, places_ref,
    dot_ref, qkv_hbm, mixed_hbm, gin_ref, res_ref, cot_ref, att_ref, part_ref,
    out_ref, dx_ref, din_out, dout_out, droute_out, dgains_out, dw_all,
    gh, gatt, got_res, qkv_ref, mixed_ref, grad, qm, dom, kt, dqt, dcat, norm_t, sums, got_c, got_x, got_z, mine, fin, got_f, total,
    send_dx, got_dx, own_gn, stage, dw_sum, ahead, got_up, got_down,
    local, send_r, recv_r, send_g, recv_g, send_c, recv_c, send_x, recv_x, send_z, recv_z, send_d, recv_d, send_f, recv_f,
    send_a, recv_a, send_b, recv_b, send_u, recv_u, send_l, recv_l, send_v, recv_v, send_h, recv_h, send_k, recv_k,
):
    dp, sq, z, x, core = place()
    rows, width = gatt.shape
    half = width // 2
    pairs = half // 128
    shard = width // nz
    part = shard // 4
    own_cols = 3 * half
    lead = own_cols + 128
    chip = x * 2 + sq
    chip_x, chip_y, chip_d = (1 - x) * 2 + sq, x * 2 + 1 - sq, (1 - x) * 2 + 1 - sq
    sibling = (x * 2 + 1 - core, sq, z)
    partner = (dp, 1 - sq, z)
    across = ((1 - x) * 2 + core, sq, z)
    others = [(dp, sq, lax.rem(z + d, nz)) for d in range(1, nz)]
    base = pl.multiple_of(sq * rows, rows)
    there = pl.multiple_of((1 - sq) * rows, rows)
    corner = [flip_chip(x, sq, *f) for f in SOURCES]
    plane = [(px * 2 + core, py, z) for px, py in corner]
    experts_of = [px * 2 + py for px, py in corner]
    greet([sibling] + [plane[j] for j in AWAY] + others)

    quarter = stage.shape[1]

    def rows_of(k):
        return pl.ds(k * quarter, quarter)

    def hop(k, t, up, src):
        to = lax.rem(z + 1, nz) if up else lax.rem(z + nz - 1, nz)
        got, send, recv = (got_up, send_u, recv_u) if up else (got_down, send_l, recv_l)
        return remote(src, got.at[k, t - 1 if up else t], send.at[k, t], recv.at[k, t], (dp, sq, to))

    def legs(slot):
        ups = (True, slot, list(range(nz - 1, slot, -1)))
        downs = (False, nz - 1 - slot, list(range(0, nz - 1 - slot)))
        return ups, downs

    def line_slot(k, slot):
        for up, sender, zones in legs(slot):

            @pl.when(z == sender)
            def _(up=up, zones=zones):
                if slot == 0:
                    for t in zones:
                        hop(k, t, up, part_ref.at[t, rows_of(k)]).start()
                    return
                loads = [
                    pltpu.make_async_copy(part_ref.at[t, rows_of(k)], stage.at[i], local.at[i])
                    for i, t in enumerate(zones)
                ]
                for c in loads:
                    c.start()
                for i, t in enumerate(zones):
                    to = ahead.at[k % 2, i if slot == 1 else 2]
                    if k > 1:
                        hop(k - 2, t, up, to).wait_send()
                    hop(k, t, up, to).wait_recv()
                    loads[i].wait()
                    got = got_up[k, t - 1] if up else got_down[k, t]
                    to[...] = (stage[i].astype(F32) + got.astype(F32)).astype(BF)
                    hop(k, t, up, to).start()

    def line_end():
        for slot in range(nz - 1):
            for up, sender, zones in legs(slot):

                @pl.when(z == sender)
                def _(up=up, zones=zones, slot=slot):
                    for k in range(PARTS) if slot == 0 else range(PARTS - 2, PARTS):
                        for i, t in enumerate(zones):
                            src = part_ref.at[t, rows_of(k)] if slot == 0 else ahead.at[k % 2, i if slot == 1 else 2]
                            hop(k, t, up, src).wait_send()

    def share(k, ch, send, recv, peer, own=False):
        at = dw_all.at[core, ch, pl.ds(k * quarter, quarter)]
        return remote(dw_sum.at[k] if own else at, at, send, recv, peer)

    def keep(k):
        return pltpu.make_async_copy(
            dw_sum.at[k], dw_all.at[core, chip, pl.ds(k * quarter, quarter)], local.at[nz + k]
        )

    def sum_part(k):
        own = pltpu.make_async_copy(part_ref.at[z, rows_of(k)], stage.at[2], local.at[2])
        own.start()
        above_zero, below_top = z > 0, z < nz - 1

        @pl.when(above_zero)
        def _():
            hop(k, z, True, ahead.at[0, 0]).wait_recv()
            stage[0] = got_up[k, z - 1]

        @pl.when(below_top)
        def _():
            hop(k, z, False, ahead.at[0, 0]).wait_recv()
            stage[1] = got_down[k, z]

        own.wait()
        acc = stage[2].astype(F32)
        acc = acc + jnp.where(above_zero, stage[0].astype(F32), 0.0)
        acc = acc + jnp.where(below_top, stage[1].astype(F32), 0.0)
        dw_sum[k] = acc.astype(BF)
        share(k, chip, send_v.at[k], recv_v.at[k], partner, True).start()
        share(k, chip, send_h.at[k, 0], recv_h.at[k, 0], across, True).start()
        share(k, chip, send_k.at[k, 0], recv_k.at[k, 0], sibling, True).start()
        keep(k).start()

    def pass_part(k):
        share(k, chip_y, send_v.at[k], recv_v.at[k], partner).wait_recv()
        share(k, chip_y, send_h.at[k, 1], recv_h.at[k, 1], across).start()
        share(k, chip_y, send_k.at[k, 1], recv_k.at[k, 1], sibling).start()

    def last_part(k):
        share(k, chip_x, send_h.at[k, 0], recv_h.at[k, 0], across).wait_recv()
        share(k, chip_x, send_k.at[k, 2], recv_k.at[k, 2], sibling).start()
        share(k, chip_d, send_h.at[k, 1], recv_h.at[k, 1], across).wait_recv()
        share(k, chip_d, send_k.at[k, 3], recv_k.at[k, 3], sibling).start()

    others_of = [chip, chip_y, chip_x, chip_d]

    def end_parts():
        for k in range(PARTS):
            for i in range(4):
                at = dw_all.at[1 - core, others_of[i], rows_of(k)]
                remote(at, at, send_k.at[k, i], recv_k.at[k, i], sibling).wait_recv()
                share(k, others_of[i], send_k.at[k, i], recv_k.at[k, i], sibling, i == 0).wait_send()
            share(k, chip, send_v.at[k], recv_v.at[k], partner, True).wait_send()
            share(k, chip, send_h.at[k, 0], recv_h.at[k, 0], across, True).wait_send()
            share(k, chip_y, send_h.at[k, 1], recv_h.at[k, 1], across).wait_send()
            keep(k).wait()
        line_end()

    spans = [((pairs - 1) * 384, lead), (lead, lead + width)] + [(p * 384, (p + 1) * 384) for p in range(pairs - 1)]
    groups = [pl.ds(lo, hi - lo) for lo, hi in spans]
    order = [lax.rem(z + d, nz) for d in range(1, nz + 1)]

    def piece(zz, px, co):
        return pl.ds(pl.multiple_of(zz * shard + (px * 2 + co) * part, part), part)

    def to_core(g, n, i):
        src = sums.at[piece(order[n], (1 - x, x)[i], 1 - core), groups[g]]
        return remote(src, got_c.at[n, i, :, groups[g]], send_c.at[g, n, i], recv_c.at[g, n, i], sibling)

    def to_x(g, n):
        src = sums.at[piece(order[n], 1 - x, core), groups[g]]
        return remote(src, got_x.at[n, :, groups[g]], send_x.at[g, n], recv_x.at[g, n], across)

    def to_z(g, n):
        return remote(
            mine.at[n, :, groups[g]], got_z.at[n, :, groups[g]], send_z.at[g, n], recv_z.at[g, n], others[n]
        )

    def cols_of(g):
        return slice(*spans[g])

    def reduce_core(g, n):
        cols = cols_of(g)
        for i in range(2):
            to_core(g, n, i).wait_recv()
            at = piece(order[n], (1 - x, x)[i], core)
            sums[at, cols] = (sums[at, cols].astype(F32) + got_c[n, i, :, cols].astype(F32)).astype(BF)
            if i == 0:
                to_x(g, n).start()

    def reduce_x(g, n):
        cols = cols_of(g)
        to_x(g, n).wait_recv()
        acc = sums[piece(order[n], x, core), cols].astype(F32) + got_x[n, :, cols].astype(F32)
        if n < nz - 1:
            mine[n, :, cols] = acc.astype(BF)
            to_z(g, n).start()
        return acc

    def reduce_z(g, acc):
        cols = cols_of(g)
        for n in range(nz - 1):
            to_z(g, n).wait_recv()
            acc = acc + got_z[n, :, cols].astype(F32)
        fin[:, cols] = acc.astype(BF)

    def pair_loads(p):
        return (
            pltpu.make_async_copy(qkv_hbm.at[p], qkv_ref, local.at[nz + PARTS]),
            pltpu.make_async_copy(mixed_hbm.at[p], mixed_ref, local.at[nz + PARTS + 1]),
        )

    for c in pair_loads(0):
        c.start()
    line_slot(0, 0)
    fetch = [pltpu.make_async_copy(gin_ref.at[j], dcat.at[pl.ds(j * capacity, capacity), 0:width], local.at[j]) for j in range(4)]
    fetch.append(pltpu.make_async_copy(cot_ref, send_dx, local.at[4]))
    fetch.append(pltpu.make_async_copy(att_ref, norm_t.at[:, 0:rows], local.at[5]))
    fetch.append(pltpu.make_async_copy(res_ref.at[OWN], got_res.at[OWN], local.at[6]))
    for c in fetch:
        c.start()
    results = {j: remote(res_ref.at[j], got_res.at[j], send_r.at[j], recv_r.at[j], plane[j]) for j in AWAY}
    for j in range(OWN):
        results[j].start()
    for c in fetch:
        c.wait()
    hidden = hidden_ref[...]
    probs = probs_ref[...]
    small = w_ref[:, own_cols:lead]
    gain_two = small.astype(F32).T[EXPERTS + 1 : EXPERTS + 2, :]
    lane = iota(probs.shape, 1)
    back = None
    grad_probs = jnp.zeros_like(probs)
    for j in range(4):
        pick = hot_cols(pick_col(places_ref[...], experts_of[j]), capacity)
        add = nn(pick, dcat[j * capacity : (j + 1) * capacity, 0:width])
        back = add if back is None else back + add
        inner = jnp.sum(pick.astype(F32) * dot_ref[j][0:1, :], axis=1, keepdims=True)
        grad_probs = jnp.where(lane == experts_of[j], inner, grad_probs)
    mixed = jnp.sum(probs * grad_probs, axis=1, keepdims=True)
    low = (probs * (grad_probs - mixed)).astype(BF)
    r_two = lax.rsqrt(jnp.mean(hidden * hidden, axis=1, keepdims=True) + EPSILON)
    h_norm = hidden * r_two
    routed = (h_norm * gain_two).astype(BF)
    grad_routed = back + nt(low, small)
    dg_two = jnp.sum(grad_routed * h_norm, axis=0, keepdims=True)
    u = grad_routed * gain_two
    grad_hidden = send_dx[...].astype(F32) + r_two * (
        u - h_norm * jnp.mean(u * h_norm, axis=1, keepdims=True)
    )
    gh[...] = grad_hidden
    hid_low = grad_hidden.astype(BF)
    gatt[...] = nt(hid_low, w_ref[:, lead:]).astype(BF)

    def give(p, to):
        return remote(
            gatt.at[:, pl.ds(al((1 - sq) * half + p * 128), 128)],
            grad.at[p, pl.ds(to, rows)],
            send_g.at[p],
            recv_g.at[p],
            partner,
        )

    for p in range(pairs):
        give(p, base).start()
    line_slot(1, 0)
    for p in range(pairs):
        grad[p, pl.ds(base, rows), :] = gatt[:, pl.ds(al(sq * half + p * 128), 128)]
    d_route = tn(routed, low)
    sums[:, cols_of(1)] = tn(norm_t[:, 0:rows], hid_low).astype(BF)
    for n in range(nz):
        for i in range(2):
            to_core(1, n, i).start()
    seg_row, seg_col = eighth(seg_ref[...], prompt)
    gain = w_ref[:, own_cols:lead].astype(F32).T[EXPERTS : EXPERTS + 1, :]

    def norm_of(at):
        xf = xs_ref[at, :].astype(F32)
        r_one = lax.rsqrt(jnp.mean(xf * xf, axis=1, keepdims=True) + EPSILON)
        return xf * r_one, r_one

    for i in range(2):
        at = slice(i * rows, (i + 1) * rows)
        norm_t[:, at] = (norm_of(at)[0] * gain).astype(BF).T

    line_slot(0, 1)
    def weight_grad(g, p):
        cols = slice(p * 384, (p + 1) * 384)
        for n in range(nz):
            zone = pl.ds(pl.multiple_of(order[n] * shard, shard), shard)
            sums[zone, cols] = nn(norm_t[zone, :], dcat[:, cols]).astype(BF)
            for i in range(2):
                to_core(g, n, i).start()

    blocks = 2 * rows // QB
    scale = HEAD_DIM ** (-0.5)
    zero = jnp.zeros((), BF)

    @pl.loop(0, pairs)
    def _(p):
        give(p, there).wait_recv()
        for c in pair_loads(p):
            c.wait()
        kt[...] = qkv_ref[1].T
        prod = (grad[p].astype(F32) * mixed_ref[...].astype(F32)).T
        delta = []
        for h in range(2):
            lanes = iota((1, 128), 1) // HEAD_DIM == h
            qm[h] = jnp.where(lanes, qkv_ref[0], zero) * jnp.asarray(scale, BF)
            dom[h] = jnp.where(lanes, grad[p], zero)
            low = h * HEAD_DIM
            delta.append(jnp.sum(prod[low : low + HEAD_DIM, :], axis=0, keepdims=True))
        for j in range(blocks):
            keys = slice(j * QB, (j + 1) * QB)
            k, v = qkv_ref[1, keys, :], qkv_ref[2, keys, :]
            dk = dv = None
            for i in range(j, blocks):
                at = slice(i * QB, (i + 1) * QB)
                mask = allowed_tile(j, i, prompt, seg_col, seg_row)
                for h in range(2):
                    s = nt(k, qm[h, at, :])
                    dpr = nt(v, dom[h, at, :])
                    pr = jnp.exp2(s * LOG2E - lse_ref[p, h : h + 1, at])
                    if mask is not None:
                        pr = jnp.where(mask, pr, 0.0)
                    ds = (pr * (dpr - delta[h][:, at])).astype(BF)
                    a = nn(pr.astype(BF), dom[h, at, :])
                    b = nn(ds, qm[h, at, :])
                    c = nn(kt[h * HEAD_DIM : (h + 1) * HEAD_DIM, keys], ds)
                    dv = a if dv is None else dv + a
                    dk = b if dk is None else dk + b
                    to = slice(h * HEAD_DIM, (h + 1) * HEAD_DIM)
                    dqt[to, at] = c if j == 0 else dqt[to, at] + c
            dcat[keys, pl.ds(al(p * 384 + 128), 128)] = dk.astype(BF)
            dcat[keys, pl.ds(al(p * 384 + 256), 128)] = dv.astype(BF)
        dcat[:, pl.ds(al(p * 384), 128)] = (dqt[...] * scale).T.astype(BF)

        @pl.when(p < pairs - 1)
        def _():
            for c in pair_loads(p + 1):
                c.start()

        @pl.when(p == 0)
        def _():
            weight_grad(2, 0)
            line_slot(2, 0)
            results[3].start()
            line_slot(0, 2)
            for n in range(nz):
                reduce_core(1, n)

        @pl.when(p == 1)
        def _():
            weight_grad(3, 1)
            line_slot(3, 0)
            line_slot(1, 1)
            sum_part(0)
            for n in range(nz - 1):
                reduce_x(1, n)
            for n in range(nz):
                reduce_core(2, n)

        @pl.when(p == 2)
        def _():
            line_slot(1, 2)
            line_slot(2, 1)
            pass_part(0)
            for n in range(nz):
                reduce_core(3, n)
            for n in range(nz - 1):
                reduce_x(2, n)

    partial = nt(dcat[pl.ds(there, rows), :], w_ref[:, 0:own_cols])
    send_dx[...] = partial.astype(BF)
    to_dx = remote(send_dx, got_dx, send_d, recv_d, partner)
    to_dx.start()
    dg_one = jnp.sum(partial * norm_of(pl.ds(there, rows))[0], axis=0, keepdims=True)
    partial = nt(dcat[pl.ds(base, rows), :], w_ref[:, 0:own_cols])
    own_gn[...] = partial
    dg_one = dg_one + jnp.sum(partial * norm_of(pl.ds(base, rows))[0], axis=0, keepdims=True)
    stacked = jnp.concatenate([dg_one, dg_two, jnp.zeros((126, width), F32)], axis=0).T
    lane = iota((1, 128), 1)
    small = jnp.where(lane < EXPERTS, d_route, 0.0)
    for i in range(2):
        small = jnp.where(lane == EXPERTS + i, stacked[:, i : i + 1], small)
    sums[:, own_cols:lead] = small.astype(BF)
    weight_grad(0, pairs - 1)
    reduce_core(0, 0)
    for n in range(1, nz):
        reduce_core(0, n)
        if n == 1:
            line_slot(2, 2)
            sum_part(1)
        reduce_x(0, n - 1)
    for n in range(nz - 1):
        reduce_x(3, n)
    line_slot(3, 1)
    last_part(0)
    pass_part(1)
    for g in (1, 2):
        reduce_z(g, reduce_x(g, nz - 1))
    total_out = hidden_ref[...]
    for j in (OWN,) + AWAY:
        if j != OWN:
            results[j].wait_recv()
        pick = hot_cols(pick_col(places_ref[...], experts_of[j]), capacity)
        total_out = total_out + pick_col(probs_ref[...], experts_of[j]) * nn(pick, got_res[j])
    out_ref[...] = total_out.astype(BF)
    sum_part(2)
    line_slot(3, 2)
    reduce_z(3, reduce_x(3, nz - 1))
    reduce_z(0, reduce_x(0, nz - 1))
    to_f = remote(fin, got_f, send_f, recv_f, partner)
    to_f.start()
    to_dx.wait_recv()
    grad_n = own_gn[...] + got_dx[...].astype(F32)
    x_norm, r_one = norm_of(pl.ds(base, rows))
    u = grad_n * gain
    dx = gh[...] + r_one * (u - x_norm * jnp.mean(u * x_norm, axis=1, keepdims=True))
    dx_ref[...] = dx.astype(BF)
    last_part(1)
    pass_part(2)
    to_f.wait_recv()

    def spot(px, co):
        return pl.ds(pl.multiple_of((px * 2 + co) * part, part), part)

    here = spot(x, core)
    for p in range(pairs):
        for i in range(3):
            cols = slice((3 * p + i) * 128, (3 * p + i + 1) * 128)
            total[here, pl.ds(al(i * width + sq * half + p * 128), 128)] = fin[:, cols]
            total[here, pl.ds(al(i * width + (1 - sq) * half + p * 128), 128)] = got_f[:, cols]
    total[here, 3 * width :] = (fin[:, own_cols:].astype(F32) + got_f[:, own_cols:].astype(F32)).astype(BF)

    def pass_on(px, co, send, recv, peer):
        return remote(total.at[spot(px, co)], total.at[spot(px, co)], send, recv, peer)

    pass_on(x, core, send_a, recv_a, across).start()
    pass_on(x, core, send_b.at[0], recv_b.at[0], sibling).start()
    sum_part(3)
    last_part(2)
    pass_part(3)
    pass_on(1 - x, core, send_a, recv_a, across).wait_recv()
    pass_on(1 - x, core, send_b.at[1], recv_b.at[1], sibling).start()
    pass_on(x, 1 - core, send_b.at[0], recv_b.at[0], sibling).wait_recv()
    pass_on(1 - x, 1 - core, send_b.at[1], recv_b.at[1], sibling).wait_recv()
    din_out[...] = total[:, 0 : 3 * width].astype(F32)
    small = total[:, 3 * width : 3 * width + 128].astype(F32)
    wide = -(-shard // 128) * 128
    turned = jnp.concatenate([small, jnp.zeros((wide - shard, 128), F32)], axis=0).T
    droute_out[...] = turned[0:EXPERTS, 0:shard]
    dgains_out[...] = turned[EXPERTS : EXPERTS + 2, 0:shard]
    dout_out[...] = total[:, 3 * width + 128 :].astype(F32)
    last_part(3)
    end_parts()
    for c in results.values():
        c.wait_send()
    pass_on(x, core, send_a, recv_a, across).wait_send()
    pass_on(x, core, send_b.at[0], recv_b.at[0], sibling).wait_send()
    pass_on(1 - x, core, send_b.at[1], recv_b.at[1], sibling).wait_send()
    to_f.wait_send()
    to_dx.wait_send()
    for g in range(len(spans)):
        for n in range(nz):
            for i in range(2):
                to_core(g, n, i).wait_send()
            to_x(g, n).wait_send()
            if n < nz - 1:
                to_z(g, n).wait_send()
    for p in range(pairs):
        give(p, base).wait_send()


def finish(
    xs, qkv, mixed, lse, whole, segments, hidden, probs, places, inner, gin, res, cot, attended, dw_half,
    prompt, nz, capacity, cid,
):
    rows, width = cot.shape
    pairs = width // 256
    cols = whole.shape[1]
    shard = width // nz
    part = shard // 4
    group = 2 * rows
    deep = dw_half.shape[1]
    quarter = (deep // PARTS, dw_half.shape[2])
    dma = pltpu.SemaphoreType.DMA
    two = lambda *shape: [dma(shape), dma(shape)]
    vm = pltpu.VMEM
    return pl.pallas_call(
        functools.partial(finish_kernel, prompt, nz, capacity),
        out_shape=(
            sds((rows, width), BF),
            sds((rows, width), BF),
            sds((shard, 3 * width), F32),
            sds((shard, width), F32),
            sds((EXPERTS, shard), F32),
            sds((2, shard), F32),
            sds((2, 4) + dw_half.shape[1:], BF),
        ),
        in_specs=[VM] * 8 + [ANY] * 7,
        out_specs=(VM,) * 6 + (ANY,),
        scratch_shapes=[
            vm((rows, width), F32),
            vm((rows, width), BF),
            vm((4, capacity, width), BF),
            vm((3, group, 128), BF),
            vm((group, 128), BF),
            vm((pairs, group, 128), BF),
            vm((2, group, 128), BF),
            vm((2, group, 128), BF),
            vm((128, group), BF),
            vm((128, group), F32),
            vm((group, 3 * width // 2), BF),
            vm((width, group), BF),
            vm((width, cols), BF),
            vm((nz, 2, part, cols), BF),
            vm((nz, part, cols), BF),
            vm((nz - 1, part, cols), BF),
            vm((nz - 1, part, cols), BF),
            vm((part, cols), BF),
            vm((part, cols), BF),
            vm((shard, 4 * width + 128), BF),
            vm((rows, width), BF),
            vm((rows, width), BF),
            vm((rows, width), F32),
            vm((nz,) + quarter, BF),
            vm((PARTS,) + quarter, BF),
            vm((2, 3) + quarter, BF),
            vm((PARTS, nz - 1) + quarter, BF),
            vm((PARTS, nz - 1) + quarter, BF),
            dma((nz + PARTS + 2,)),
        ]
        + two(4) + two(pairs) + two(pairs + 1, nz, 2) + two(pairs + 1, nz) + two(pairs + 1, nz - 1) + two() + two() + two() + two(2)
        + two(PARTS, nz) + two(PARTS, nz) + two(PARTS) + two(PARTS, 2) + two(PARTS, 4),
        compiler_params=params(cid),
        name="finish",
    )(xs, lse, whole, segments, hidden, probs, places, inner, qkv, mixed, gin, res, cot, attended, dw_half)


def spread_kernel(in_ref, out_ref):
    for e in range(EXPERTS):
        out_ref[:, e, :] = in_ref[e].astype(F32)


def spread_experts(parts):
    cores, experts_, r, k = parts.shape
    block = r // 2
    return pl.pallas_call(
        spread_kernel,
        grid=(cores, r // block),
        out_shape=sds((cores * r, experts_, k), F32),
        in_specs=[pl.BlockSpec((None, experts_, block, k), lambda c, i: (c, 0, i, 0))],
        out_specs=pl.BlockSpec((block, experts_, k), lambda c, i: (c * (r // block) + i, 0, 0)),
        compiler_params=params(),
        name="spread",
    )(parts)


def shards(tokens, attn_in, attn_out, router, gains, expert_w, expert_ids, segments, cotangent):
    x = tokens[0]
    cot = cotangent[0]
    rows, width = x.shape
    nz = lax.axis_size("fsdp")
    group = 2 * rows
    prompt = group - segments.shape[1]
    capacity = 2 * rows // EXPERTS
    dp, sq = lax.axis_index("dp"), lax.axis_index("seq")
    core = lax.rem(dp, 2)
    mine = (dp // 2) * 2 + sq

    part = expert_w.shape[0] // 2
    piece = lax.dynamic_slice(expert_w, (core * part, mine, 0), (part, 1, 2 * width))[:, 0]
    xs, whole, qkv, mixed, lse, attended, raw, places_row, places_col, near = begin(
        x, attn_in, attn_out, router.T, gains.T, segments, expert_ids[0].T, cot, piece, prompt, nz, capacity, 0
    )
    hidden, probs, gin, res, inner, dw_half = experts(
        x, attended, whole, places_row, places_col, raw, near, capacity, nz, 1
    )
    block_out, d_tokens, d_in, d_out, d_route, d_gains, dw_all = finish(
        xs, qkv, mixed, lse, whole, segments, hidden, probs, places_col, inner, gin, res, cot, attended, dw_half,
        prompt, nz, capacity, 2,
    )
    d_expert = spread_experts(dw_all)
    return (
        block_out[None],
        d_tokens[None],
        d_in,
        d_out,
        d_route.T,
        d_gains.T,
        d_expert,
    )


def route(choose, capacity, experts_count):
    pair_expert = choose.reshape(-1)
    one_hot = (pair_expert[:, None] == jnp.arange(experts_count, dtype=jnp.int32)[None, :]).astype(
        jnp.int32
    )
    before = jnp.cumsum(one_hot, axis=0) - one_hot
    place = jnp.sum(before * one_hot, axis=1)
    kept = place < capacity
    slots = jnp.where(kept, pair_expert * capacity + place, experts_count * capacity)
    pair_count = pair_expert.shape[0]
    pair_of = (
        jnp.zeros((experts_count * capacity + 1,), jnp.int32)
        .at[slots]
        .set(jnp.arange(pair_count, dtype=jnp.int32))
    )
    filled = (
        jnp.zeros((experts_count * capacity + 1,), jnp.int32)
        .at[slots]
        .set(jnp.ones((pair_count,), jnp.int32))
    )
    return (slots, kept, pair_of[:-1], filled[:-1] > 0)


def expert_pre(expert_in, piece):
    width = piece.shape[2] // 2
    return jnp.einsum(
        "ecd,fed->ecf", expert_in, piece[:, :, :width], preferred_element_type=jnp.float32
    )


def expert_out(activity, piece):
    width = piece.shape[2] // 2
    return jnp.einsum(
        "ecf,fed->ecd", activity, piece[:, :, width:], preferred_element_type=jnp.float32
    )


def expert_back(grad_result, pre_rows, piece):
    width = piece.shape[2] // 2
    grad_act = jnp.einsum(
        "ecd,fed->ecf", grad_result, piece[:, :, width:], preferred_element_type=jnp.float32
    )
    grad_pre = jax.vjp(jax.nn.gelu, pre_rows)[1](grad_act)[0].astype(jnp.bfloat16)
    grad_in = jnp.einsum(
        "ecf,fed->ecd", grad_pre, piece[:, :, :width], preferred_element_type=jnp.float32
    )
    return (grad_pre, grad_in)


def general_shards(tokens, attn_in, attn_out, router, gains, expert_w, expert_ids, segments, cotangent):
    x_rows = tokens[0].astype(jnp.float32)
    tok_rows = x_rows.shape[0]
    width = x_rows.shape[1]
    seq_count = lax.axis_size("seq")
    scale = HEAD_DIM ** (-0.5)
    w_qkv, w_proj, w_route, gain_pair = (
        lax.all_gather(attn_in, "fsdp", axis=0, tiled=True),
        lax.all_gather(attn_out, "fsdp", axis=0, tiled=True),
        lax.all_gather(router, "fsdp", axis=0, tiled=True),
        lax.all_gather(gains, "fsdp", axis=0, tiled=True),
    )
    gain_f = gain_pair.astype(jnp.float32)
    r_one = lax.rsqrt(jnp.mean(x_rows * x_rows, axis=-1, keepdims=True) + EPSILON)
    normed_one = x_rows * r_one
    normed_low = (normed_one * gain_f[:, 0]).astype(jnp.bfloat16)
    projected = jnp.dot(normed_low, w_qkv, preferred_element_type=jnp.float32).astype(jnp.bfloat16)
    local_heads = HEADS // seq_count
    head_cols = local_heads * HEAD_DIM
    arrived = lax.all_to_all(
        projected.reshape(tok_rows, 3, seq_count, head_cols),
        "seq",
        split_axis=2,
        concat_axis=0,
        tiled=True,
    )
    group_len = arrived.shape[0]
    queries = arrived[:, 0, 0].reshape(group_len, local_heads, HEAD_DIM)
    keys = arrived[:, 1, 0].reshape(group_len, local_heads, HEAD_DIM)
    values = arrived[:, 2, 0].reshape(group_len, local_heads, HEAD_DIM)
    seg_full = jnp.concatenate([jnp.full((PROMPT,), -1, jnp.int32), segments[0]])
    block = min(512, group_len)
    key_place = jnp.arange(group_len, dtype=jnp.int32)
    begins = jnp.arange(group_len // block, dtype=jnp.int32) * block

    def block_scores(begin):
        query_block = lax.dynamic_slice_in_dim(queries, begin, block, 0)
        query_place = begin + jnp.arange(block, dtype=jnp.int32)
        query_seg = lax.dynamic_slice_in_dim(seg_full, begin, block, 0)
        raw = (
            jnp.einsum("qhd,khd->hqk", query_block, keys, preferred_element_type=jnp.float32)
            * scale
        )
        allowed = (key_place[None, :] <= query_place[:, None]) & (
            (seg_full[None, :] < 0) | (seg_full[None, :] == query_seg[:, None])
        )
        return (jnp.where(allowed[None], raw, NEGATIVE), query_block)

    def forward_block(begin):
        masked, query_block = block_scores(begin)
        row_max = jnp.max(masked, axis=-1, keepdims=True)
        expo = jnp.exp(masked - row_max)
        row_total = jnp.sum(expo, axis=-1, keepdims=True)
        probs = expo / row_total
        mixed_block = jnp.einsum(
            "hqk,khd->qhd", probs.astype(jnp.bfloat16), values, preferred_element_type=jnp.float32
        )
        return (mixed_block.astype(jnp.bfloat16), (row_max + jnp.log(row_total))[:, :, 0])

    mixed_blocks, log_totals = lax.map(forward_block, begins)
    mixed_heads = mixed_blocks.reshape(group_len, 1, head_cols)
    returned = lax.all_to_all(mixed_heads, "seq", split_axis=0, concat_axis=1, tiled=True)
    attended = returned.reshape(tok_rows, width)
    hidden = x_rows + jnp.dot(attended, w_proj, preferred_element_type=jnp.float32)
    r_two = lax.rsqrt(jnp.mean(hidden * hidden, axis=-1, keepdims=True) + EPSILON)
    normed_two = hidden * r_two
    routed_low = (normed_two * gain_f[:, 1]).astype(jnp.bfloat16)
    logits = jnp.dot(routed_low, w_route, preferred_element_type=jnp.float32)
    probs_r = jax.nn.softmax(logits, axis=-1)
    choose = expert_ids[0]
    choose_map = (choose[:, :, None] == jnp.arange(EXPERTS, dtype=jnp.int32)[None, None, :]).astype(
        jnp.float32
    )
    gates = jnp.sum(probs_r[:, None, :] * choose_map, axis=-1)
    capacity = 2 * tok_rows // EXPERTS
    slots, kept, pair_of, filled = route(choose, capacity, EXPERTS)
    token_of = pair_of // 2
    expert_in = jnp.where(
        filled[:, None], routed_low[token_of], jnp.zeros((), jnp.bfloat16)
    ).reshape(EXPERTS, capacity, width)
    piece = lax.all_gather(expert_w, "fsdp", axis=0, tiled=True)
    pre_rows = expert_pre(expert_in, piece)
    result = expert_out(jax.nn.gelu(pre_rows).astype(jnp.bfloat16), piece)
    padded = jnp.concatenate(
        [result.reshape(EXPERTS * capacity, width), jnp.zeros((1, width), jnp.float32)], axis=0
    )
    picked = padded[slots].reshape(tok_rows, 2, width)
    kept_f = kept.astype(jnp.float32).reshape(tok_rows, 2)
    weight_pair = gates * kept_f
    block_out = hidden + jnp.sum(weight_pair[..., None] * picked, axis=1)
    grad_out_rows = cotangent[0].astype(jnp.float32)
    grad_gates = kept_f * jnp.sum(grad_out_rows[:, None, :] * picked, axis=-1)
    grad_probs = jnp.sum(grad_gates[:, :, None] * choose_map, axis=1)
    grad_logits = probs_r * (grad_probs - jnp.sum(probs_r * grad_probs, axis=-1, keepdims=True))
    grad_route_w = jnp.dot(routed_low.astype(jnp.float32).T, grad_logits, precision=HIGH)
    grad_routed = jnp.dot(grad_logits, w_route.astype(jnp.float32).T, precision=HIGH)
    scaled = (weight_pair[:, :, None] * grad_out_rows[:, None, :]).reshape(2 * tok_rows, width)
    grad_result = (
        jnp.where(filled[:, None], scaled[pair_of], 0.0)
        .astype(jnp.bfloat16)
        .reshape(EXPERTS, capacity, width)
    )
    piece = lax.all_gather(expert_w, "fsdp", axis=0, tiled=True)
    pre_rows = expert_pre(expert_in, piece)
    act_rows = jax.nn.gelu(pre_rows).astype(jnp.bfloat16)
    grad_pre_rows, grad_in_rows = expert_back(grad_result, pre_rows, piece)
    act_store = act_rows
    pre_rows = grad_pre_rows
    act_rows = act_store
    grad_first = jnp.einsum("ecd,ecf->fed", expert_in, pre_rows, preferred_element_type=jnp.float32)
    grad_second = jnp.einsum(
        "ecf,ecd->fed", act_rows, grad_result, preferred_element_type=jnp.float32
    )
    expert_shard = lax.psum_scatter(
        jnp.concatenate([grad_first, grad_second], axis=2).astype(jnp.bfloat16),
        "fsdp",
        scatter_dimension=0,
        tiled=True,
    )
    padded_in = jnp.concatenate(
        [grad_in_rows.reshape(EXPERTS * capacity, width), jnp.zeros((1, width), jnp.float32)],
        axis=0,
    )
    grad_routed = grad_routed + jnp.sum(padded_in[slots].reshape(tok_rows, 2, width), axis=1)
    grad_gain_two = jnp.sum(grad_routed * normed_two, axis=0)
    scaled_two = grad_routed * gain_f[:, 1]
    grad_hidden = grad_out_rows + r_two * (
        scaled_two - normed_two * jnp.mean(scaled_two * normed_two, axis=-1, keepdims=True)
    )
    hid_low = grad_hidden.astype(jnp.bfloat16)
    grad_proj_w = jnp.dot(attended.T, hid_low, preferred_element_type=jnp.float32)
    grad_attended = jnp.dot(hid_low, w_proj.T, preferred_element_type=jnp.float32).astype(
        jnp.bfloat16
    )
    grad_heads = lax.all_to_all(
        grad_attended.reshape(tok_rows, seq_count, head_cols),
        "seq",
        split_axis=1,
        concat_axis=0,
        tiled=True,
    )
    grad_mixed = grad_heads.reshape(group_len, local_heads, HEAD_DIM)

    def back_block(carry, inputs):
        begin, log_rows = inputs
        masked, query_block = block_scores(begin)
        probs = jnp.exp(masked - log_rows[:, :, None])
        grad_block = lax.dynamic_slice_in_dim(grad_mixed, begin, block, 0)
        grad_p = jnp.einsum("qhd,khd->hqk", grad_block, values, preferred_element_type=jnp.float32)
        inner = jnp.sum(probs * grad_p, axis=-1, keepdims=True)
        grad_scores = (probs * (grad_p - inner)).astype(jnp.bfloat16)
        grad_query = (
            jnp.einsum("hqk,khd->qhd", grad_scores, keys, preferred_element_type=jnp.float32)
            * scale
        )
        grad_key = (
            carry[0]
            + jnp.einsum(
                "hqk,qhd->khd", grad_scores, query_block, preferred_element_type=jnp.float32
            )
            * scale
        )
        grad_value = carry[1] + jnp.einsum(
            "hqk,qhd->khd",
            probs.astype(jnp.bfloat16),
            grad_block,
            preferred_element_type=jnp.float32,
        )
        return ((grad_key, grad_value), grad_query)

    zero_heads = jnp.zeros((group_len, local_heads, HEAD_DIM), jnp.float32)
    (grad_keys, grad_values), grad_queries = lax.scan(
        back_block, (zero_heads, zero_heads), (begins, log_totals)
    )
    stacked = jnp.stack(
        [
            grad_queries.reshape(group_len, head_cols),
            grad_keys.reshape(group_len, head_cols),
            grad_values.reshape(group_len, head_cols),
        ],
        axis=1,
    )
    stacked = stacked.astype(jnp.bfloat16).reshape(group_len, 3, 1, head_cols)
    grad_back = lax.all_to_all(stacked, "seq", split_axis=0, concat_axis=2, tiled=True)
    grad_proj_rows = grad_back.reshape(tok_rows, 3 * width)
    grad_qkv_w = jnp.dot(normed_low.T, grad_proj_rows, preferred_element_type=jnp.float32)
    grad_normed = jnp.dot(grad_proj_rows, w_qkv.T, preferred_element_type=jnp.float32)
    grad_gain_one = jnp.sum(grad_normed * normed_one, axis=0)
    scaled_one = grad_normed * gain_f[:, 0]
    grad_x = grad_hidden + r_one * (
        scaled_one - normed_one * jnp.mean(scaled_one * normed_one, axis=-1, keepdims=True)
    )
    grad_gains = jnp.stack([grad_gain_one, grad_gain_two], axis=1)
    shard_qkv, shard_proj, shard_route, shard_gains = (
        lax.psum_scatter(
            grad_qkv_w.astype(jnp.bfloat16), "fsdp", scatter_dimension=0, tiled=True
        ).astype(jnp.float32),
        lax.psum_scatter(
            grad_proj_w.astype(jnp.bfloat16), "fsdp", scatter_dimension=0, tiled=True
        ).astype(jnp.float32),
        lax.psum_scatter(
            grad_route_w.astype(jnp.bfloat16), "fsdp", scatter_dimension=0, tiled=True
        ).astype(jnp.float32),
        lax.psum_scatter(
            grad_gains.astype(jnp.bfloat16), "fsdp", scatter_dimension=0, tiled=True
        ).astype(jnp.float32),
    )
    part_qkv, part_proj, part_expert = (
        lax.psum_scatter(
            shard_qkv.astype(jnp.bfloat16), ("dp", "seq"), scatter_dimension=1, tiled=True
        ).astype(jnp.float32),
        lax.psum_scatter(
            shard_proj.astype(jnp.bfloat16), ("dp", "seq"), scatter_dimension=1, tiled=True
        ).astype(jnp.float32),
        lax.psum_scatter(expert_shard, ("dp", "seq"), scatter_dimension=2, tiled=True).astype(
            jnp.float32
        ),
    )
    summed_qkv, summed_proj, summed_expert = (
        lax.all_gather(part_qkv.astype(jnp.bfloat16), ("dp", "seq"), axis=1, tiled=True).astype(
            part_qkv.dtype
        ),
        lax.all_gather(part_proj.astype(jnp.bfloat16), ("dp", "seq"), axis=1, tiled=True).astype(
            part_proj.dtype
        ),
        lax.all_gather(part_expert.astype(jnp.bfloat16), ("dp", "seq"), axis=2, tiled=True).astype(
            part_expert.dtype
        ),
    )
    summed_route, summed_gains = lax.psum((shard_route, shard_gains), ("dp", "seq"))
    return (
        block_out.astype(jnp.bfloat16)[None],
        grad_x.astype(jnp.bfloat16)[None],
        summed_qkv,
        summed_proj,
        summed_route,
        summed_gains,
        summed_expert,
    )


def fits(mesh):
    return mesh.shape["fsdp"] == 4 and mesh.shape["dp"] == 4 and mesh.shape["seq"] == 2


def solution(mesh):
    body = shards if fits(mesh) else general_shards
    in_specs = (
        P(("dp", "fsdp"), "seq", None),
        P("fsdp", None),
        P("fsdp", None),
        P("fsdp", None),
        P("fsdp", None),
        P("fsdp", None, None),
        P(("dp", "fsdp"), "seq", None),
        P(("dp", "fsdp"), None),
        P(("dp", "fsdp"), "seq", None),
    )
    out_specs = (
        P(("dp", "fsdp"), "seq", None),
        P(("dp", "fsdp"), "seq", None),
        P("fsdp", None),
        P("fsdp", None),
        P("fsdp", None),
        P("fsdp", None),
        P("fsdp", None, None),
    )
    return jax.shard_map(body, mesh=mesh, in_specs=in_specs, out_specs=out_specs, check_vma=False)
```
